256 devices in a mesh: seq: 256 (over z, x, y, core).
Axes of the slice: x: 4, y: 4, z: 8, core: 2. Of those that a mesh axis runs over, the one named last changes fastest.
Arguments:
- tokens: bfloat16 [32768, 1024], P('seq'), may hold values from -96 to 96
- query_weight: bfloat16 [1024, 1024], replicated, may hold values from -1 to 1
- key_weight: bfloat16 [1024, 512], replicated, may hold values from -1 to 1
- value_matrix: bfloat16 [1024, 512], replicated, may hold values from -0.1875 to 0.1875
- out_weight: bfloat16 [1024, 1024], replicated, may hold values from -0.1875 to 0.1875
- out_cotangent: bfloat16 [32768, 1024], P('seq'), may hold values from -24 to 24
Outputs:
- attn_out: bfloat16 [32768, 1024], P('seq')
- tokens_grad: bfloat16 [32768, 1024], P('seq')
- query_weight_grad: float32 [1024, 1024], P('seq')
- key_weight_grad: float32 [1024, 512], P('seq')
- value_weight_grad: float32 [1024, 512], P('seq')
- out_weight_grad: float32 [1024, 1024], P(None, 'seq')
The draws below stay inside these ranges and needn't reach their ends.
All inputs are finite; a program needn't handle non-finite values.
Results may differ from the reference program's by a relative error of at most 0.015.
The reference program's roundings to bfloat16 on the way count: a program that leaves them out, or rounds other values in their place, can miss the bound.
Values may be sent and summed in bfloat16 or wider, within the bound.
No kernel may reach another device: no remote copies, remote signals or barrier semaphores. Data moves between devices by JAX's collectives and lax.ppermute only.
A program may use at most 128 MiB of HBM per device.

```python
import jax
import jax.numpy as jnp
from jax import lax

MODEL_SIZE = 1024
QUERY_HEADS = 16
KEY_HEADS = 8
HEAD_SIZE = 64
PRIOR_SHARDS = 2
DEVICE_TOKENS = 128
QUERY_PER_KEY = 2
TOKEN_COUNT = 32768
N_SEQ = 256


def paired_projections(key):
    anchor_row = jax.random.fold_in(key, 4711)
    query_piece = jnp.clip(jax.random.normal(jax.random.fold_in(anchor_row, 1), (MODEL_SIZE, QUERY_HEADS * HEAD_SIZE), jnp.float32), -6.0, 6.0) / MODEL_SIZE ** 0.5
    key_piece = jnp.clip(jax.random.normal(jax.random.fold_in(anchor_row, 2), (MODEL_SIZE, KEY_HEADS * HEAD_SIZE), jnp.float32), -6.0, 6.0) / MODEL_SIZE ** 0.5
    return (query_piece, key_piece)


def draw_query_weight(key, part):
    return paired_projections(key)[0].astype(jnp.bfloat16)


def draw_key_weight(key, part):
    return paired_projections(key)[1].astype(jnp.bfloat16)


def draw_tokens(key, part):
    row_ids = jnp.arange(TOKEN_COUNT, dtype=jnp.int32)
    raw = jnp.clip(jax.random.normal(jax.random.fold_in(key, 11), (TOKEN_COUNT, MODEL_SIZE), jnp.float32), -6.0, 6.0)
    values_now = raw
    order = jax.random.permutation(jax.random.fold_in(key, 14), N_SEQ)
    block_width = MODEL_SIZE // N_SEQ
    chosen = order[row_ids // DEVICE_TOKENS]
    lifted = jnp.where(jnp.arange(MODEL_SIZE, dtype=jnp.int32)[None, :] // block_width == chosen[:, None], 4.0, 1.0)
    return jnp.clip(values_now * lifted, -96.0, 96.0).astype(jnp.bfloat16)


def spiked(entries, rng, source, target, blocks, factor):
    owner, partner = [(jnp.arange(entries.shape[axis_at]) // (entries.shape[axis_at] // blocks)).reshape([-1 if axis == axis_at else 1 for axis in range(entries.ndim)]) for axis_at in (source, target)]
    chosen = jax.random.permutation(rng, blocks)[partner]
    strong = (owner == chosen) | (owner == (partner + blocks // 2) % blocks)
    return jnp.where(strong, factor * entries, entries)


def level_of(stream_key, extent, shards, smallest, high):
    def one(position, parts):
        draws = jax.random.uniform(jax.random.fold_in(jax.random.fold_in(stream_key, 6), position), (parts,), jnp.float32, smallest / len(shards), high / len(shards))
        return jnp.repeat(jnp.exp(draws), extent[position] // parts).reshape((-1,) + (1,) * (len(extent) - position - 1))

    factor_of = one(*shards[0])
    for cut in shards[1:]:
        factor_of = factor_of * one(*cut)
    return factor_of


def centred(rng, dims, scale, most, cuts=(), held_as=jnp.bfloat16):
    loudness = level_of(rng, dims, cuts, -0.22, 0.18) if cuts else 1.0
    drawn = jax.random.normal(rng, dims, jnp.float32) * scale * loudness
    return jnp.minimum(jnp.maximum(drawn, -most), most).astype(held_as)


def gaussian_with(own_key, extent, deviation, most, cuts, heavy, kind=jnp.bfloat16):
    values = deviation * jax.random.normal(own_key, extent, jnp.float32)
    if cuts:
        values = values * level_of(own_key, extent, cuts, -0.22, 0.18)
    return jnp.clip(spiked(values, jax.random.fold_in(own_key, 3), *heavy), -most, most).astype(kind)


def setup_inputs(seed: int = 0) -> dict:
    splits = jax.random.split(jax.random.key(seed), 7)
    tokens = draw_tokens(jax.random.fold_in(splits[6], 71), 0)
    query_weight = draw_query_weight(jax.random.fold_in(splits[6], 71), 0)
    key_weight = draw_key_weight(jax.random.fold_in(splits[6], 71), 0)
    value_matrix = centred(splits[3], (MODEL_SIZE, KEY_HEADS * HEAD_SIZE), MODEL_SIZE ** -0.5, 0.1875)
    out_weight = centred(splits[4], (QUERY_HEADS * HEAD_SIZE, MODEL_SIZE), (QUERY_HEADS * HEAD_SIZE) ** -0.5, 0.1875)
    out_cotangent = gaussian_with(splits[5], (TOKEN_COUNT, MODEL_SIZE), 1.0, 24.0, ((0, 256),), (0, 1, 256, 6.0))
    return dict(tokens=tokens, query_weight=query_weight, key_weight=key_weight, value_matrix=value_matrix, out_weight=out_weight, out_cotangent=out_cotangent)


SCALE = 0.125
MASKED = -1e30


def permitted(shard_idx):
    query_pos = shard_idx * DEVICE_TOKENS + jnp.arange(DEVICE_TOKENS, dtype=jnp.int32)
    key_pos = (shard_idx - PRIOR_SHARDS) * DEVICE_TOKENS + jnp.arange((PRIOR_SHARDS + 1) * DEVICE_TOKENS, dtype=jnp.int32)
    return (key_pos[None, :] <= query_pos[:, None]) & (key_pos[None, :] >= 0)


def split_queries(weight_matrix):
    return jnp.transpose(weight_matrix.reshape(weight_matrix.shape[0], KEY_HEADS, QUERY_PER_KEY, HEAD_SIZE), (1, 0, 2, 3))


def split_keys(weight_matrix):
    return jnp.transpose(weight_matrix.reshape(weight_matrix.shape[0], KEY_HEADS, HEAD_SIZE), (1, 0, 2))


def join_queries(head_rows):
    return jnp.transpose(head_rows, (1, 0, 2, 3)).reshape(head_rows.shape[1], QUERY_HEADS * HEAD_SIZE)


def join_keys(head_rows):
    return jnp.transpose(head_rows, (1, 0, 2)).reshape(head_rows.shape[1], KEY_HEADS * HEAD_SIZE)


def head_scores(queries, key_head, allowed):
    scores = jnp.einsum("tgd,wd->tgw", queries.astype(jnp.float32), key_head.astype(jnp.float32)) * SCALE
    return jnp.where(allowed[:, None, :], scores, MASKED)


def head_forward(queries, key_head, value_head, allowed):
    scores = head_scores(queries, key_head, allowed)
    highest = jnp.max(scores, axis=-1, keepdims=True)
    summed_total = jnp.sum(jnp.exp(scores - highest), axis=-1, keepdims=True)
    logsum = highest + jnp.log(summed_total)
    probs = jnp.exp(scores - logsum).astype(jnp.bfloat16)
    attended = jnp.einsum("tgw,wd->tgd", probs.astype(jnp.float32), value_head.astype(jnp.float32)).astype(jnp.bfloat16)
    return attended, logsum[..., 0]


def head_backward(queries, key_head, value_head, logsum, d_attended, attended, allowed):
    scores = head_scores(queries, key_head, allowed)
    weights = jnp.exp(scores - logsum[..., None])
    probs = weights.astype(jnp.bfloat16)
    d_float = d_attended.astype(jnp.float32)
    spread = jnp.sum(d_float * attended.astype(jnp.float32), axis=-1)
    value_part = jnp.einsum("tgw,tgd->wd", probs.astype(jnp.float32), d_float)
    dprobs = jnp.einsum("tgd,wd->tgw", d_float, value_head.astype(jnp.float32))
    dscores = (weights * (dprobs - spread[..., None])).astype(jnp.bfloat16)
    ds_float = dscores.astype(jnp.float32)
    query_piece = jnp.einsum("tgw,wd->tgd", ds_float, key_head.astype(jnp.float32)) * SCALE
    key_piece = jnp.einsum("tgw,tgd->wd", ds_float, queries.astype(jnp.float32)) * SCALE
    return query_piece, key_piece, value_part


def fold_window(pieces):
    pieces = pieces.reshape(N_SEQ, PRIOR_SHARDS + 1, DEVICE_TOKENS, KEY_HEADS * HEAD_SIZE)
    tail_rows = jnp.zeros((PRIOR_SHARDS, PRIOR_SHARDS + 1, DEVICE_TOKENS, KEY_HEADS * HEAD_SIZE), pieces.dtype)
    padded = jnp.concatenate([pieces, tail_rows], axis=0)
    summed_total = padded[0:N_SEQ, PRIOR_SHARDS]
    for offset in range(1, PRIOR_SHARDS + 1):
        summed_total = summed_total + padded[offset:offset + N_SEQ, PRIOR_SHARDS - offset]
    return summed_total.reshape(TOKEN_COUNT, KEY_HEADS * HEAD_SIZE).astype(jnp.bfloat16)


def reference(tokens, query_weight, key_weight, value_matrix, out_weight, out_cotangent):
    window = (PRIOR_SHARDS + 1) * DEVICE_TOKENS
    queries = jnp.dot(tokens, query_weight, preferred_element_type=jnp.float32).astype(jnp.bfloat16)
    keys_all = jnp.dot(tokens, key_weight, preferred_element_type=jnp.float32).astype(jnp.bfloat16)
    values_all = jnp.dot(tokens, value_matrix, preferred_element_type=jnp.float32).astype(jnp.bfloat16)
    leading_padding = jnp.zeros((PRIOR_SHARDS * DEVICE_TOKENS, KEY_HEADS * HEAD_SIZE), jnp.bfloat16)
    keys_padded = jnp.concatenate([leading_padding, keys_all], axis=0)
    values_padded = jnp.concatenate([leading_padding, values_all], axis=0)
    shard_ids = jnp.arange(N_SEQ, dtype=jnp.int32)

    def blocks_of(shard_idx):
        start_row = (shard_idx * DEVICE_TOKENS).astype(jnp.int32)
        q_block = lax.dynamic_slice_in_dim(queries, start_row, DEVICE_TOKENS, 0)
        k_block = lax.dynamic_slice_in_dim(keys_padded, start_row, window, 0)
        v_block = lax.dynamic_slice_in_dim(values_padded, start_row, window, 0)
        return split_queries(q_block), split_keys(k_block), split_keys(v_block)

    def forward_shard(shard_idx):
        allowed = permitted(shard_idx)
        q_heads, k_heads, v_heads = blocks_of(shard_idx)
        att_heads, logsum = lax.map(lambda operands: head_forward(operands[0], operands[1], operands[2], allowed), (q_heads, k_heads, v_heads))
        return join_queries(att_heads), logsum

    attended_all, logsum_all = lax.map(forward_shard, shard_ids)
    attended_all = attended_all.reshape(TOKEN_COUNT, QUERY_HEADS * HEAD_SIZE)
    attn_out = jnp.dot(attended_all, out_weight, preferred_element_type=jnp.float32).astype(jnp.bfloat16)
    out_weight_grad = jnp.dot(attended_all.T, out_cotangent, preferred_element_type=jnp.float32)
    d_attended = jnp.dot(out_cotangent, out_weight.T, preferred_element_type=jnp.float32).astype(jnp.bfloat16)

    def backward_shard(operands):
        shard_idx, logsum = operands
        allowed = permitted(shard_idx)
        q_heads, k_heads, v_heads = blocks_of(shard_idx)
        start_row = (shard_idx * DEVICE_TOKENS).astype(jnp.int32)
        d_heads = split_queries(lax.dynamic_slice_in_dim(d_attended, start_row, DEVICE_TOKENS, 0))
        a_heads = split_queries(lax.dynamic_slice_in_dim(attended_all, start_row, DEVICE_TOKENS, 0))
        q_part, k_part, v_part = lax.map(lambda inner: head_backward(inner[0], inner[1], inner[2], inner[3], inner[4], inner[5], allowed), (q_heads, k_heads, v_heads, logsum, d_heads, a_heads))
        return join_queries(q_part), join_keys(k_part), join_keys(v_part)

    q_parts, k_parts, v_parts = lax.map(backward_shard, (shard_ids, logsum_all))
    query_grad = q_parts.reshape(TOKEN_COUNT, QUERY_HEADS * HEAD_SIZE).astype(jnp.bfloat16)
    key_grad = fold_window(k_parts)
    value_grad = fold_window(v_parts)
    query_weight_grad = jnp.dot(tokens.T, query_grad, preferred_element_type=jnp.float32)
    key_weight_grad = jnp.dot(tokens.T, key_grad, preferred_element_type=jnp.float32)
    value_weight_grad = jnp.dot(tokens.T, value_grad, preferred_element_type=jnp.float32)
    tokens_grad = (jnp.dot(query_grad, query_weight.T, preferred_element_type=jnp.float32)
                   + jnp.dot(key_grad, key_weight.T, preferred_element_type=jnp.float32)
                   + jnp.dot(value_grad, value_matrix.T, preferred_element_type=jnp.float32)).astype(jnp.bfloat16)
    return (attn_out, tokens_grad, query_weight_grad, key_weight_grad, value_weight_grad, out_weight_grad)
```

```python
import functools

import jax
import jax.numpy as jnp
from jax import lax
from jax.experimental import pallas as pl
from jax.experimental.pallas import tpu as pltpu
from jax.sharding import PartitionSpec as P

AXIS = "seq"
SHAPE = (8, 4, 4, 2)
ROWS = 128
MODEL = 1024
LANES = 128
STEPS = 4
CHUNKS = (1, 1, 1, 1)
QCOLS = 256
KCOLS = 128
GCOLS = 768
SCALE = 0.125
MASKED = -1e30
BF16 = jnp.bfloat16
F32 = jnp.float32
NT = (((1,), (1,)), ((), ()))
TN = (((0,), (0,)), ((), ()))


def dot(a, b, dims=(((1,), (0,)), ((), ()))):
    return lax.dot_general(a, b, dims, preferred_element_type=F32)


def flat(z, x, y, c):
    return ((z * 4 + x) * 4 + y) * 2 + c


def moved(array, axis, distance):
    route = []
    for z in range(8):
        for x in range(4):
            for y in range(4):
                for c in range(2):
                    place = [z, x, y, c]
                    place[axis] = (place[axis] + distance) % SHAPE[axis]
                    route.append((flat(z, x, y, c), flat(*place)))
    return lax.ppermute(array, AXIS, route)


def passed_along(block, distance):
    devices = range(256)
    route = [(i - distance, i) for i in devices if i - distance in devices]
    return lax.ppermute(block, AXIS, route)


Z_GROUPS = [
    [flat(z, x, y, c) for z in range(8)] for x in range(4) for y in range(4) for c in range(2)
]


def prep_kernel(place, a_ref, b_ref, out_ref, t_ref):
    x, y, core = place[0], place[1], place[2]
    t_ref[:, :LANES] = a_ref[...].astype(F32).T
    t_ref[:, LANES:] = b_ref[...].astype(F32).T
    low = lax.broadcasted_iota(jnp.int32, (8, 2 * LANES), 0) < 4
    first = core == 0
    for dx in range(4):
        xs = lax.rem(x + dx, 4)
        for dy in range(4):
            ys = lax.rem(y + dy, 4)
            for z in range(0, 8, 4):
                keeps, sends = [], []
                for pair in range(2):
                    base = (z + 2 * pair) * 128 + xs * 32 + ys * 8
                    one = t_ref[pl.ds(pl.multiple_of(base, 8), 8), :]
                    two = t_ref[pl.ds(pl.multiple_of(base + 128, 8), 8), :]
                    c0 = jnp.where(low, one, pltpu.roll(two, 4, 0))
                    c1 = jnp.where(low, pltpu.roll(one, 4, 0), two)
                    keeps.append(jnp.where(first, c0, c1))
                    sends.append(jnp.where(first, c1, c0))
                row = (dx * 4 + dy) * 32 + z * 4
                out_ref[0, row : row + 16, :] = jnp.concatenate(sends, 0).astype(BF16)
                out_ref[1, row : row + 16, :] = jnp.concatenate(keeps, 0).astype(BF16)


def prepared(place, a, b):
    vmem = pl.BlockSpec(memory_space=pltpu.VMEM)
    return pl.pallas_call(
        prep_kernel,
        out_shape=jax.ShapeDtypeStruct((2, 512, 2 * LANES), BF16),
        in_specs=[pl.BlockSpec(memory_space=pltpu.SMEM), vmem, vmem],
        out_specs=vmem,
        scratch_shapes=[pltpu.VMEM((MODEL, 2 * LANES), F32)],
        compiler_params=pltpu.CompilerParams(vmem_limit_bytes=32 << 20),
        name="prep",
    )(place, a, b)


def swapped(a):
    return pltpu.roll(a, 64, 1)


def attention_kernel(
    place,
    far_ref,
    near_ref,
    own_ref,
    q_ref,
    da_ref,
    wk_ref,
    wv_ref,
    tp_ref,
    th_ref,
    att_ref,
    dq_ref,
    own_grad_ref,
    near_grad_ref,
    far_grad_ref,
    send_ref,
    keep_ref,
):
    window = jnp.concatenate([far_ref[...], near_ref[...], own_ref[...]], axis=0)
    keys = dot(window, wk_ref[...])
    values = dot(window, wv_ref[...])
    start = place[3]
    row = lax.rem(lax.broadcasted_iota(jnp.int32, (256, 384), 0), 128)
    col = lax.broadcasted_iota(jnp.int32, (256, 384), 1)
    allowed = (col <= row + 256) & (col >= start)
    low_k = lax.broadcasted_iota(jnp.int32, (384, LANES), 1) < 64
    low_q = lax.broadcasted_iota(jnp.int32, (ROWS, LANES), 1) < 64
    zero = jnp.zeros((ROWS, LANES), BF16)
    keys_swapped, values_swapped = swapped(keys), swapped(values)
    atts, dqs, dks, dvs = [], [], [], []
    for head in range(2):
        own_half = low_k if head == 0 else ~low_k
        key = jnp.where(own_half, keys, keys_swapped).astype(BF16)
        value = jnp.where(own_half, values, values_swapped).astype(BF16)
        cols = slice(head * LANES, (head + 1) * LANES)
        q = q_ref[:, cols]
        da = da_ref[:, cols]
        q2 = jnp.concatenate([jnp.where(low_q, q, zero), jnp.where(low_q, zero, q)], 0)
        da2 = jnp.concatenate([jnp.where(low_q, da, zero), jnp.where(low_q, zero, da)], 0)
        scores = jnp.where(allowed, dot(q2, key, NT) * SCALE, MASKED)
        highest = jnp.max(scores, axis=-1, keepdims=True)
        weights = jnp.exp(scores - highest)
        weights = weights * (1.0 / jnp.sum(weights, axis=-1, keepdims=True))
        probs = weights.astype(BF16)
        both = dot(probs, value)
        att = jnp.where(low_q, both[:ROWS], both[ROWS:]).astype(BF16)
        att_f = att.astype(F32)
        delta = jnp.sum(
            da2.astype(F32) * jnp.concatenate([att_f, att_f], 0), axis=-1, keepdims=True
        )
        dscores = (weights * (dot(da2, value, NT) - delta)).astype(BF16)
        both = dot(dscores, key) * SCALE
        dqs.append(jnp.where(low_q, both[:ROWS], both[ROWS:]).astype(BF16))
        dk = dot(dscores, q2, TN) * SCALE
        dv = dot(probs, da2, TN)
        dks.append(dk + swapped(dk))
        dvs.append(dv + swapped(dv))
        atts.append(att)
    att = jnp.concatenate(atts, 1)
    dq = jnp.concatenate(dqs, 1)
    dkv = jnp.concatenate(
        [jnp.where(low_k, dks[0], dks[1]), jnp.where(low_k, dvs[0], dvs[1])], axis=1
    )
    att_ref[...] = att
    dq_ref[...] = dq
    own_grad_ref[...] = dkv[256:]
    rounded = dkv.astype(BF16)
    far_grad_ref[...] = rounded[:128]
    near_grad_ref[...] = rounded[128:256]
    for half, out in ((0, send_ref), (1, keep_ref)):
        tp = tp_ref[half]
        t_own, t_out = tp[:, :LANES], tp[:, LANES:]
        out[:, :256] = dot(t_out, att).astype(BF16)
        out[:, 256:512] = dot(t_own, dq).astype(BF16)
        out[:, 512:] = (dot(t_own, rounded[256:]) + dot(th_ref[half], rounded[:256])).astype(BF16)


def attention(first, steps, place, far, near, own, q, da, wk, wv, tp, th):
    def whole(shape):
        return pl.BlockSpec(shape, lambda i: (0,) * len(shape))

    def columns(rows, cols):
        return pl.BlockSpec((rows, cols), lambda i: (0, first + i))

    def fresh(rows, cols):
        return pl.BlockSpec((rows, cols), lambda i: (0, i))

    def struct(rows, cols, dtype):
        return jax.ShapeDtypeStruct((rows, cols * steps), dtype)

    return pl.pallas_call(
        attention_kernel,
        grid=(steps,),
        out_shape=(
            struct(ROWS, QCOLS, BF16),
            struct(ROWS, QCOLS, BF16),
            struct(ROWS, QCOLS, F32),
            struct(ROWS, QCOLS, BF16),
            struct(ROWS, QCOLS, BF16),
            struct(512, GCOLS, BF16),
            struct(512, GCOLS, BF16),
        ),
        in_specs=[
            pl.BlockSpec(memory_space=pltpu.SMEM),
            whole((ROWS, MODEL)),
            whole((ROWS, MODEL)),
            whole((ROWS, MODEL)),
            columns(ROWS, QCOLS),
            columns(ROWS, QCOLS),
            columns(MODEL, KCOLS),
            columns(MODEL, KCOLS),
            whole((2, 512, 2 * LANES)),
            whole((2, 512, 2 * LANES)),
        ],
        out_specs=(
            fresh(ROWS, QCOLS),
            fresh(ROWS, QCOLS),
            fresh(ROWS, QCOLS),
            fresh(ROWS, QCOLS),
            fresh(ROWS, QCOLS),
            fresh(512, GCOLS),
            fresh(512, GCOLS),
        ),
        compiler_params=pltpu.CompilerParams(
            dimension_semantics=("arbitrary",), vmem_limit_bytes=48 << 20
        ),
        name="attention",
    )(place, far, near, own, q, da, wk, wv, tp, th)


def summed_on_planes(send, keep):
    cols = send.shape[1]
    half = cols // 2
    total = keep.astype(F32) + moved(send, 3, 1).astype(F32)
    total = total.reshape(4, 4, 32, cols)
    a, b = total[..., :half], total[..., half:]
    a_got = [moved(a[d].astype(BF16), 1, d) for d in (1, 3, 2)]
    b_got = [moved(b[:, d].astype(BF16), 2, d) for d in (1, 3, 2)]
    a = a[0] + sum(g.astype(F32) for g in a_got)
    b = b[:, 0] + sum(g.astype(F32) for g in b_got)
    a_got = [moved(a[d].astype(BF16), 2, d) for d in (1, 3, 2)]
    b_got = [moved(b[d].astype(BF16), 1, d) for d in (1, 3, 2)]
    a = a[0] + sum(g.astype(F32) for g in a_got)
    b = b[0] + sum(g.astype(F32) for g in b_got)
    return jnp.concatenate([a, b], axis=1)


def summed_along_z(total):
    cols = total.shape[1]
    blocks = total.astype(BF16).reshape(8, 4, cols)
    got = lax.all_to_all(blocks, AXIS, 0, 0, axis_index_groups=Z_GROUPS, tiled=True)
    return jnp.sum(got.astype(F32), axis=0)


def shards(tokens, query_weight, key_weight, value_matrix, out_weight, out_cotangent):
    near = passed_along(tokens, 1)
    far = passed_along(tokens, 2)
    me = lax.axis_index(AXIS)
    start = jnp.maximum(2 - me, 0) * ROWS
    place = jnp.stack([(me // 8) % 4, (me // 2) % 4, me % 2, start]).astype(jnp.int32)
    q = dot(tokens, query_weight).astype(BF16)
    da = dot(out_cotangent, out_weight, NT).astype(BF16)
    tp = prepared(place, tokens, out_cotangent)
    th = prepared(place, far, near)
    parts, grads = [], []
    first = 0
    for steps in CHUNKS:
        res = attention(
            first, steps, place, far, near, tokens, q, da, key_weight, value_matrix, tp, th
        )
        first += steps
        parts.append(res[:5])
        grads.append(summed_along_z(summed_on_planes(res[5], res[6])))
    att, dq, own_kv, near_kv, far_kv = (jnp.concatenate(p, axis=1) for p in zip(*parts))
    attn_out = dot(att, out_weight).astype(BF16)
    back_near = passed_along(near_kv, -1)
    back_far = passed_along(far_kv, -2)
    kv = (own_kv + back_near.astype(F32) + back_far.astype(F32)).astype(BF16)
    kv = kv.reshape(ROWS, STEPS, 2, KCOLS)
    key_grad = kv[:, :, 0].reshape(ROWS, 512)
    value_grad = kv[:, :, 1].reshape(ROWS, 512)
    tokens_grad = (
        dot(dq, query_weight, NT) + dot(key_grad, key_weight, NT) + dot(value_grad, value_matrix, NT)
    ).astype(BF16)
    total = jnp.concatenate(grads, axis=1).reshape(4, STEPS, GCOLS)
    out_rows = total[:, :, :256].reshape(4, 1024)
    query_rows = total[:, :, 256:512].reshape(4, 1024)
    key_rows = total[:, :, 512:640].reshape(4, 512)
    value_rows = total[:, :, 640:].reshape(4, 512)
    return attn_out, tokens_grad, query_rows, key_rows, value_rows, out_rows.T


def solution(mesh):
    rows = P(AXIS, None)
    return jax.shard_map(
        shards,
        mesh=mesh,
        in_specs=(rows, P(), P(), P(), P(), rows),
        out_specs=(rows, rows, rows, rows, rows, P(None, AXIS)),
        check_vma=False,
    )
```

```python
import functools

import jax
import jax.numpy as jnp
from jax import lax
from jax.experimental import pallas as pl
from jax.experimental.pallas import tpu as pltpu
from jax.sharding import PartitionSpec as P

AXIS = "seq"
SHAPE = (8, 4, 4, 2)
ROWS = 128
MODEL = 1024
LANES = 128
STEPS = 4
QCOLS = 256
KCOLS = 128
GCOLS = 768
SCALE = 0.125
MASKED = -1e30
BF16 = jnp.bfloat16
SMALL = pl.CostEstimate(flops=1000, transcendentals=0, bytes_accessed=1000)
F32 = jnp.float32
NT = (((1,), (1,)), ((), ()))
TN = (((0,), (0,)), ((), ()))


def dot(a, b, dims=(((1,), (0,)), ((), ()))):
    return lax.dot_general(a, b, dims, preferred_element_type=F32)


def flat(z, x, y, c):
    return ((z * 4 + x) * 4 + y) * 2 + c


def moved(array, axis, distance):
    route = []
    for z in range(8):
        for x in range(4):
            for y in range(4):
                for c in range(2):
                    place = [z, x, y, c]
                    place[axis] = (place[axis] + distance) % SHAPE[axis]
                    route.append((flat(z, x, y, c), flat(*place)))
    return lax.ppermute(array, AXIS, route)


def passed_along(block, distance):
    devices = range(256)
    route = [(i - distance, i) for i in devices if i - distance in devices]
    return lax.ppermute(block, AXIS, route)


XY_GROUPS = [
    [flat(z, x, y, c) for x in range(4) for y in range(4)] for z in range(8) for c in range(2)
]
Z_GROUPS = [
    [flat(z, x, y, c) for z in range(8)] for x in range(4) for y in range(4) for c in range(2)
]


def prep_kernel(place, a_ref, b_ref, out_ref, t_ref):
    x, y, core = place[0], place[1], place[2]
    t_ref[:, :LANES] = a_ref[...].astype(F32).T
    t_ref[:, LANES:] = b_ref[...].astype(F32).T
    low = lax.broadcasted_iota(jnp.int32, (8, 2 * LANES), 0) < 4
    first = core == 0
    for dx in range(4):
        xs = lax.rem(x + dx, 4)
        for dy in range(4):
            ys = lax.rem(y + dy, 4)
            for z in range(0, 8, 4):
                keeps, sends = [], []
                for pair in range(2):
                    base = (z + 2 * pair) * 128 + xs * 32 + ys * 8
                    one = t_ref[pl.ds(pl.multiple_of(base, 8), 8), :]
                    two = t_ref[pl.ds(pl.multiple_of(base + 128, 8), 8), :]
                    c0 = jnp.where(low, one, pltpu.roll(two, 4, 0))
                    c1 = jnp.where(low, pltpu.roll(one, 4, 0), two)
                    keeps.append(jnp.where(first, c0, c1))
                    sends.append(jnp.where(first, c1, c0))
                row = (dx * 4 + dy) * 32 + z * 4
                out_ref[0, row : row + 16, :] = jnp.concatenate(sends, 0).astype(BF16)
                out_ref[1, row : row + 16, :] = jnp.concatenate(keeps, 0).astype(BF16)


def prepared(place, a, b):
    vmem = pl.BlockSpec(memory_space=pltpu.VMEM)
    return pl.pallas_call(
        prep_kernel,
        out_shape=jax.ShapeDtypeStruct((2, 512, 2 * LANES), BF16),
        in_specs=[pl.BlockSpec(memory_space=pltpu.SMEM), vmem, vmem],
        out_specs=vmem,
        scratch_shapes=[pltpu.VMEM((MODEL, 2 * LANES), F32)],
        compiler_params=pltpu.CompilerParams(vmem_limit_bytes=32 << 20),
        name="prep",
    )(place, a, b)


def swapped(a):
    return pltpu.roll(a, 64, 1)


def attention_kernel(
    place,
    far_ref,
    near_ref,
    own_ref,
    q_ref,
    da_ref,
    wk_ref,
    wv_ref,
    tp_ref,
    th_ref,
    att_ref,
    dq_ref,
    own_grad_ref,
    near_grad_ref,
    far_grad_ref,
    send_ref,
    keep_ref,
):
    window = jnp.concatenate([far_ref[...], near_ref[...], own_ref[...]], axis=0)
    keys = dot(window, wk_ref[...])
    values = dot(window, wv_ref[...])
    start = place[3]
    row = lax.rem(lax.broadcasted_iota(jnp.int32, (256, 384), 0), 128)
    col = lax.broadcasted_iota(jnp.int32, (256, 384), 1)
    allowed = (col <= row + 256) & (col >= start)
    low_k = lax.broadcasted_iota(jnp.int32, (384, LANES), 1) < 64
    low_q = lax.broadcasted_iota(jnp.int32, (ROWS, LANES), 1) < 64
    zero = jnp.zeros((ROWS, LANES), BF16)
    keys_swapped, values_swapped = swapped(keys), swapped(values)
    atts, dqs, dks, dvs = [], [], [], []
    for head in range(2):
        own_half = low_k if head == 0 else ~low_k
        key = jnp.where(own_half, keys, keys_swapped).astype(BF16)
        value = jnp.where(own_half, values, values_swapped).astype(BF16)
        cols = slice(head * LANES, (head + 1) * LANES)
        q = q_ref[:, cols]
        da = da_ref[:, cols]
        q2 = jnp.concatenate([jnp.where(low_q, q, zero), jnp.where(low_q, zero, q)], 0)
        da2 = jnp.concatenate([jnp.where(low_q, da, zero), jnp.where(low_q, zero, da)], 0)
        scores = jnp.where(allowed, dot(q2, key, NT) * SCALE, MASKED)
        highest = jnp.max(scores, axis=-1, keepdims=True)
        weights = jnp.exp(scores - highest)
        weights = weights * (1.0 / jnp.sum(weights, axis=-1, keepdims=True))
        probs = weights.astype(BF16)
        both = dot(probs, value)
        att = jnp.where(low_q, both[:ROWS], both[ROWS:]).astype(BF16)
        att_f = att.astype(F32)
        delta = jnp.sum(
            da2.astype(F32) * jnp.concatenate([att_f, att_f], 0), axis=-1, keepdims=True
        )
        dscores = (weights * (dot(da2, value, NT) - delta)).astype(BF16)
        both = dot(dscores, key) * SCALE
        dqs.append(jnp.where(low_q, both[:ROWS], both[ROWS:]).astype(BF16))
        dk = dot(dscores, q2, TN) * SCALE
        dv = dot(probs, da2, TN)
        dks.append(dk + swapped(dk))
        dvs.append(dv + swapped(dv))
        atts.append(att)
    att = jnp.concatenate(atts, 1)
    dq = jnp.concatenate(dqs, 1)
    dk = jnp.where(low_k, dks[0], dks[1])
    dv = jnp.where(low_k, dvs[0], dvs[1])
    att_ref[...] = att
    dq_ref[...] = dq
    own_grad_ref[0] = dk[256:]
    own_grad_ref[1] = dv[256:]
    dk, dv = dk.astype(BF16), dv.astype(BF16)
    far_grad_ref[0] = dk[:128]
    far_grad_ref[1] = dv[:128]
    near_grad_ref[0] = dk[128:256]
    near_grad_ref[1] = dv[128:256]
    rounded = jnp.concatenate([dk, dv], axis=1)
    for half, out in ((0, send_ref), (1, keep_ref)):
        tp = tp_ref[half]
        t_own, t_out = tp[:, :LANES], tp[:, LANES:]
        out[:, :256] = dot(t_out, att).astype(BF16)
        out[:, 256:512] = dot(t_own, dq).astype(BF16)
        out[:, 512:] = (dot(t_own, rounded[256:]) + dot(th_ref[half], rounded[:256])).astype(BF16)


def attention(first, steps, place, far, near, own, q, da, wk, wv, tp, th):
    def whole(shape):
        return pl.BlockSpec(shape, lambda i: (0,) * len(shape))

    def columns(rows, cols):
        return pl.BlockSpec((rows, cols), lambda i: (0, first + i))

    def fresh(rows, cols):
        return pl.BlockSpec((rows, cols), lambda i: (0, i))

    def struct(rows, cols, dtype):
        return jax.ShapeDtypeStruct((rows, cols * steps), dtype)

    return pl.pallas_call(
        attention_kernel,
        grid=(steps,),
        out_shape=(
            struct(ROWS, QCOLS, BF16),
            struct(ROWS, QCOLS, BF16),
            jax.ShapeDtypeStruct((2, ROWS, KCOLS * steps), F32),
            jax.ShapeDtypeStruct((2, ROWS, KCOLS * steps), BF16),
            jax.ShapeDtypeStruct((2, ROWS, KCOLS * steps), BF16),
            struct(512, GCOLS, BF16),
            struct(512, GCOLS, BF16),
        ),
        in_specs=[
            pl.BlockSpec(memory_space=pltpu.SMEM),
            whole((ROWS, MODEL)),
            whole((ROWS, MODEL)),
            whole((ROWS, MODEL)),
            columns(ROWS, QCOLS),
            columns(ROWS, QCOLS),
            columns(MODEL, KCOLS),
            columns(MODEL, KCOLS),
            whole((2, 512, 2 * LANES)),
            whole((2, 512, 2 * LANES)),
        ],
        out_specs=(
            fresh(ROWS, QCOLS),
            fresh(ROWS, QCOLS),
            pl.BlockSpec((2, ROWS, KCOLS), lambda i: (0, 0, i)),
            pl.BlockSpec((2, ROWS, KCOLS), lambda i: (0, 0, i)),
            pl.BlockSpec((2, ROWS, KCOLS), lambda i: (0, 0, i)),
            fresh(512, GCOLS),
            fresh(512, GCOLS),
        ),
        compiler_params=pltpu.CompilerParams(
            dimension_semantics=("arbitrary",), vmem_limit_bytes=48 << 20
        ),
        cost_estimate=SMALL,
        name="attention",
    )(place, far, near, own, q, da, wk, wv, tp, th)


VMEM_SPEC = pl.BlockSpec(memory_space=pltpu.VMEM)
SMEM_SPEC = pl.BlockSpec(memory_space=pltpu.SMEM)


XCOLS = 1152


def cut(addends, rows, cols):
    total = addends[0][rows, cols].astype(F32)
    for other in addends[1:]:
        total = total + other[rows, cols].astype(F32)
    return total


def first_fold_kernel(keep_one, got_one, keep_two, got_two, *outs):
    one, two = (keep_one, got_one), (keep_two, got_two)
    for d in range(4):
        out = outs[d]
        out[...] = cut(one, slice(d * 128, d * 128 + 128), slice(0, XCOLS)).astype(out.dtype)
        out = outs[4 + d]
        for g in range(4):
            rows, at = slice(g * 128 + d * 32, g * 128 + d * 32 + 32), slice(g * 32, g * 32 + 32)
            out[at, :384] = cut(one, rows, slice(XCOLS, 1536)).astype(out.dtype)
            out[at, 384:] = cut(two, rows, slice(0, 768)).astype(out.dtype)


def second_fold_kernel(*refs):
    addends, outs = refs[:8], refs[8:]
    for group in range(2):
        for d in range(4):
            out = outs[group * 4 + d]
            rows = slice(d * 32, d * 32 + 32)
            out[...] = cut(addends[group * 4 : group * 4 + 4], rows, slice(0, XCOLS)).astype(out.dtype)


def folded(kernel, rows, *addends):
    kinds = (F32, BF16, BF16, BF16) * 2
    outs = pl.pallas_call(
        kernel,
        out_shape=tuple(jax.ShapeDtypeStruct((rows, XCOLS), kind) for kind in kinds),
        in_specs=[VMEM_SPEC] * len(addends),
        out_specs=(VMEM_SPEC,) * 8,
        compiler_params=pltpu.CompilerParams(vmem_limit_bytes=32 << 20),
        cost_estimate=SMALL,
        name="fold",
    )(*addends)
    return outs[:4], outs[4:]


def plane_kernel(place, keep_ref, got_ref, out_ref):
    x, y = place[0], place[1]
    for xd in range(4):
        for yd in range(4):
            block = lax.rem(xd - x + 4, 4) * 4 + lax.rem(yd - y + 4, 4)
            rows = pl.ds(pl.multiple_of(block * 32, 32), 32)
            total = keep_ref[rows, :].astype(F32) + got_ref[rows, :].astype(F32)
            out_ref[xd * 4 + yd] = total.astype(BF16)


def in_plane_order(place, keep, got):
    return pl.pallas_call(
        plane_kernel,
        out_shape=jax.ShapeDtypeStruct((16, 32, keep.shape[1]), BF16),
        in_specs=[SMEM_SPEC, VMEM_SPEC, VMEM_SPEC],
        out_specs=VMEM_SPEC,
        compiler_params=pltpu.CompilerParams(vmem_limit_bytes=32 << 20),
        cost_estimate=SMALL,
        name="plane",
    )(place, keep, got)


def column_kernel(counts, *refs):
    out_ref, sum_ref = refs[-2], refs[-1]
    at, col = 0, 0
    for count in counts:
        if count:
            group = refs[at : at + count]
            at += count
            total = group[0][...].astype(F32)
            for other in group[1:]:
                total = total + other[...].astype(F32)
        else:
            stack = refs[at]
            at += 1
            total = stack[0].astype(F32)
            for i in range(1, stack.shape[0]):
                total = total + stack[i].astype(F32)
        sum_ref[:, col : col + total.shape[1]] = total
        col += total.shape[1]
    low = lax.broadcasted_iota(jnp.int32, (8, LANES), 0) < 4
    for z in range(4):
        for block in range(0, 24, 4):
            even, odd = [], []
            for pair in range(2):
                c = (block + 2 * pair) * LANES
                one = sum_ref[8 * z : 8 * z + 8, c : c + LANES]
                two = sum_ref[8 * z : 8 * z + 8, c + LANES : c + 2 * LANES]
                even.append(jnp.where(low, one, pltpu.roll(two, 4, 0)))
                odd.append(jnp.where(low, pltpu.roll(one, 4, 0), two))
            rows = slice(block * 4, block * 4 + 16)
            out_ref[2 * z, rows, :] = jnp.concatenate(even, 0).astype(BF16)
            out_ref[2 * z + 1, rows, :] = jnp.concatenate(odd, 0).astype(BF16)


def in_column_order(groups):
    counts, flat_args = [], []
    for group in groups:
        if isinstance(group, (tuple, list)):
            counts.append(len(group))
            flat_args.extend(group)
        else:
            counts.append(0)
            flat_args.append(group)
    return pl.pallas_call(
        functools.partial(column_kernel, tuple(counts)),
        out_shape=jax.ShapeDtypeStruct((8, 96, LANES), BF16),
        in_specs=[VMEM_SPEC] * len(flat_args),
        out_specs=VMEM_SPEC,
        scratch_shapes=[pltpu.VMEM((32, 4 * GCOLS), F32)],
        compiler_params=pltpu.CompilerParams(vmem_limit_bytes=32 << 20),
        cost_estimate=SMALL,
        name="column",
    )(*flat_args)


def last_kernel(got_ref, q_ref, k_ref, v_ref, o_ref):
    total = got_ref[0].astype(F32)
    for i in range(1, 8):
        total = total + got_ref[i].astype(F32)
    for step in range(STEPS):
        base = step * 24
        out, q, kv = (total[base + 8 * i : base + 8 * i + 8] for i in range(3))
        turned = out.T
        o_ref[step * 256 : step * 256 + 128, :] = turned[:, :4]
        o_ref[step * 256 + 128 : step * 256 + 256, :] = turned[:, 4:]
        q_ref[:, step * 256 : step * 256 + 128] = q[:4]
        q_ref[:, step * 256 + 128 : step * 256 + 256] = q[4:]
        k_ref[:, step * 128 : step * 128 + 128] = kv[:4]
        v_ref[:, step * 128 : step * 128 + 128] = kv[4:]


def summed_last(got):
    return pl.pallas_call(
        last_kernel,
        out_shape=(
            jax.ShapeDtypeStruct((4, 1024), F32),
            jax.ShapeDtypeStruct((4, 512), F32),
            jax.ShapeDtypeStruct((4, 512), F32),
            jax.ShapeDtypeStruct((1024, 4), F32),
        ),
        in_specs=[VMEM_SPEC],
        out_specs=(VMEM_SPEC,) * 4,
        name="last",
    )(got)


def after(value, *others):
    return lax.optimization_barrier((value, *others))[0]


def shards(tokens, query_weight, key_weight, value_matrix, out_weight, out_cotangent):
    near = passed_along(tokens, 1)
    far = passed_along(tokens, 2)
    me = lax.axis_index(AXIS)
    start = jnp.maximum(2 - me, 0) * ROWS
    place = jnp.stack([(me // 8) % 4, (me // 2) % 4, me % 2, start]).astype(jnp.int32)
    q = dot(tokens, query_weight).astype(BF16)
    da = dot(out_cotangent, out_weight, NT).astype(BF16)
    tp = prepared(place, tokens, out_cotangent)
    th = prepared(place, far, near)

    def attend(first, steps, place):
        return attention(
            first, steps, place, far, near, tokens, q, da, key_weight, value_matrix, tp, th
        )

    one = attend(0, 2, place)
    got_one = moved(one[-2], 3, 1)
    two = attend(2, 1, after(place, one[-1]))
    got_two = moved(two[-2], 3, 1)
    xs, ys = folded(first_fold_kernel, 128, one[-1], got_one, two[-1], got_two)
    ring_x = [moved(xs[1], 1, 1), moved(xs[3], 1, 3)]
    ring_y = [moved(ys[1], 2, 1), moved(ys[3], 2, 3)]
    three = attend(3, 1, after(place, xs[0]))
    got_three = moved(three[-2], 3, 1)
    blocks = in_plane_order(place, three[-1], got_three)
    ring_x.append(moved(after(xs[2], blocks), 1, 2))
    ring_y.append(moved(after(ys[2], blocks), 2, 2))
    plane = lax.all_to_all(blocks, AXIS, 0, 0, axis_index_groups=XY_GROUPS, tiled=True)
    xs, ys = folded(second_fold_kernel, 32, xs[0], *ring_x, ys[0], *ring_y)
    ring_x = [moved(xs[d], 2, d) for d in (1, 3, 2)]
    ring_y = [moved(ys[d], 1, d) for d in (1, 3, 2)]

    parts = zip(one[:-2], two[:-2], three[:-2])
    att, dq, own_kv, near_kv, far_kv = (jnp.concatenate(p, axis=-1) for p in parts)
    back_near = passed_along(after(near_kv, xs[0]), -1)
    back_far = passed_along(after(far_kv, xs[0]), -2)

    attn_out = dot(att, out_weight).astype(BF16)
    kv = (own_kv + back_near.astype(F32) + back_far.astype(F32)).astype(BF16)
    tokens_grad = (
        dot(dq, query_weight, NT) + dot(kv[0], key_weight, NT) + dot(kv[1], value_matrix, NT)
    ).astype(BF16)

    column = in_column_order([[xs[0], *ring_x], [ys[0], *ring_y], plane])
    got = lax.all_to_all(column, AXIS, 0, 0, axis_index_groups=Z_GROUPS, tiled=True)
    query_rows, key_rows, value_rows, out_columns = summed_last(got)
    return attn_out, tokens_grad, query_rows, key_rows, value_rows, out_columns


def solution(mesh):
    rows = P(AXIS, None)
    return jax.shard_map(
        shards,
        mesh=mesh,
        in_specs=(rows, P(), P(), P(), P(), rows),
        out_specs=(rows, rows, rows, rows, rows, P(None, AXIS)),
        check_vma=False,
    )
```

```python
import functools

import jax
import jax.numpy as jnp
from jax import lax
from jax.experimental import pallas as pl
from jax.experimental.pallas import tpu as pltpu
from jax.sharding import PartitionSpec as P

AXIS = "seq"
ROWS = 128
MODEL = 1024
LANES = 128
STEPS = 4
QCOLS = 256
KCOLS = 128
GCOLS = 768
SCALE = 0.125
MASKED = -1e30
BF16 = jnp.bfloat16
SMALL = pl.CostEstimate(flops=1000, transcendentals=0, bytes_accessed=1000)
F32 = jnp.float32
NT = (((1,), (1,)), ((), ()))
TN = (((0,), (0,)), ((), ()))


def dot(a, b, dims=(((1,), (0,)), ((), ()))):
    return lax.dot_general(a, b, dims, preferred_element_type=F32)


def flat(z, x, y, c):
    return ((z * 4 + x) * 4 + y) * 2 + c


def in_hbm(array):
    return pltpu.with_memory_space_constraint(array, pltpu.HBM)


def route_of(step):
    places = [(z, x, y, c) for z in range(8) for x in range(4) for y in range(4) for c in range(2)]
    return [(flat(*p), flat(*step(*p))) for p in places]


def to_mate(array):
    return lax.ppermute(array, AXIS, route_of(lambda z, x, y, c: (z, x, y, 1 - c)))


def ring(blocks, phase):
    def step(d, z, x, y, c):
        if c == phase:
            return z, (x + d) % 4, y, c
        return z, x, (y + d) % 4, c

    order = (1, 3, 2)
    return [
        lax.ppermute(blocks[d], AXIS, route_of(functools.partial(step, d))) for d in order
    ]


def passed_along(block, distance):
    devices = range(256)
    route = [(i - distance, i) for i in devices if i - distance in devices]
    return lax.ppermute(block, AXIS, route)


Z_GROUPS = [
    [flat(z, x, y, c) for z in range(8)] for x in range(4) for y in range(4) for c in range(2)
]


def reorder(place, t_ref, out_ref):
    x, y, core = place[0], place[1], place[2]
    low = lax.broadcasted_iota(jnp.int32, (8, 2 * LANES), 0) < 4
    for half in range(2):
        target = 1 - core if half == 0 else core
        zero = target == 0
        for d1 in range(4):
            for d2 in range(4):
                xs = lax.rem(x + jnp.where(zero, d1, d2), 4)
                ys = lax.rem(y + jnp.where(zero, d2, d1), 4)
                for z in range(0, 8, 4):
                    rows = []
                    for pair in range(2):
                        base = (z + 2 * pair) * 128 + xs * 32 + ys * 8
                        one = t_ref[pl.ds(pl.multiple_of(base, 8), 8), :]
                        two = t_ref[pl.ds(pl.multiple_of(base + 128, 8), 8), :]
                        c0 = jnp.where(low, one, pltpu.roll(two, 4, 0))
                        c1 = jnp.where(low, pltpu.roll(one, 4, 0), two)
                        rows.append(jnp.where(zero, c0, c1))
                    row = (d1 * 4 + d2) * 32 + z * 4
                    out_ref[half, row : row + 16, :] = jnp.concatenate(rows, 0).astype(BF16)


def early_kernel(place, tok_ref, cot_ref, wq_ref, wo_ref, q_ref, da_ref, out_ref, t_ref):
    q_ref[...] = dot(tok_ref[...], wq_ref[...]).astype(BF16)
    da_ref[...] = dot(cot_ref[...], wo_ref[...], NT).astype(BF16)

    @pl.when(pl.program_id(0) == 0)
    def _():
        t_ref[:, :LANES] = tok_ref[...].astype(F32).T
        t_ref[:, LANES:] = cot_ref[...].astype(F32).T
        reorder(place, t_ref, out_ref)


def whole(*shape):
    return pl.BlockSpec(shape, lambda i: (0,) * len(shape))


def early(place, tokens, cotangent, wq, wo):
    block = pl.BlockSpec((ROWS, QCOLS), lambda i: (0, i))
    return pl.pallas_call(
        early_kernel,
        grid=(STEPS,),
        out_shape=(
            jax.ShapeDtypeStruct((ROWS, MODEL), BF16),
            jax.ShapeDtypeStruct((ROWS, MODEL), BF16),
            jax.ShapeDtypeStruct((2, 512, 2 * LANES), BF16),
        ),
        in_specs=[
            pl.BlockSpec(memory_space=pltpu.SMEM),
            whole(ROWS, MODEL),
            whole(ROWS, MODEL),
            pl.BlockSpec((MODEL, QCOLS), lambda i: (0, i)),
            pl.BlockSpec((QCOLS, MODEL), lambda i: (i, 0)),
        ],
        out_specs=(block, block, whole(2, 512, 2 * LANES)),
        scratch_shapes=[pltpu.VMEM((MODEL, 2 * LANES), F32)],
        compiler_params=pltpu.CompilerParams(
            dimension_semantics=("arbitrary",), vmem_limit_bytes=20 << 20
        ),
        name="early",
    )(place, tokens, cotangent, wq, wo)


def prep_kernel(place, a_ref, b_ref, out_ref, t_ref):
    t_ref[:, :LANES] = a_ref[...].astype(F32).T
    t_ref[:, LANES:] = b_ref[...].astype(F32).T
    reorder(place, t_ref, out_ref)


def prepared(place, a, b):
    return pl.pallas_call(
        prep_kernel,
        grid=(1,),
        out_shape=jax.ShapeDtypeStruct((2, 512, 2 * LANES), BF16),
        in_specs=[pl.BlockSpec(memory_space=pltpu.SMEM), whole(ROWS, MODEL), whole(ROWS, MODEL)],
        out_specs=whole(2, 512, 2 * LANES),
        scratch_shapes=[pltpu.VMEM((MODEL, 2 * LANES), F32)],
        compiler_params=pltpu.CompilerParams(vmem_limit_bytes=12 << 20),
        name="prep",
    )(place, a, b)


def swapped(a):
    return pltpu.roll(a, 64, 1)


def attention_kernel(
    place,
    far_ref,
    near_ref,
    own_ref,
    q_ref,
    da_ref,
    wk_ref,
    wv_ref,
    tp_ref,
    th_ref,
    att_ref,
    dq_ref,
    own_grad_ref,
    near_grad_ref,
    far_grad_ref,
    send_ref,
    keep_ref,
):
    window = jnp.concatenate([far_ref[...], near_ref[...], own_ref[...]], axis=0)
    keys = dot(window, wk_ref[...])
    values = dot(window, wv_ref[...])
    start = place[3]
    row = lax.rem(lax.broadcasted_iota(jnp.int32, (256, 384), 0), 128)
    col = lax.broadcasted_iota(jnp.int32, (256, 384), 1)
    allowed = (col <= row + 256) & (col >= start)
    low_k = lax.broadcasted_iota(jnp.int32, (384, LANES), 1) < 64
    low_q = lax.broadcasted_iota(jnp.int32, (ROWS, LANES), 1) < 64
    zero = jnp.zeros((ROWS, LANES), BF16)
    keys_swapped, values_swapped = swapped(keys), swapped(values)
    atts, dqs, dks, dvs = [], [], [], []
    for head in range(2):
        own_half = low_k if head == 0 else ~low_k
        key = jnp.where(own_half, keys, keys_swapped).astype(BF16)
        value = jnp.where(own_half, values, values_swapped).astype(BF16)
        cols = slice(head * LANES, (head + 1) * LANES)
        q = q_ref[:, cols]
        da = da_ref[:, cols]
        q2 = jnp.concatenate([jnp.where(low_q, q, zero), jnp.where(low_q, zero, q)], 0)
        da2 = jnp.concatenate([jnp.where(low_q, da, zero), jnp.where(low_q, zero, da)], 0)
        scores = jnp.where(allowed, dot(q2, key, NT) * SCALE, MASKED)
        highest = jnp.max(scores, axis=-1, keepdims=True)
        weights = jnp.exp(scores - highest)
        weights = weights * (1.0 / jnp.sum(weights, axis=-1, keepdims=True))
        probs = weights.astype(BF16)
        both = dot(probs, value)
        att = jnp.where(low_q, both[:ROWS], both[ROWS:]).astype(BF16)
        att_f = att.astype(F32)
        delta = jnp.sum(
            da2.astype(F32) * jnp.concatenate([att_f, att_f], 0), axis=-1, keepdims=True
        )
        dscores = (weights * (dot(da2, value, NT) - delta)).astype(BF16)
        both = dot(dscores, key) * SCALE
        dqs.append(jnp.where(low_q, both[:ROWS], both[ROWS:]).astype(BF16))
        dk = dot(dscores, q2, TN) * SCALE
        dv = dot(probs, da2, TN)
        dks.append(dk + swapped(dk))
        dvs.append(dv + swapped(dv))
        atts.append(att)
    att = jnp.concatenate(atts, 1)
    dq = jnp.concatenate(dqs, 1)
    dk = jnp.where(low_k, dks[0], dks[1])
    dv = jnp.where(low_k, dvs[0], dvs[1])
    att_ref[...] = att
    dq_ref[...] = dq
    own_grad_ref[0] = dk[256:]
    own_grad_ref[1] = dv[256:]
    dk, dv = dk.astype(BF16), dv.astype(BF16)
    far_grad_ref[0] = dk[:128]
    far_grad_ref[1] = dv[:128]
    near_grad_ref[0] = dk[128:256]
    near_grad_ref[1] = dv[128:256]
    rounded = jnp.concatenate([dk, dv], axis=1)
    for half, out in ((0, send_ref), (1, keep_ref)):
        tp = tp_ref[half]
        t_own, t_out = tp[:, :LANES], tp[:, LANES:]
        out[:, :256] = dot(t_out, att).astype(BF16)
        out[:, 256:512] = dot(t_own, dq).astype(BF16)
        out[:, 512:] = (dot(t_own, rounded[256:]) + dot(th_ref[half], rounded[:256])).astype(BF16)


def attention(first, steps, place, far, near, own, q, da, wk, wv, tp, th):
    def columns(rows, cols):
        return pl.BlockSpec((rows, cols), lambda i: (0, first + i))

    def fresh(rows, cols):
        return pl.BlockSpec((rows, cols), lambda i: (0, i))

    def struct(rows, cols, dtype):
        return jax.ShapeDtypeStruct((rows, cols * steps), dtype)

    return pl.pallas_call(
        attention_kernel,
        grid=(steps,),
        out_shape=(
            struct(ROWS, QCOLS, BF16),
            struct(ROWS, QCOLS, BF16),
            jax.ShapeDtypeStruct((2, ROWS, KCOLS * steps), F32),
            jax.ShapeDtypeStruct((2, ROWS, KCOLS * steps), BF16),
            jax.ShapeDtypeStruct((2, ROWS, KCOLS * steps), BF16),
            struct(512, GCOLS, BF16),
            struct(512, GCOLS, BF16),
        ),
        in_specs=[
            pl.BlockSpec(memory_space=pltpu.SMEM),
            whole(ROWS, MODEL),
            whole(ROWS, MODEL),
            whole(ROWS, MODEL),
            columns(ROWS, QCOLS),
            columns(ROWS, QCOLS),
            columns(MODEL, KCOLS),
            columns(MODEL, KCOLS),
            whole(2, 512, 2 * LANES),
            whole(2, 512, 2 * LANES),
        ],
        out_specs=(
            fresh(ROWS, QCOLS),
            fresh(ROWS, QCOLS),
            pl.BlockSpec((2, ROWS, KCOLS), lambda i: (0, 0, i)),
            pl.BlockSpec((2, ROWS, KCOLS), lambda i: (0, 0, i)),
            pl.BlockSpec((2, ROWS, KCOLS), lambda i: (0, 0, i)),
            fresh(512, GCOLS),
            fresh(512, GCOLS),
        ),
        compiler_params=pltpu.CompilerParams(
            dimension_semantics=("arbitrary",), vmem_limit_bytes=28 << 20
        ),
        cost_estimate=SMALL,
        name="attention",
    )(place, far, near, own, q, da, wk, wv, tp, th)


def cut(addends, rows):
    total = addends[0][rows, :].astype(F32)
    for other in addends[1:]:
        total = total + other[rows, :].astype(F32)
    return total


def fold_kernel(count, quarter, *refs):
    addends, outs = refs[:count], refs[count:]
    for d in range(4):
        outs[d][...] = cut(addends, slice(d * quarter, (d + 1) * quarter)).astype(outs[d].dtype)


def folded(*addends):
    rows, cols = addends[0].shape
    quarter = rows // 4
    return pl.pallas_call(
        functools.partial(fold_kernel, len(addends), quarter),
        grid=(cols // GCOLS,),
        out_shape=tuple(
            jax.ShapeDtypeStruct((quarter, cols), BF16 if d else F32) for d in range(4)
        ),
        in_specs=[pl.BlockSpec((rows, GCOLS), lambda i: (0, i))] * len(addends),
        out_specs=(pl.BlockSpec((quarter, GCOLS), lambda i: (0, i)),) * 4,
        compiler_params=pltpu.CompilerParams(vmem_limit_bytes=12 << 20),
        name="fold",
    )(*addends)


def column_kernel(counts, *refs):
    out_ref, sum_ref = refs[-2], refs[-1]
    at, col = 0, 0
    for count in counts:
        total = cut(refs[at : at + count], slice(0, 32))
        at += count
        sum_ref[:, col : col + total.shape[1]] = total
        col += total.shape[1]
    low = lax.broadcasted_iota(jnp.int32, (8, LANES), 0) < 4
    for z in range(4):
        for block in range(0, 24, 4):
            even, odd = [], []
            for pair in range(2):
                c = (block + 2 * pair) * LANES
                one = sum_ref[8 * z : 8 * z + 8, c : c + LANES]
                two = sum_ref[8 * z : 8 * z + 8, c + LANES : c + 2 * LANES]
                even.append(jnp.where(low, one, pltpu.roll(two, 4, 0)))
                odd.append(jnp.where(low, pltpu.roll(one, 4, 0), two))
            rows = slice(block * 4, block * 4 + 16)
            out_ref[2 * z, rows, :] = jnp.concatenate(even, 0).astype(BF16)
            out_ref[2 * z + 1, rows, :] = jnp.concatenate(odd, 0).astype(BF16)


def in_column_order(*groups):
    args = [a for group in groups for a in group]
    return pl.pallas_call(
        functools.partial(column_kernel, tuple(len(group) for group in groups)),
        grid=(1,),
        out_shape=jax.ShapeDtypeStruct((8, 96, LANES), BF16),
        in_specs=[whole(*a.shape) for a in args],
        out_specs=whole(8, 96, LANES),
        scratch_shapes=[pltpu.VMEM((32, 4 * GCOLS), F32)],
        compiler_params=pltpu.CompilerParams(vmem_limit_bytes=8 << 20),
        name="column",
    )(*args)


def last_kernel(got_ref, q_ref, k_ref, v_ref, o_ref):
    total = got_ref[0].astype(F32)
    for i in range(1, 8):
        total = total + got_ref[i].astype(F32)
    for step in range(STEPS):
        base = step * 24
        out, q, kv = (total[base + 8 * i : base + 8 * i + 8] for i in range(3))
        for ref, pair in ((o_ref, out), (q_ref, q)):
            ref[:, step * 256 : step * 256 + 128] = pair[:4]
            ref[:, step * 256 + 128 : step * 256 + 256] = pair[4:]
        k_ref[:, step * 128 : step * 128 + 128] = kv[:4]
        v_ref[:, step * 128 : step * 128 + 128] = kv[4:]


def summed_last(got):
    shapes = [(4, 1024), (4, 512), (4, 512), (4, 1024)]
    return pl.pallas_call(
        last_kernel,
        grid=(1,),
        out_shape=tuple(jax.ShapeDtypeStruct(shape, F32) for shape in shapes),
        in_specs=[whole(8, 96, LANES)],
        out_specs=tuple(whole(*shape) for shape in shapes),
        compiler_params=pltpu.CompilerParams(vmem_limit_bytes=4 << 20),
        name="last",
    )(got)


def after(value, *others):
    return lax.optimization_barrier((value, *others))[0]


def shards(tokens, query_weight, key_weight, value_matrix, out_weight, out_cotangent):
    near = passed_along(tokens, 1)
    far = passed_along(tokens, 2)
    me = lax.axis_index(AXIS)
    start = jnp.maximum(2 - me, 0) * ROWS
    place = jnp.stack([(me // 8) % 4, (me // 2) % 4, me % 2, start]).astype(jnp.int32)
    q, da, tp = early(place, tokens, out_cotangent, in_hbm(query_weight), in_hbm(out_weight))
    th = prepared(place, far, near)

    wk, wv = in_hbm(key_weight), in_hbm(value_matrix)

    def attend(first, steps, place):
        return attention(
            first, steps, place, far, near, tokens, q, da, wk, wv, tp, th
        )

    one = attend(0, 3, place)
    got_one = to_mate(one[-2])
    two = attend(3, 1, after(place, one[-1]))
    got_two = to_mate(two[-2])
    own_one, *sends = folded(one[-1], after(got_one, two[-1]))
    ring_one = ring([None, *sends], 0)
    own_two, *sends = folded(two[-1], after(got_two, own_one))
    ring_two = ring([None, *(after(s, ring_one[0]) for s in sends)], 0)
    own_one, *sends = folded(own_one, *ring_one)
    ring_one = ring([None, *sends], 1)
    own_two, *sends = folded(own_two, *ring_two)
    ring_two = ring([None, *sends], 1)
    column = in_column_order([own_one, *ring_one], [own_two, *ring_two])
    got = lax.all_to_all(column, AXIS, 0, 0, axis_index_groups=Z_GROUPS, tiled=True)
    query_rows, key_rows, value_rows, out_rows = summed_last(got)

    parts = zip(one[:-2], two[:-2])
    att, dq, own_kv, near_kv, far_kv = (jnp.concatenate(p, axis=-1) for p in parts)
    back_near = passed_along(after(near_kv, own_two), -1)
    back_far = passed_along(after(far_kv, own_two), -2)
    attn_out = dot(att, out_weight).astype(BF16)
    kv = (own_kv + back_near.astype(F32) + back_far.astype(F32)).astype(BF16)
    tokens_grad = (
        dot(dq, query_weight, NT) + dot(kv[0], key_weight, NT) + dot(kv[1], value_matrix, NT)
    ).astype(BF16)

    return attn_out, tokens_grad, query_rows, key_rows, value_rows, out_rows.T


def solution(mesh):
    rows = P(AXIS, None)
    return jax.shard_map(
        shards,
        mesh=mesh,
        in_specs=(rows, P(), P(), P(), P(), rows),
        out_specs=(rows, rows, rows, rows, rows, P(None, AXIS)),
        check_vma=False,
    )
```

```python
import functools

import jax
import jax.numpy as jnp
from jax import lax
from jax.experimental import pallas as pl
from jax.experimental.pallas import tpu as pltpu
from jax.sharding import PartitionSpec as P

AXIS = "seq"
ROWS = 128
MODEL = 1024
LANES = 128
STEPS = 4
QCOLS = 256
KCOLS = 128
GCOLS = 768
SCALE = 0.125
MASKED = -1e30
BF16 = jnp.bfloat16
SMALL = pl.CostEstimate(flops=1000, transcendentals=0, bytes_accessed=1000)
F32 = jnp.float32
NT = (((1,), (1,)), ((), ()))
TN = (((0,), (0,)), ((), ()))


def dot(a, b, dims=(((1,), (0,)), ((), ()))):
    return lax.dot_general(a, b, dims, preferred_element_type=F32)


def flat(z, x, y, c):
    return ((z * 4 + x) * 4 + y) * 2 + c


def in_hbm(array):
    return pltpu.with_memory_space_constraint(array, pltpu.HBM)


def route_of(step):
    places = [(z, x, y, c) for z in range(8) for x in range(4) for y in range(4) for c in range(2)]
    return [(flat(*p), flat(*step(*p))) for p in places]


def to_mate(array):
    return lax.ppermute(array, AXIS, route_of(lambda z, x, y, c: (z, x, y, 1 - c)))


def plane_step(phase, d, z, x, y, c):
    if c == phase:
        return z, (x + d) % 4, y, c
    return z, x, (y + d) % 4, c


def ring(blocks, phase):
    return [
        lax.ppermute(blocks[d], AXIS, route_of(functools.partial(plane_step, phase, d)))
        for d in (1, 3, 2)
    ]


def along_z(block, distance):
    return lax.ppermute(
        block, AXIS, route_of(lambda z, x, y, c: ((z + distance) % 8, x, y, c))
    )


def passed_along(block, distance):
    devices = range(256)
    route = [(i - distance, i) for i in devices if i - distance in devices]
    return lax.ppermute(block, AXIS, route)


def reorder(place, t_ref, out_ref):
    x, y, core, mine = place[0], place[1], place[2], place[3]
    low = lax.broadcasted_iota(jnp.int32, (8, 2 * LANES), 0) < 4
    for half in range(2):
        target = 1 - core if half == 0 else core
        zero = target == 0
        for d1 in range(4):
            for d2 in range(4):
                xs = lax.rem(x + jnp.where(zero, d1, d2), 4)
                ys = lax.rem(y + jnp.where(zero, d2, d1), 4)
                for z in range(0, 8, 4):
                    rows = []
                    for pair in range(2):
                        base = xs * 32 + ys * 8
                        at = base + lax.rem(mine + z + 2 * pair, 8) * 128
                        one = t_ref[pl.ds(pl.multiple_of(at, 8), 8), :]
                        at = base + lax.rem(mine + z + 2 * pair + 1, 8) * 128
                        two = t_ref[pl.ds(pl.multiple_of(at, 8), 8), :]
                        c0 = jnp.where(low, one, pltpu.roll(two, 4, 0))
                        c1 = jnp.where(low, pltpu.roll(one, 4, 0), two)
                        rows.append(jnp.where(zero, c0, c1))
                    row = (d1 * 4 + d2) * 32 + z * 4
                    out_ref[half, row : row + 16, :] = jnp.concatenate(rows, 0).astype(BF16)


def early_kernel(place, tok_ref, cot_ref, wq_ref, wo_ref, q_ref, da_ref, out_ref, t_ref):
    q_ref[...] = dot(tok_ref[...], wq_ref[...]).astype(BF16)
    da_ref[...] = dot(cot_ref[...], wo_ref[...], NT).astype(BF16)

    @pl.when(pl.program_id(0) == 0)
    def _():
        t_ref[:, :LANES] = tok_ref[...].astype(F32).T
        t_ref[:, LANES:] = cot_ref[...].astype(F32).T
        reorder(place, t_ref, out_ref)


def whole(*shape):
    return pl.BlockSpec(shape, lambda i: (0,) * len(shape))


def early(place, tokens, cotangent, wq, wo):
    block = pl.BlockSpec((ROWS, QCOLS), lambda i: (0, i))
    return pl.pallas_call(
        early_kernel,
        grid=(STEPS,),
        out_shape=(
            jax.ShapeDtypeStruct((ROWS, MODEL), BF16),
            jax.ShapeDtypeStruct((ROWS, MODEL), BF16),
            jax.ShapeDtypeStruct((2, 512, 2 * LANES), BF16),
        ),
        in_specs=[
            pl.BlockSpec(memory_space=pltpu.SMEM),
            whole(ROWS, MODEL),
            whole(ROWS, MODEL),
            pl.BlockSpec((MODEL, QCOLS), lambda i: (0, i)),
            pl.BlockSpec((QCOLS, MODEL), lambda i: (i, 0)),
        ],
        out_specs=(block, block, whole(2, 512, 2 * LANES)),
        scratch_shapes=[pltpu.VMEM((MODEL, 2 * LANES), F32)],
        compiler_params=pltpu.CompilerParams(
            dimension_semantics=("arbitrary",), vmem_limit_bytes=20 << 20
        ),
        name="early",
    )(place, tokens, cotangent, wq, wo)


def prep_kernel(place, a_ref, b_ref, out_ref, t_ref):
    t_ref[:, :LANES] = a_ref[...].astype(F32).T
    t_ref[:, LANES:] = b_ref[...].astype(F32).T
    reorder(place, t_ref, out_ref)


def prepared(place, a, b):
    return pl.pallas_call(
        prep_kernel,
        grid=(1,),
        out_shape=jax.ShapeDtypeStruct((2, 512, 2 * LANES), BF16),
        in_specs=[pl.BlockSpec(memory_space=pltpu.SMEM), whole(ROWS, MODEL), whole(ROWS, MODEL)],
        out_specs=whole(2, 512, 2 * LANES),
        scratch_shapes=[pltpu.VMEM((MODEL, 2 * LANES), F32)],
        compiler_params=pltpu.CompilerParams(vmem_limit_bytes=12 << 20),
        name="prep",
    )(place, a, b)


def swapped(a):
    return pltpu.roll(a, 64, 1)


def attention_kernel(
    place,
    far_ref,
    near_ref,
    own_ref,
    q_ref,
    da_ref,
    wk_ref,
    wv_ref,
    tp_ref,
    th_ref,
    att_ref,
    dq_ref,
    own_grad_ref,
    near_grad_ref,
    far_grad_ref,
    send_ref,
    keep_ref,
):
    window = jnp.concatenate([far_ref[...], near_ref[...], own_ref[...]], axis=0)
    keys = dot(window, wk_ref[...])
    values = dot(window, wv_ref[...])
    start = place[4]
    row = lax.rem(lax.broadcasted_iota(jnp.int32, (256, 384), 0), 128)
    col = lax.broadcasted_iota(jnp.int32, (256, 384), 1)
    allowed = (col <= row + 256) & (col >= start)
    low_k = lax.broadcasted_iota(jnp.int32, (384, LANES), 1) < 64
    low_q = lax.broadcasted_iota(jnp.int32, (ROWS, LANES), 1) < 64
    zero = jnp.zeros((ROWS, LANES), BF16)
    keys_swapped, values_swapped = swapped(keys), swapped(values)
    atts, dqs, dks, dvs = [], [], [], []
    for head in range(2):
        own_half = low_k if head == 0 else ~low_k
        key = jnp.where(own_half, keys, keys_swapped).astype(BF16)
        value = jnp.where(own_half, values, values_swapped).astype(BF16)
        cols = slice(head * LANES, (head + 1) * LANES)
        q = q_ref[:, cols]
        da = da_ref[:, cols]
        q2 = jnp.concatenate([jnp.where(low_q, q, zero), jnp.where(low_q, zero, q)], 0)
        da2 = jnp.concatenate([jnp.where(low_q, da, zero), jnp.where(low_q, zero, da)], 0)
        scores = jnp.where(allowed, dot(q2, key, NT) * SCALE, MASKED)
        highest = jnp.max(scores, axis=-1, keepdims=True)
        weights = jnp.exp(scores - highest)
        weights = weights * (1.0 / jnp.sum(weights, axis=-1, keepdims=True))
        probs = weights.astype(BF16)
        both = dot(probs, value)
        att = jnp.where(low_q, both[:ROWS], both[ROWS:]).astype(BF16)
        att_f = att.astype(F32)
        delta = jnp.sum(
            da2.astype(F32) * jnp.concatenate([att_f, att_f], 0), axis=-1, keepdims=True
        )
        dscores = (weights * (dot(da2, value, NT) - delta)).astype(BF16)
        both = dot(dscores, key) * SCALE
        dqs.append(jnp.where(low_q, both[:ROWS], both[ROWS:]).astype(BF16))
        dk = dot(dscores, q2, TN) * SCALE
        dv = dot(probs, da2, TN)
        dks.append(dk + swapped(dk))
        dvs.append(dv + swapped(dv))
        atts.append(att)
    att = jnp.concatenate(atts, 1)
    dq = jnp.concatenate(dqs, 1)
    dk = jnp.where(low_k, dks[0], dks[1])
    dv = jnp.where(low_k, dvs[0], dvs[1])
    att_ref[...] = att
    dq_ref[...] = dq
    own_grad_ref[0] = dk[256:]
    own_grad_ref[1] = dv[256:]
    dk, dv = dk.astype(BF16), dv.astype(BF16)
    far_grad_ref[0] = dk[:128]
    far_grad_ref[1] = dv[:128]
    near_grad_ref[0] = dk[128:256]
    near_grad_ref[1] = dv[128:256]
    rounded = jnp.concatenate([dk, dv], axis=1)
    for half, out in ((0, send_ref), (1, keep_ref)):
        tp = tp_ref[half]
        t_own, t_out = tp[:, :LANES], tp[:, LANES:]
        out[:, :256] = dot(t_out, att).astype(BF16)
        out[:, 256:512] = dot(t_own, dq).astype(BF16)
        out[:, 512:] = (dot(t_own, rounded[256:]) + dot(th_ref[half], rounded[:256])).astype(BF16)


def attention(first, steps, place, far, near, own, q, da, wk, wv, tp, th):
    def columns(rows, cols):
        return pl.BlockSpec((rows, cols), lambda i: (0, first + i))

    def fresh(rows, cols):
        return pl.BlockSpec((rows, cols), lambda i: (0, i))

    def struct(rows, cols, dtype):
        return jax.ShapeDtypeStruct((rows, cols * steps), dtype)

    return pl.pallas_call(
        attention_kernel,
        grid=(steps,),
        out_shape=(
            struct(ROWS, QCOLS, BF16),
            struct(ROWS, QCOLS, BF16),
            jax.ShapeDtypeStruct((2, ROWS, KCOLS * steps), F32),
            jax.ShapeDtypeStruct((2, ROWS, KCOLS * steps), BF16),
            jax.ShapeDtypeStruct((2, ROWS, KCOLS * steps), BF16),
            struct(512, GCOLS, BF16),
            struct(512, GCOLS, BF16),
        ),
        in_specs=[
            pl.BlockSpec(memory_space=pltpu.SMEM),
            whole(ROWS, MODEL),
            whole(ROWS, MODEL),
            whole(ROWS, MODEL),
            columns(ROWS, QCOLS),
            columns(ROWS, QCOLS),
            columns(MODEL, KCOLS),
            columns(MODEL, KCOLS),
            whole(2, 512, 2 * LANES),
            whole(2, 512, 2 * LANES),
        ],
        out_specs=(
            fresh(ROWS, QCOLS),
            fresh(ROWS, QCOLS),
            pl.BlockSpec((2, ROWS, KCOLS), lambda i: (0, 0, i)),
            pl.BlockSpec((2, ROWS, KCOLS), lambda i: (0, 0, i)),
            pl.BlockSpec((2, ROWS, KCOLS), lambda i: (0, 0, i)),
            fresh(512, GCOLS),
            fresh(512, GCOLS),
        ),
        compiler_params=pltpu.CompilerParams(
            dimension_semantics=("arbitrary",), vmem_limit_bytes=28 << 20
        ),
        cost_estimate=SMALL,
        name="attention",
    )(place, far, near, own, q, da, wk, wv, tp, th)


def cut(addends, rows):
    total = addends[0][rows, :].astype(F32)
    for other in addends[1:]:
        total = total + other[rows, :].astype(F32)
    return total


def fold_kernel(count, quarter, *refs):
    addends, outs = refs[:count], refs[count:]
    for d in range(4):
        outs[d][...] = cut(addends, slice(d * quarter, (d + 1) * quarter)).astype(outs[d].dtype)


def folded(*addends):
    rows, cols = addends[0].shape
    quarter = rows // 4
    width = GCOLS if rows > 128 else cols
    return pl.pallas_call(
        functools.partial(fold_kernel, len(addends), quarter),
        grid=(cols // width,),
        out_shape=tuple(
            jax.ShapeDtypeStruct((quarter, cols), BF16 if d else F32) for d in range(4)
        ),
        in_specs=[pl.BlockSpec((rows, width), lambda i: (0, i))] * len(addends),
        out_specs=(pl.BlockSpec((quarter, width), lambda i: (0, i)),) * 4,
        compiler_params=pltpu.CompilerParams(vmem_limit_bytes=12 << 20),
        name="fold",
    )(*addends)


def join_kernel(*refs):
    one, two, outs = refs[:4], refs[4:8], refs[8:]
    split = one[0].shape[1]
    for d in range(4):
        rows = slice(d * 32, (d + 1) * 32)
        outs[d][:, :split] = cut(one, rows).astype(outs[d].dtype)
        outs[d][:, split:] = cut(two, rows).astype(outs[d].dtype)


def joined(one, two):
    args = [*one, *two]
    cols = one[0].shape[1] + two[0].shape[1]
    return pl.pallas_call(
        join_kernel,
        grid=(1,),
        out_shape=tuple(jax.ShapeDtypeStruct((32, cols), BF16 if d else F32) for d in range(4)),
        in_specs=[whole(*a.shape) for a in args],
        out_specs=(whole(32, cols),) * 4,
        compiler_params=pltpu.CompilerParams(vmem_limit_bytes=16 << 20),
        name="join",
    )(*args)


def halve_kernel(own_ref, a_ref, b_ref, c_ref, keep_ref, send_ref):
    total = cut((own_ref, a_ref, b_ref, c_ref), slice(0, 8))
    keep_ref[...] = total[:4]
    send_ref[...] = total[4:].astype(BF16)


def halved(*addends):
    cols = addends[0].shape[1]
    return pl.pallas_call(
        halve_kernel,
        grid=(1,),
        out_shape=(
            jax.ShapeDtypeStruct((4, cols), F32),
            jax.ShapeDtypeStruct((4, cols), BF16),
        ),
        in_specs=[whole(8, cols)] * 4,
        out_specs=(whole(4, cols),) * 2,
        compiler_params=pltpu.CompilerParams(vmem_limit_bytes=4 << 20),
        name="halve",
    )(*addends)


def last_kernel(own_ref, got_ref, q_ref, k_ref, v_ref, o_ref):
    total = own_ref[...] + got_ref[...].astype(F32)
    for step in range(STEPS):
        base = step * GCOLS
        at = slice(step * 256, step * 256 + 256)
        o_ref[:, at] = total[:, base : base + 256]
        q_ref[:, at] = total[:, base + 256 : base + 512]
        at = slice(step * 128, step * 128 + 128)
        k_ref[:, at] = total[:, base + 512 : base + 640]
        v_ref[:, at] = total[:, base + 640 : base + 768]


def summed_last(own, got):
    shapes = [(4, 1024), (4, 512), (4, 512), (4, 1024)]
    return pl.pallas_call(
        last_kernel,
        grid=(1,),
        out_shape=tuple(jax.ShapeDtypeStruct(shape, F32) for shape in shapes),
        in_specs=[whole(*own.shape)] * 2,
        out_specs=tuple(whole(*shape) for shape in shapes),
        compiler_params=pltpu.CompilerParams(vmem_limit_bytes=4 << 20),
        name="last",
    )(own, got)


def after(value, *others):
    return lax.optimization_barrier((value, *others))[0]


def shards(tokens, query_weight, key_weight, value_matrix, out_weight, out_cotangent):
    near = passed_along(tokens, 1)
    far = passed_along(tokens, 2)
    me = lax.axis_index(AXIS)
    start = jnp.maximum(2 - me, 0) * ROWS
    place = jnp.stack([(me // 8) % 4, (me // 2) % 4, me % 2, me // 32, start]).astype(jnp.int32)
    q, da, tp = early(place, tokens, out_cotangent, in_hbm(query_weight), in_hbm(out_weight))
    th = prepared(place, far, near)

    wk, wv = in_hbm(key_weight), in_hbm(value_matrix)

    def attend(first, steps, place):
        return attention(
            first, steps, place, far, near, tokens, q, da, wk, wv, tp, th
        )

    one = attend(0, 3, place)
    got_one = to_mate(one[-2])
    two = attend(3, 1, after(place, one[-1]))
    got_two = to_mate(two[-2])
    own_one, *sends = folded(one[-1], after(got_one, two[-1]))
    ring_one = ring([None, *sends], 0)
    own_two, *sends = folded(two[-1], after(got_two, own_one))
    ring_two = ring([None, *(after(s, ring_one[0]) for s in sends)], 0)
    own, *sends = joined([own_one, *ring_one], [own_two, *ring_two])
    ring_three = ring([None, *sends], 1)
    own, *sends = folded(own, *ring_three)
    ring_four = [along_z(block, 2 * d) for d, block in ((1, sends[0]), (3, sends[2]), (2, sends[1]))]
    z_own = own
    own, send = halved(own, *ring_four)
    got = along_z(send, 1)
    query_rows, key_rows, value_rows, out_rows = summed_last(own, got)

    parts = zip(one[:-2], two[:-2])
    att, dq, own_kv, near_kv, far_kv = (jnp.concatenate(p, axis=-1) for p in parts)
    back_near = passed_along(after(near_kv, z_own), -1)
    back_far = passed_along(after(far_kv, z_own), -2)
    attn_out = dot(att, out_weight).astype(BF16)
    kv = (own_kv + back_near.astype(F32) + back_far.astype(F32)).astype(BF16)
    tokens_grad = (
        dot(dq, query_weight, NT) + dot(kv[0], key_weight, NT) + dot(kv[1], value_matrix, NT)
    ).astype(BF16)

    return attn_out, tokens_grad, query_rows, key_rows, value_rows, out_rows.T


def solution(mesh):
    rows = P(AXIS, None)
    return jax.shard_map(
        shards,
        mesh=mesh,
        in_specs=(rows, P(), P(), P(), P(), rows),
        out_specs=(rows, rows, rows, rows, rows, P(None, AXIS)),
        check_vma=False,
    )
```

```python
import functools

import jax
import jax.numpy as jnp
from jax import lax
from jax.experimental import pallas as pl
from jax.experimental.pallas import tpu as pltpu
from jax.sharding import PartitionSpec as P

AXIS = "seq"
ROWS = 128
MODEL = 1024
LANES = 128
STEPS = 4
QCOLS = 256
KCOLS = 128
GCOLS = 768
SCALE = 0.125
MASKED = -1e30
BF16 = jnp.bfloat16
SMALL = pl.CostEstimate(flops=1000, transcendentals=0, bytes_accessed=1000)
F32 = jnp.float32
NT = (((1,), (1,)), ((), ()))
TN = (((0,), (0,)), ((), ()))


def dot(a, b, dims=(((1,), (0,)), ((), ()))):
    return lax.dot_general(a, b, dims, preferred_element_type=F32)


def flat(z, x, y, c):
    return ((z * 4 + x) * 4 + y) * 2 + c


def in_hbm(array):
    return pltpu.with_memory_space_constraint(array, pltpu.HBM)


def route_of(step):
    places = [(z, x, y, c) for z in range(8) for x in range(4) for y in range(4) for c in range(2)]
    return [(flat(*p), flat(*step(*p))) for p in places]


def to_mate(array):
    return lax.ppermute(array, AXIS, route_of(lambda z, x, y, c: (z, x, y, 1 - c)))


def plane_step(phase, d, z, x, y, c):
    if c == phase:
        return z, (x + d) % 4, y, c
    return z, x, (y + d) % 4, c


def ring(blocks, phase):
    return [
        lax.ppermute(blocks[d], AXIS, route_of(functools.partial(plane_step, phase, d)))
        for d in (1, 3, 2)
    ]


def along_z(block, distance):
    return lax.ppermute(
        block, AXIS, route_of(lambda z, x, y, c: ((z + distance) % 8, x, y, c))
    )


def passed_along(block, distance):
    devices = range(256)
    route = [(i - distance, i) for i in devices if i - distance in devices]
    return lax.ppermute(block, AXIS, route)


def reorder(place, t_ref, out_ref):
    x, y, core, mine = place[0], place[1], place[2], place[3]
    low = lax.broadcasted_iota(jnp.int32, (8, 2 * LANES), 0) < 4
    for half in range(2):
        target = 1 - core if half == 0 else core
        zero = target == 0
        for d1 in range(4):
            for d2 in range(4):
                xs = lax.rem(x + jnp.where(zero, d1, d2), 4)
                ys = lax.rem(y + jnp.where(zero, d2, d1), 4)
                for z in range(0, 8, 4):
                    rows = []
                    for pair in range(2):
                        base = xs * 32 + ys * 8
                        at = base + lax.rem(mine + z + 2 * pair, 8) * 128
                        one = t_ref[pl.ds(pl.multiple_of(at, 8), 8), :]
                        at = base + lax.rem(mine + z + 2 * pair + 1, 8) * 128
                        two = t_ref[pl.ds(pl.multiple_of(at, 8), 8), :]
                        c0 = jnp.where(low, one, pltpu.roll(two, 4, 0))
                        c1 = jnp.where(low, pltpu.roll(one, 4, 0), two)
                        rows.append(jnp.where(zero, c0, c1))
                    row = (d1 * 4 + d2) * 32 + z * 4
                    out_ref[half, row : row + 16, :] = jnp.concatenate(rows, 0).astype(BF16)


def early_kernel(place, tok_ref, cot_ref, wq_ref, wo_ref, q_ref, da_ref, out_ref, t_ref):
    q_ref[...] = dot(tok_ref[...], wq_ref[...]).astype(BF16)
    da_ref[...] = dot(cot_ref[...], wo_ref[...], NT).astype(BF16)

    @pl.when(pl.program_id(0) == 0)
    def _():
        t_ref[:, :LANES] = tok_ref[...].astype(F32).T
        t_ref[:, LANES:] = cot_ref[...].astype(F32).T
        reorder(place, t_ref, out_ref)


def whole(*shape):
    return pl.BlockSpec(shape, lambda i: (0,) * len(shape))


def early(place, tokens, cotangent, wq, wo):
    block = pl.BlockSpec((ROWS, QCOLS), lambda i: (0, i))
    return pl.pallas_call(
        early_kernel,
        grid=(STEPS,),
        out_shape=(
            jax.ShapeDtypeStruct((ROWS, MODEL), BF16),
            jax.ShapeDtypeStruct((ROWS, MODEL), BF16),
            jax.ShapeDtypeStruct((2, 512, 2 * LANES), BF16),
        ),
        in_specs=[
            pl.BlockSpec(memory_space=pltpu.SMEM),
            whole(ROWS, MODEL),
            whole(ROWS, MODEL),
            pl.BlockSpec((MODEL, QCOLS), lambda i: (0, i)),
            pl.BlockSpec((QCOLS, MODEL), lambda i: (i, 0)),
        ],
        out_specs=(block, block, whole(2, 512, 2 * LANES)),
        scratch_shapes=[pltpu.VMEM((MODEL, 2 * LANES), F32)],
        compiler_params=pltpu.CompilerParams(
            dimension_semantics=("arbitrary",), vmem_limit_bytes=20 << 20
        ),
        name="early",
    )(place, tokens, cotangent, wq, wo)


def prep_kernel(place, a_ref, b_ref, out_ref, t_ref):
    t_ref[:, :LANES] = a_ref[...].astype(F32).T
    t_ref[:, LANES:] = b_ref[...].astype(F32).T
    reorder(place, t_ref, out_ref)


def prepared(place, a, b):
    return pl.pallas_call(
        prep_kernel,
        grid=(1,),
        out_shape=jax.ShapeDtypeStruct((2, 512, 2 * LANES), BF16),
        in_specs=[pl.BlockSpec(memory_space=pltpu.SMEM), whole(ROWS, MODEL), whole(ROWS, MODEL)],
        out_specs=whole(2, 512, 2 * LANES),
        scratch_shapes=[pltpu.VMEM((MODEL, 2 * LANES), F32)],
        compiler_params=pltpu.CompilerParams(vmem_limit_bytes=12 << 20),
        name="prep",
    )(place, a, b)


def swapped(a):
    return pltpu.roll(a, 64, 1)


def attention_kernel(
    place,
    far_ref,
    near_ref,
    own_ref,
    q_ref,
    da_ref,
    wk_ref,
    wv_ref,
    tp_ref,
    th_ref,
    att_ref,
    dq_ref,
    own_grad_ref,
    near_grad_ref,
    far_grad_ref,
    send_ref,
    keep_ref,
):
    window = jnp.concatenate([far_ref[...], near_ref[...], own_ref[...]], axis=0)
    keys = dot(window, wk_ref[...])
    values = dot(window, wv_ref[...])
    start = place[4]
    row = lax.rem(lax.broadcasted_iota(jnp.int32, (256, 384), 0), 128)
    col = lax.broadcasted_iota(jnp.int32, (256, 384), 1)
    allowed = (col <= row + 256) & (col >= start)
    low_k = lax.broadcasted_iota(jnp.int32, (384, LANES), 1) < 64
    low_q = lax.broadcasted_iota(jnp.int32, (ROWS, LANES), 1) < 64
    zero = jnp.zeros((ROWS, LANES), BF16)
    keys_swapped, values_swapped = swapped(keys), swapped(values)
    atts, dqs, dks, dvs = [], [], [], []
    for head in range(2):
        own_half = low_k if head == 0 else ~low_k
        key = jnp.where(own_half, keys, keys_swapped).astype(BF16)
        value = jnp.where(own_half, values, values_swapped).astype(BF16)
        cols = slice(head * LANES, (head + 1) * LANES)
        q = q_ref[:, cols]
        da = da_ref[:, cols]
        q2 = jnp.concatenate([jnp.where(low_q, q, zero), jnp.where(low_q, zero, q)], 0)
        da2 = jnp.concatenate([jnp.where(low_q, da, zero), jnp.where(low_q, zero, da)], 0)
        scores = jnp.where(allowed, dot(q2, key, NT) * SCALE, MASKED)
        highest = jnp.max(scores, axis=-1, keepdims=True)
        weights = jnp.exp(scores - highest)
        weights = weights * (1.0 / jnp.sum(weights, axis=-1, keepdims=True))
        probs = weights.astype(BF16)
        both = dot(probs, value)
        att = jnp.where(low_q, both[:ROWS], both[ROWS:]).astype(BF16)
        att_f = att.astype(F32)
        delta = jnp.sum(
            da2.astype(F32) * jnp.concatenate([att_f, att_f], 0), axis=-1, keepdims=True
        )
        dscores = (weights * (dot(da2, value, NT) - delta)).astype(BF16)
        both = dot(dscores, key) * SCALE
        dqs.append(jnp.where(low_q, both[:ROWS], both[ROWS:]).astype(BF16))
        dk = dot(dscores, q2, TN) * SCALE
        dv = dot(probs, da2, TN)
        dks.append(dk + swapped(dk))
        dvs.append(dv + swapped(dv))
        atts.append(att)
    att = jnp.concatenate(atts, 1)
    dq = jnp.concatenate(dqs, 1)
    dk = jnp.where(low_k, dks[0], dks[1])
    dv = jnp.where(low_k, dvs[0], dvs[1])
    att_ref[...] = att
    dq_ref[...] = dq
    own_grad_ref[0] = dk[256:]
    own_grad_ref[1] = dv[256:]
    dk, dv = dk.astype(BF16), dv.astype(BF16)
    far_grad_ref[0] = dk[:128]
    far_grad_ref[1] = dv[:128]
    near_grad_ref[0] = dk[128:256]
    near_grad_ref[1] = dv[128:256]
    rounded = jnp.concatenate([dk, dv], axis=1)
    for half, out in ((0, send_ref), (1, keep_ref)):
        tp = tp_ref[half]
        t_own, t_out = tp[:, :LANES], tp[:, LANES:]
        out[:, :256] = dot(t_out, att).astype(BF16)
        out[:, 256:512] = dot(t_own, dq).astype(BF16)
        out[:, 512:] = (dot(t_own, rounded[256:]) + dot(th_ref[half], rounded[:256])).astype(BF16)


def attention(first, steps, place, far, near, own, q, da, wk, wv, tp, th):
    def columns(rows, cols):
        return pl.BlockSpec((rows, cols), lambda i: (0, first + i))

    def fresh(rows, cols):
        return pl.BlockSpec((rows, cols), lambda i: (0, i))

    def struct(rows, cols, dtype):
        return jax.ShapeDtypeStruct((rows, cols * steps), dtype)

    return pl.pallas_call(
        attention_kernel,
        grid=(steps,),
        out_shape=(
            struct(ROWS, QCOLS, BF16),
            struct(ROWS, QCOLS, BF16),
            jax.ShapeDtypeStruct((2, ROWS, KCOLS * steps), F32),
            jax.ShapeDtypeStruct((2, ROWS, KCOLS * steps), BF16),
            jax.ShapeDtypeStruct((2, ROWS, KCOLS * steps), BF16),
            struct(512, GCOLS, BF16),
            struct(512, GCOLS, BF16),
        ),
        in_specs=[
            pl.BlockSpec(memory_space=pltpu.SMEM),
            whole(ROWS, MODEL),
            whole(ROWS, MODEL),
            whole(ROWS, MODEL),
            columns(ROWS, QCOLS),
            columns(ROWS, QCOLS),
            columns(MODEL, KCOLS),
            columns(MODEL, KCOLS),
            whole(2, 512, 2 * LANES),
            whole(2, 512, 2 * LANES),
        ],
        out_specs=(
            fresh(ROWS, QCOLS),
            fresh(ROWS, QCOLS),
            pl.BlockSpec((2, ROWS, KCOLS), lambda i: (0, 0, i)),
            pl.BlockSpec((2, ROWS, KCOLS), lambda i: (0, 0, i)),
            pl.BlockSpec((2, ROWS, KCOLS), lambda i: (0, 0, i)),
            fresh(512, GCOLS),
            fresh(512, GCOLS),
        ),
        compiler_params=pltpu.CompilerParams(
            dimension_semantics=("arbitrary",), vmem_limit_bytes=28 << 20
        ),
        cost_estimate=SMALL,
        name="attention",
    )(place, far, near, own, q, da, wk, wv, tp, th)


def cut(addends, rows):
    total = addends[0][rows, :].astype(F32)
    for other in addends[1:]:
        total = total + other[rows, :].astype(F32)
    return total


def fold_kernel(count, quarter, *refs):
    addends, outs = refs[:count], refs[count:]
    for d in range(4):
        outs[d][...] = cut(addends, slice(d * quarter, (d + 1) * quarter)).astype(outs[d].dtype)


def folded(*addends):
    rows, cols = addends[0].shape
    return pl.pallas_call(
        functools.partial(fold_kernel, len(addends), rows // 4),
        grid=(1,),
        out_shape=tuple(
            jax.ShapeDtypeStruct((rows // 4, cols), BF16 if d else F32) for d in range(4)
        ),
        in_specs=[whole(rows, cols)] * len(addends),
        out_specs=(whole(rows // 4, cols),) * 4,
        compiler_params=pltpu.CompilerParams(vmem_limit_bytes=20 << 20),
        name="fold",
    )(*addends)


def place_kernel(count, *refs):
    fold_kernel(2, 128, *refs[:2], *refs[2 + count :])


def folded_into(first, keep, got, wide=()):
    rows, cols = keep.shape
    given = pl.BlockSpec((rows, GCOLS), lambda i: (0, i))
    return pl.pallas_call(
        functools.partial(place_kernel, len(wide)),
        grid=(cols // GCOLS,),
        out_shape=tuple(
            jax.ShapeDtypeStruct((rows // 4, STEPS * GCOLS), BF16 if d else F32) for d in range(4)
        ),
        in_specs=[given, given] + [pl.BlockSpec(memory_space=pl.ANY)] * len(wide),
        out_specs=(pl.BlockSpec((rows // 4, GCOLS), lambda i: (0, first + i)),) * 4,
        input_output_aliases={2 + d: d for d in range(len(wide))},
        compiler_params=pltpu.CompilerParams(vmem_limit_bytes=12 << 20),
        name="place",
    )(keep, got, *wide)


def halve_kernel(own_ref, a_ref, b_ref, c_ref, keep_ref, send_ref):
    total = cut((own_ref, a_ref, b_ref, c_ref), slice(0, 8))
    keep_ref[...] = total[:4]
    send_ref[...] = total[4:].astype(BF16)


def halved(*addends):
    cols = addends[0].shape[1]
    return pl.pallas_call(
        halve_kernel,
        grid=(1,),
        out_shape=(
            jax.ShapeDtypeStruct((4, cols), F32),
            jax.ShapeDtypeStruct((4, cols), BF16),
        ),
        in_specs=[whole(8, cols)] * 4,
        out_specs=(whole(4, cols),) * 2,
        compiler_params=pltpu.CompilerParams(vmem_limit_bytes=4 << 20),
        name="halve",
    )(*addends)


def last_kernel(own_ref, got_ref, q_ref, k_ref, v_ref, o_ref):
    total = own_ref[...] + got_ref[...].astype(F32)
    for step in range(STEPS):
        base = step * GCOLS
        at = slice(step * 256, step * 256 + 256)
        o_ref[:, at] = total[:, base : base + 256]
        q_ref[:, at] = total[:, base + 256 : base + 512]
        at = slice(step * 128, step * 128 + 128)
        k_ref[:, at] = total[:, base + 512 : base + 640]
        v_ref[:, at] = total[:, base + 640 : base + 768]


def summed_last(own, got):
    shapes = [(4, 1024), (4, 512), (4, 512), (4, 1024)]
    return pl.pallas_call(
        last_kernel,
        grid=(1,),
        out_shape=tuple(jax.ShapeDtypeStruct(shape, F32) for shape in shapes),
        in_specs=[whole(*own.shape)] * 2,
        out_specs=tuple(whole(*shape) for shape in shapes),
        compiler_params=pltpu.CompilerParams(vmem_limit_bytes=4 << 20),
        name="last",
    )(own, got)


def middle_kernel(att_ref, dq_ref, wo_ref, wq_ref, out_ref, base_ref):
    out_ref[...] = dot(att_ref[...], wo_ref[...]).astype(BF16)
    base_ref[...] = dot(dq_ref[...], wq_ref[...], NT)


def middle(att, dq, wo, wq):
    block = pl.BlockSpec((ROWS, QCOLS), lambda i: (0, i))
    return pl.pallas_call(
        middle_kernel,
        grid=(STEPS,),
        out_shape=(
            jax.ShapeDtypeStruct((ROWS, MODEL), BF16),
            jax.ShapeDtypeStruct((ROWS, MODEL), F32),
        ),
        in_specs=[
            whole(ROWS, MODEL),
            whole(ROWS, MODEL),
            pl.BlockSpec((MODEL, QCOLS), lambda i: (0, i)),
            pl.BlockSpec((QCOLS, MODEL), lambda i: (i, 0)),
        ],
        out_specs=(block, block),
        compiler_params=pltpu.CompilerParams(vmem_limit_bytes=12 << 20),
        name="middle",
    )(att, dq, wo, wq)


def tail_kernel(base_ref, own_ref, near_ref, far_ref, wk_ref, wv_ref, out_ref):
    total = base_ref[...]
    for i, w_ref in enumerate((wk_ref, wv_ref)):
        grad = own_ref[i] + near_ref[i].astype(F32) + far_ref[i].astype(F32)
        total = total + dot(grad.astype(BF16), w_ref[...], NT)
    out_ref[...] = total.astype(BF16)


def tail(base, own, near, far, wk, wv):
    block = pl.BlockSpec((ROWS, QCOLS), lambda i: (0, i))
    return pl.pallas_call(
        tail_kernel,
        grid=(STEPS,),
        out_shape=jax.ShapeDtypeStruct((ROWS, MODEL), BF16),
        in_specs=[block, *[whole(2, ROWS, 512)] * 3]
        + [pl.BlockSpec((QCOLS, 512), lambda i: (i, 0))] * 2,
        out_specs=block,
        compiler_params=pltpu.CompilerParams(vmem_limit_bytes=12 << 20),
        name="tail",
    )(base, own, near, far, wk, wv)


def after(value, *others):
    return lax.optimization_barrier((value, *others))[0]


def shards(tokens, query_weight, key_weight, value_matrix, out_weight, out_cotangent):
    far = passed_along(tokens, 2)
    near = passed_along(tokens, 1)
    me = lax.axis_index(AXIS)
    start = jnp.maximum(2 - me, 0) * ROWS
    place = jnp.stack([(me // 8) % 4, (me // 2) % 4, me % 2, me // 32, start]).astype(jnp.int32)
    wq, wk, wv, wo = map(in_hbm, (query_weight, key_weight, value_matrix, out_weight))
    q, da, tp = early(place, in_hbm(tokens), in_hbm(out_cotangent), wq, wo)
    th = prepared(place, far, near)

    def attend(first, steps, place):
        return attention(first, steps, place, far, near, tokens, q, da, wk, wv, tp, th)

    one = attend(0, 3, place)
    got_one = to_mate(one[-2])
    two = attend(3, 1, after(place, one[-1]))
    got_two = to_mate(two[-2])
    sums = folded_into(0, one[-1], after(got_one, two[-1]))
    own, *sends = folded_into(3, two[-1], after(got_two, sums[0]), sums)
    ring_one = ring([None, *sends], 0)

    parts = zip(one[:-2], two[:-2])
    att, dq, own_kv, near_kv, far_kv = (jnp.concatenate(p, axis=-1) for p in parts)
    back_near = passed_along(after(near_kv, ring_one[0]), -1)
    back_far = passed_along(after(far_kv, ring_one[0]), -2)
    attn_out, base = middle(after(att, own), after(dq, own), wo, wq)

    own, *sends = folded(after(own, base), *ring_one)
    ring_two = ring([None, *sends], 1)
    own, *sends = folded(own, *ring_two)
    ring_three = [along_z(sends[d - 1], 2 * d) for d in (1, 3, 2)]
    own, send = halved(own, *ring_three)
    got = along_z(send, 1)
    tokens_grad = tail(base, own_kv, back_near, back_far, wk, wv)
    query_rows, key_rows, value_rows, out_rows = summed_last(after(own, tokens_grad), got)
    return attn_out, tokens_grad, query_rows, key_rows, value_rows, out_rows.T


def solution(mesh):
    rows = P(AXIS, None)
    return jax.shard_map(
        shards,
        mesh=mesh,
        in_specs=(rows, P(), P(), P(), P(), rows),
        out_specs=(rows, rows, rows, rows, rows, P(None, AXIS)),
        check_vma=False,
    )
```

```python
import functools

import jax
import jax.numpy as jnp
from jax import lax
from jax.experimental import pallas as pl
from jax.experimental.pallas import tpu as pltpu
from jax.sharding import PartitionSpec as P

AXIS = "seq"
ROWS = 128
MODEL = 1024
LANES = 128
STEPS = 4
QCOLS = 256
KCOLS = 128
GCOLS = 768
SCALE = 0.125
MASKED = -1e30
BF16 = jnp.bfloat16
SMALL = pl.CostEstimate(flops=1000, transcendentals=0, bytes_accessed=1000)
F32 = jnp.float32
NT = (((1,), (1,)), ((), ()))
TN = (((0,), (0,)), ((), ()))


def dot(a, b, dims=(((1,), (0,)), ((), ()))):
    return lax.dot_general(a, b, dims, preferred_element_type=F32)


def flat(z, x, y, c):
    return ((z * 4 + x) * 4 + y) * 2 + c


def in_hbm(array):
    return pltpu.with_memory_space_constraint(array, pltpu.HBM)


def route_of(step):
    places = [(z, x, y, c) for z in range(8) for x in range(4) for y in range(4) for c in range(2)]
    return [(flat(*p), flat(*step(*p))) for p in places]


def to_mate(array):
    return lax.ppermute(array, AXIS, route_of(lambda z, x, y, c: (z, x, y, 1 - c)))


def plane_step(phase, d, z, x, y, c):
    if c == phase:
        return z, (x + d) % 4, y, c
    return z, x, (y + d) % 4, c


def ring(blocks, phase):
    return [
        lax.ppermute(blocks[d], AXIS, route_of(functools.partial(plane_step, phase, d)))
        for d in (1, 3, 2)
    ]


def along_z(block, distance):
    return lax.ppermute(
        block, AXIS, route_of(lambda z, x, y, c: ((z + distance) % 8, x, y, c))
    )


def passed_along(block, distance, sources=range(256)):
    return lax.ppermute(
        block, AXIS, [(i, i + distance) for i in sources if i + distance in range(256)]
    )


def reorder(place, t_ref, out_ref):
    x, y, core, mine = place[0], place[1], place[2], place[3]
    low = lax.broadcasted_iota(jnp.int32, (8, 2 * LANES), 0) < 4
    for half in range(2):
        target = 1 - core if half == 0 else core
        zero = target == 0
        for d1 in range(4):
            for d2 in range(4):
                xs = lax.rem(x + jnp.where(zero, d1, d2), 4)
                ys = lax.rem(y + jnp.where(zero, d2, d1), 4)
                for z in range(0, 8, 4):
                    rows = []
                    for pair in range(2):
                        base = xs * 32 + ys * 8
                        at = base + lax.rem(mine + z + 2 * pair, 8) * 128
                        one = t_ref[pl.ds(pl.multiple_of(at, 8), 8), :]
                        at = base + lax.rem(mine + z + 2 * pair + 1, 8) * 128
                        two = t_ref[pl.ds(pl.multiple_of(at, 8), 8), :]
                        c0 = jnp.where(low, one, pltpu.roll(two, 4, 0))
                        c1 = jnp.where(low, pltpu.roll(one, 4, 0), two)
                        rows.append(jnp.where(zero, c0, c1))
                    row = (d1 * 4 + d2) * 32 + z * 4
                    out_ref[half, row : row + 16, :] = jnp.concatenate(rows, 0).astype(BF16)


def early_kernel(tok_ref, cot_ref, wq_ref, wo_ref, q_ref, da_ref):
    q_ref[...] = dot(tok_ref[...], wq_ref[...]).astype(BF16)
    da_ref[...] = dot(cot_ref[...], wo_ref[...], NT).astype(BF16)


def whole(*shape):
    return pl.BlockSpec(shape, lambda i: (0,) * len(shape))


def early(tokens, cotangent, wq, wo):
    block = pl.BlockSpec((ROWS, QCOLS), lambda i: (0, i))
    return pl.pallas_call(
        early_kernel,
        grid=(STEPS,),
        out_shape=(jax.ShapeDtypeStruct((ROWS, MODEL), BF16),) * 2,
        in_specs=[
            whole(ROWS, MODEL),
            whole(ROWS, MODEL),
            pl.BlockSpec((MODEL, QCOLS), lambda i: (0, i)),
            pl.BlockSpec((QCOLS, MODEL), lambda i: (i, 0)),
        ],
        out_specs=(block, block),
        compiler_params=pltpu.CompilerParams(
            dimension_semantics=("arbitrary",), vmem_limit_bytes=12 << 20
        ),
        name="early",
    )(tokens, cotangent, wq, wo)


def prep_kernel(place, a_ref, b_ref, out_ref, t_ref):
    t_ref[:, :LANES] = a_ref[...].astype(F32).T
    t_ref[:, LANES:] = b_ref[...].astype(F32).T
    reorder(place, t_ref, out_ref)


def halo_kernel(place, far_ref, mate_ref, near_ref, out_ref, got_ref, t_ref):
    @pl.when(place[2] == 0)
    def _():
        got_ref[...] = far_ref[...]

    @pl.when(place[2] == 1)
    def _():
        got_ref[...] = mate_ref[...]

    prep_kernel(place, got_ref, near_ref, out_ref, t_ref)


def prepared(kernel, place, *blocks):
    order = jax.ShapeDtypeStruct((2, 512, 2 * LANES), BF16), whole(2, 512, 2 * LANES)
    outs = [order] if len(blocks) == 2 else [order, (jax.ShapeDtypeStruct((ROWS, MODEL), BF16), whole(ROWS, MODEL))]
    return pl.pallas_call(
        kernel,
        grid=(1,),
        out_shape=[o[0] for o in outs],
        in_specs=[pl.BlockSpec(memory_space=pltpu.SMEM)] + [whole(ROWS, MODEL)] * len(blocks),
        out_specs=[o[1] for o in outs],
        scratch_shapes=[pltpu.VMEM((MODEL, 2 * LANES), F32)],
        compiler_params=pltpu.CompilerParams(vmem_limit_bytes=12 << 20),
        name="prep",
    )(place, *blocks)


def swapped(a):
    return pltpu.roll(a, 64, 1)


def attention_kernel(
    place,
    far_ref,
    near_ref,
    own_ref,
    q_ref,
    da_ref,
    wk_ref,
    wv_ref,
    tp_ref,
    th_ref,
    att_ref,
    dq_ref,
    own_grad_ref,
    near_grad_ref,
    far_grad_ref,
    send_ref,
    keep_ref,
):
    window = jnp.concatenate([far_ref[...], near_ref[...], own_ref[...]], axis=0)
    keys = dot(window, wk_ref[...])
    values = dot(window, wv_ref[...])
    start = place[4]
    row = lax.rem(lax.broadcasted_iota(jnp.int32, (256, 384), 0), 128)
    col = lax.broadcasted_iota(jnp.int32, (256, 384), 1)
    allowed = (col <= row + 256) & (col >= start)
    low_k = lax.broadcasted_iota(jnp.int32, (384, LANES), 1) < 64
    low_q = lax.broadcasted_iota(jnp.int32, (ROWS, LANES), 1) < 64
    zero = jnp.zeros((ROWS, LANES), BF16)
    keys_swapped, values_swapped = swapped(keys), swapped(values)
    atts, dqs, dks, dvs = [], [], [], []
    for head in range(2):
        own_half = low_k if head == 0 else ~low_k
        key = jnp.where(own_half, keys, keys_swapped).astype(BF16)
        value = jnp.where(own_half, values, values_swapped).astype(BF16)
        cols = slice(head * LANES, (head + 1) * LANES)
        q = q_ref[:, cols]
        da = da_ref[:, cols]
        q2 = jnp.concatenate([jnp.where(low_q, q, zero), jnp.where(low_q, zero, q)], 0)
        da2 = jnp.concatenate([jnp.where(low_q, da, zero), jnp.where(low_q, zero, da)], 0)
        scores = jnp.where(allowed, dot(q2, key, NT) * SCALE, MASKED)
        highest = jnp.max(scores, axis=-1, keepdims=True)
        weights = jnp.exp(scores - highest)
        weights = weights * (1.0 / jnp.sum(weights, axis=-1, keepdims=True))
        probs = weights.astype(BF16)
        both = dot(probs, value)
        att = jnp.where(low_q, both[:ROWS], both[ROWS:]).astype(BF16)
        att_f = att.astype(F32)
        delta = jnp.sum(
            da2.astype(F32) * jnp.concatenate([att_f, att_f], 0), axis=-1, keepdims=True
        )
        dscores = (weights * (dot(da2, value, NT) - delta)).astype(BF16)
        both = dot(dscores, key) * SCALE
        dqs.append(jnp.where(low_q, both[:ROWS], both[ROWS:]).astype(BF16))
        dk = dot(dscores, q2, TN) * SCALE
        dv = dot(probs, da2, TN)
        dks.append(dk + swapped(dk))
        dvs.append(dv + swapped(dv))
        atts.append(att)
    att = jnp.concatenate(atts, 1)
    dq = jnp.concatenate(dqs, 1)
    dk = jnp.where(low_k, dks[0], dks[1])
    dv = jnp.where(low_k, dvs[0], dvs[1])
    att_ref[...] = att
    dq_ref[...] = dq
    own_grad_ref[0] = dk[256:]
    own_grad_ref[1] = dv[256:]
    dk, dv = dk.astype(BF16), dv.astype(BF16)
    far_grad_ref[0] = dk[:128]
    far_grad_ref[1] = dv[:128]
    near_grad_ref[0] = dk[128:256]
    near_grad_ref[1] = dv[128:256]
    rounded = jnp.concatenate([dk, dv], axis=1)
    for half, out in ((0, send_ref), (1, keep_ref)):
        tp = tp_ref[half]
        t_own, t_out = tp[:, :LANES], tp[:, LANES:]
        out[:, :256] = dot(t_out, att).astype(BF16)
        out[:, 256:512] = dot(t_own, dq).astype(BF16)
        out[:, 512:] = (dot(t_own, rounded[256:]) + dot(th_ref[half], rounded[:256])).astype(BF16)


def attention(first, steps, place, far, near, own, q, da, wk, wv, tp, th):
    def columns(rows, cols):
        return pl.BlockSpec((rows, cols), lambda i: (0, first + i))

    def fresh(rows, cols):
        return pl.BlockSpec((rows, cols), lambda i: (0, i))

    def struct(rows, cols, dtype):
        return jax.ShapeDtypeStruct((rows, cols * steps), dtype)

    return pl.pallas_call(
        attention_kernel,
        grid=(steps,),
        out_shape=(
            struct(ROWS, QCOLS, BF16),
            struct(ROWS, QCOLS, BF16),
            jax.ShapeDtypeStruct((2, ROWS, KCOLS * steps), F32),
            jax.ShapeDtypeStruct((2, ROWS, KCOLS * steps), BF16),
            jax.ShapeDtypeStruct((2, ROWS, KCOLS * steps), BF16),
            struct(512, GCOLS, BF16),
            struct(512, GCOLS, BF16),
        ),
        in_specs=[
            pl.BlockSpec(memory_space=pltpu.SMEM),
            whole(ROWS, MODEL),
            whole(ROWS, MODEL),
            whole(ROWS, MODEL),
            columns(ROWS, QCOLS),
            columns(ROWS, QCOLS),
            columns(MODEL, KCOLS),
            columns(MODEL, KCOLS),
            whole(2, 512, 2 * LANES),
            whole(2, 512, 2 * LANES),
        ],
        out_specs=(
            fresh(ROWS, QCOLS),
            fresh(ROWS, QCOLS),
            pl.BlockSpec((2, ROWS, KCOLS), lambda i: (0, 0, i)),
            pl.BlockSpec((2, ROWS, KCOLS), lambda i: (0, 0, i)),
            pl.BlockSpec((2, ROWS, KCOLS), lambda i: (0, 0, i)),
            fresh(512, GCOLS),
            fresh(512, GCOLS),
        ),
        compiler_params=pltpu.CompilerParams(
            dimension_semantics=("arbitrary",), vmem_limit_bytes=28 << 20
        ),
        cost_estimate=SMALL,
        name="attention",
    )(place, far, near, own, q, da, wk, wv, tp, th)


def cut(addends, rows):
    total = addends[0][rows, :].astype(F32)
    for other in addends[1:]:
        total = total + other[rows, :].astype(F32)
    return total


def fold_kernel(count, quarter, *refs):
    addends, outs = refs[:count], refs[count:]
    for d in range(4):
        outs[d][...] = cut(addends, slice(d * quarter, (d + 1) * quarter)).astype(outs[d].dtype)


def folded(*addends):
    rows, cols = addends[0].shape
    return pl.pallas_call(
        functools.partial(fold_kernel, len(addends), rows // 4),
        grid=(1,),
        out_shape=tuple(
            jax.ShapeDtypeStruct((rows // 4, cols), BF16 if d else F32) for d in range(4)
        ),
        in_specs=[whole(rows, cols)] * len(addends),
        out_specs=(whole(rows // 4, cols),) * 4,
        compiler_params=pltpu.CompilerParams(vmem_limit_bytes=20 << 20),
        name="fold",
    )(*addends)


def place_kernel(count, *refs):
    fold_kernel(2, 128, *refs[:2], *refs[2 + count :])


def folded_into(first, keep, got, wide=()):
    rows, cols = keep.shape
    given = pl.BlockSpec((rows, GCOLS), lambda i: (0, i))
    return pl.pallas_call(
        functools.partial(place_kernel, len(wide)),
        grid=(cols // GCOLS,),
        out_shape=tuple(
            jax.ShapeDtypeStruct((rows // 4, STEPS * GCOLS), BF16 if d else F32) for d in range(4)
        ),
        in_specs=[given, given] + [pl.BlockSpec(memory_space=pl.ANY)] * len(wide),
        out_specs=(pl.BlockSpec((rows // 4, GCOLS), lambda i: (0, first + i)),) * 4,
        input_output_aliases={2 + d: d for d in range(len(wide))},
        compiler_params=pltpu.CompilerParams(vmem_limit_bytes=12 << 20),
        name="place",
    )(keep, got, *wide)


def halve_kernel(own_ref, a_ref, b_ref, c_ref, keep_ref, send_ref):
    total = cut((own_ref, a_ref, b_ref, c_ref), slice(0, 8))
    keep_ref[...] = total[:4]
    send_ref[...] = total[4:].astype(BF16)


def halved(*addends):
    cols = addends[0].shape[1]
    return pl.pallas_call(
        halve_kernel,
        grid=(1,),
        out_shape=(
            jax.ShapeDtypeStruct((4, cols), F32),
            jax.ShapeDtypeStruct((4, cols), BF16),
        ),
        in_specs=[whole(8, cols)] * 4,
        out_specs=(whole(4, cols),) * 2,
        compiler_params=pltpu.CompilerParams(vmem_limit_bytes=4 << 20),
        name="halve",
    )(*addends)


def last_kernel(own_ref, got_ref, q_ref, k_ref, v_ref, o_ref):
    total = own_ref[...] + got_ref[...].astype(F32)
    for step in range(STEPS):
        base = step * GCOLS
        at = slice(step * 256, step * 256 + 256)
        o_ref[:, at] = total[:, base : base + 256]
        q_ref[:, at] = total[:, base + 256 : base + 512]
        at = slice(step * 128, step * 128 + 128)
        k_ref[:, at] = total[:, base + 512 : base + 640]
        v_ref[:, at] = total[:, base + 640 : base + 768]


def summed_last(own, got):
    shapes = [(4, 1024), (4, 512), (4, 512), (4, 1024)]
    return pl.pallas_call(
        last_kernel,
        grid=(1,),
        out_shape=tuple(jax.ShapeDtypeStruct(shape, F32) for shape in shapes),
        in_specs=[whole(*own.shape)] * 2,
        out_specs=tuple(whole(*shape) for shape in shapes),
        compiler_params=pltpu.CompilerParams(vmem_limit_bytes=4 << 20),
        name="last",
    )(own, got)


def middle_kernel(att_one, att_two, dq_one, dq_two, wo_ref, wq_ref, out_ref, base_ref):
    att = jnp.concatenate([att_one[...], att_two[...]], axis=1)
    out_ref[...] = dot(att, wo_ref[...]).astype(BF16)
    dq = jnp.concatenate([dq_one[...], dq_two[...]], axis=1)
    base_ref[...] = dot(dq, wq_ref[...], NT)


def middle(atts, dqs, wo, wq):
    block = pl.BlockSpec((ROWS, QCOLS), lambda i: (0, i))
    return pl.pallas_call(
        middle_kernel,
        grid=(STEPS,),
        out_shape=(
            jax.ShapeDtypeStruct((ROWS, MODEL), BF16),
            jax.ShapeDtypeStruct((ROWS, MODEL), F32),
        ),
        in_specs=[whole(*a.shape) for a in (*atts, *dqs)]
        + [
            pl.BlockSpec((MODEL, QCOLS), lambda i: (0, i)),
            pl.BlockSpec((QCOLS, MODEL), lambda i: (i, 0)),
        ],
        out_specs=(block, block),
        compiler_params=pltpu.CompilerParams(vmem_limit_bytes=12 << 20),
        name="middle",
    )(*atts, *dqs, wo, wq)


def tail_kernel(base_ref, own_one, own_two, handed, near, far, wk_ref, wv_ref, out_ref):
    total = base_ref[...]
    for i, w_ref in enumerate((wk_ref, wv_ref)):
        grad = jnp.concatenate([own_one[i], own_two[i]], axis=1)
        for part in (handed[0, i], near[i], far[i]):
            grad = grad + part.astype(F32)
        total = total + dot(grad.astype(BF16), w_ref[...], NT)
    out_ref[...] = total.astype(BF16)


def tail(*args):
    return pl.pallas_call(
        tail_kernel,
        grid=(1,),
        out_shape=jax.ShapeDtypeStruct((ROWS, MODEL), BF16),
        in_specs=[whole(*a.shape) for a in args],
        out_specs=whole(ROWS, MODEL),
        compiler_params=pltpu.CompilerParams(vmem_limit_bytes=20 << 20),
        name="tail",
    )(*args)


def after(value, *others):
    return lax.optimization_barrier((value, *others))[0]


def shards(tokens, query_weight, key_weight, value_matrix, out_weight, out_cotangent):
    near = passed_along(tokens, 1)
    far = passed_along(tokens, 2, range(0, 256, 2))
    mate = passed_along(near, 1, range(0, 256, 2))
    me = lax.axis_index(AXIS)
    start = jnp.maximum(2 - me, 0) * ROWS
    place = jnp.stack([(me // 8) % 4, (me // 2) % 4, me % 2, me // 32, start]).astype(jnp.int32)
    wq, wk, wv, wo = map(in_hbm, (query_weight, key_weight, value_matrix, out_weight))
    q, da = early(in_hbm(tokens), in_hbm(out_cotangent), wq, wo)
    (tp,) = prepared(prep_kernel, after(place, q, near), tokens, out_cotangent)
    th, far = prepared(halo_kernel, after(place, tp), far, mate, near)

    def attend(first, steps, place):
        return attention(first, steps, place, far, near, tokens, q, da, wk, wv, tp, th)

    one = attend(0, 3, place)
    got_one = to_mate(one[-2])
    two = attend(3, 1, after(place, one[-1]))
    got_two = to_mate(two[-2])
    sums = folded_into(0, one[-1], after(got_one, two[-1]))
    own, *sends = folded_into(3, two[-1], after(got_two, sums[0]), sums)
    ring_one = ring([None, *sends], 0)

    near_grad = jnp.concatenate([one[3], after(two[3], own)], axis=-1)
    far_grad = jnp.concatenate([one[4], after(two[4], own)], axis=-1)
    handed = passed_along(jnp.stack([near_grad, far_grad]), -1, range(1, 256, 2))
    attn_out, base = middle((one[0], after(two[0], own)), (one[1], two[1]), wo, wq)
    summed = (near_grad.astype(F32) + handed[1].astype(F32)).astype(BF16)
    base, summed = lax.optimization_barrier((base, summed))

    own, *sends = folded(after(own, base), *ring_one)
    ring_two = ring([None, *sends], 1)
    own, *sends = folded(own, *ring_two)
    z_own = own
    ring_three = [along_z(sends[d - 1], 2 * d) for d in (1, 3, 2)]
    own, send = halved(own, *ring_three)
    got = along_z(send, 1)
    back_near = passed_along(after(summed, z_own), -1, range(0, 256, 2))
    back_far = passed_along(after(far_grad, z_own), -2, range(0, 256, 2))
    tokens_grad = tail(base, one[2], two[2], handed, back_near, back_far, key_weight, value_matrix)
    query_rows, key_rows, value_rows, out_rows = summed_last(after(own, tokens_grad), got)
    return attn_out, tokens_grad, query_rows, key_rows, value_rows, out_rows.T


def solution(mesh):
    rows = P(AXIS, None)
    return jax.shard_map(
        shards,
        mesh=mesh,
        in_specs=(rows, P(), P(), P(), P(), rows),
        out_specs=(rows, rows, rows, rows, rows, P(None, AXIS)),
        check_vma=False,
    )
```

```python
import functools

import jax
import jax.numpy as jnp
from jax import lax
from jax.experimental import pallas as pl
from jax.experimental.pallas import tpu as pltpu
from jax.sharding import PartitionSpec as P

AXIS = "seq"
ROWS = 128
MODEL = 1024
LANES = 128
STEPS = 4
QCOLS = 256
KCOLS = 128
GCOLS = 768
SCALE = 0.125
MASKED = -1e30
BF16 = jnp.bfloat16
SMALL = pl.CostEstimate(flops=1000, transcendentals=0, bytes_accessed=1000)
F32 = jnp.float32
NT = (((1,), (1,)), ((), ()))
TN = (((0,), (0,)), ((), ()))


def dot(a, b, dims=(((1,), (0,)), ((), ()))):
    return lax.dot_general(a, b, dims, preferred_element_type=F32)


def flat(z, x, y, c):
    return ((z * 4 + x) * 4 + y) * 2 + c


def in_hbm(array):
    return pltpu.with_memory_space_constraint(array, pltpu.HBM)


def route_of(step):
    places = [(z, x, y, c) for z in range(8) for x in range(4) for y in range(4) for c in range(2)]
    return [(flat(*p), flat(*step(*p))) for p in places]


def to_mate(array):
    return lax.ppermute(array, AXIS, route_of(lambda z, x, y, c: (z, x, y, 1 - c)))


def plane_step(phase, d, z, x, y, c):
    if c == phase:
        return z, (x + d) % 4, y, c
    return z, x, (y + d) % 4, c


def ring(blocks, phase):
    return [
        lax.ppermute(blocks[d], AXIS, route_of(functools.partial(plane_step, phase, d)))
        for d in (1, 3, 2)
    ]


def along_z(block, distance):
    return lax.ppermute(
        block, AXIS, route_of(lambda z, x, y, c: ((z + distance) % 8, x, y, c))
    )


def passed_along(block, distance, sources=range(256)):
    return lax.ppermute(
        block, AXIS, [(i, i + distance) for i in sources if i + distance in range(256)]
    )


def reorder(place, t_ref, out_ref):
    x, y, core, mine = place[0], place[1], place[2], place[3]
    low = lax.broadcasted_iota(jnp.int32, (8, 2 * LANES), 0) < 4
    for half in range(2):
        target = 1 - core if half == 0 else core
        zero = target == 0
        for d1 in range(4):
            for d2 in range(4):
                xs = lax.rem(x + jnp.where(zero, d1, d2), 4)
                ys = lax.rem(y + jnp.where(zero, d2, d1), 4)
                for z in range(0, 8, 4):
                    rows = []
                    for pair in range(2):
                        base = xs * 32 + ys * 8
                        at = base + lax.rem(mine + z + 2 * pair, 8) * 128
                        one = t_ref[pl.ds(pl.multiple_of(at, 8), 8), :]
                        at = base + lax.rem(mine + z + 2 * pair + 1, 8) * 128
                        two = t_ref[pl.ds(pl.multiple_of(at, 8), 8), :]
                        c0 = jnp.where(low, one, pltpu.roll(two, 4, 0))
                        c1 = jnp.where(low, pltpu.roll(one, 4, 0), two)
                        rows.append(jnp.where(zero, c0, c1))
                    row = (d1 * 4 + d2) * 32 + z * 4
                    out_ref[half, row : row + 16, :] = jnp.concatenate(rows, 0).astype(BF16)


def early_kernel(tok_ref, cot_ref, wq_ref, wo_ref, q_ref, da_ref):
    q_ref[...] = dot(tok_ref[...], wq_ref[...]).astype(BF16)
    da_ref[...] = dot(cot_ref[...], wo_ref[...], NT).astype(BF16)


def whole(*shape):
    return pl.BlockSpec(shape, lambda i: (0,) * len(shape))


def early(tokens, cotangent, wq, wo):
    block = pl.BlockSpec((ROWS, QCOLS), lambda i: (0, i))
    return pl.pallas_call(
        early_kernel,
        grid=(STEPS,),
        out_shape=(jax.ShapeDtypeStruct((ROWS, MODEL), BF16),) * 2,
        in_specs=[
            whole(ROWS, MODEL),
            whole(ROWS, MODEL),
            pl.BlockSpec((MODEL, QCOLS), lambda i: (0, i)),
            pl.BlockSpec((QCOLS, MODEL), lambda i: (i, 0)),
        ],
        out_specs=(block, block),
        compiler_params=pltpu.CompilerParams(
            dimension_semantics=("arbitrary",), vmem_limit_bytes=12 << 20
        ),
        name="early",
    )(tokens, cotangent, wq, wo)


def prep_kernel(place, a_ref, b_ref, out_ref, t_ref):
    t_ref[:, :LANES] = a_ref[...].astype(F32).T
    t_ref[:, LANES:] = b_ref[...].astype(F32).T
    reorder(place, t_ref, out_ref)


def halo_kernel(place, far_ref, mate_ref, near_ref, out_ref, got_ref, t_ref):
    @pl.when(place[2] == 0)
    def _():
        got_ref[...] = far_ref[...]

    @pl.when(place[2] == 1)
    def _():
        got_ref[...] = mate_ref[...]

    prep_kernel(place, got_ref, near_ref, out_ref, t_ref)


def prepared(kernel, place, *blocks):
    order = jax.ShapeDtypeStruct((2, 512, 2 * LANES), BF16), whole(2, 512, 2 * LANES)
    outs = [order] if len(blocks) == 2 else [order, (jax.ShapeDtypeStruct((ROWS, MODEL), BF16), whole(ROWS, MODEL))]
    return pl.pallas_call(
        kernel,
        grid=(1,),
        out_shape=[o[0] for o in outs],
        in_specs=[pl.BlockSpec(memory_space=pltpu.SMEM)] + [whole(ROWS, MODEL)] * len(blocks),
        out_specs=[o[1] for o in outs],
        scratch_shapes=[pltpu.VMEM((MODEL, 2 * LANES), F32)],
        compiler_params=pltpu.CompilerParams(vmem_limit_bytes=12 << 20),
        name="prep",
    )(place, *blocks)


def swapped(a):
    return pltpu.roll(a, 64, 1)


def attention_kernel(
    place,
    far_ref,
    near_ref,
    own_ref,
    q_ref,
    da_ref,
    wk_ref,
    wv_ref,
    tp_ref,
    th_ref,
    att_ref,
    dq_ref,
    own_grad_ref,
    near_grad_ref,
    far_grad_ref,
    send_ref,
    keep_ref,
):
    window = jnp.concatenate([far_ref[...], near_ref[...], own_ref[...]], axis=0)
    keys = dot(window, wk_ref[...])
    values = dot(window, wv_ref[...])
    start = place[4]
    row = lax.rem(lax.broadcasted_iota(jnp.int32, (256, 384), 0), 128)
    col = lax.broadcasted_iota(jnp.int32, (256, 384), 1)
    allowed = (col <= row + 256) & (col >= start)
    low_k = lax.broadcasted_iota(jnp.int32, (384, LANES), 1) < 64
    low_q = lax.broadcasted_iota(jnp.int32, (ROWS, LANES), 1) < 64
    zero = jnp.zeros((ROWS, LANES), BF16)
    keys_swapped, values_swapped = swapped(keys), swapped(values)
    atts, dqs, dks, dvs = [], [], [], []
    for head in range(2):
        own_half = low_k if head == 0 else ~low_k
        key = jnp.where(own_half, keys, keys_swapped).astype(BF16)
        value = jnp.where(own_half, values, values_swapped).astype(BF16)
        cols = slice(head * LANES, (head + 1) * LANES)
        q = q_ref[:, cols]
        da = da_ref[:, cols]
        q2 = jnp.concatenate([jnp.where(low_q, q, zero), jnp.where(low_q, zero, q)], 0)
        da2 = jnp.concatenate([jnp.where(low_q, da, zero), jnp.where(low_q, zero, da)], 0)
        scores = jnp.where(allowed, dot(q2, key, NT) * SCALE, MASKED)
        highest = jnp.max(scores, axis=-1, keepdims=True)
        weights = jnp.exp(scores - highest)
        weights = weights * (1.0 / jnp.sum(weights, axis=-1, keepdims=True))
        probs = weights.astype(BF16)
        both = dot(probs, value)
        att = jnp.where(low_q, both[:ROWS], both[ROWS:]).astype(BF16)
        att_f = att.astype(F32)
        delta = jnp.sum(
            da2.astype(F32) * jnp.concatenate([att_f, att_f], 0), axis=-1, keepdims=True
        )
        dscores = (weights * (dot(da2, value, NT) - delta)).astype(BF16)
        both = dot(dscores, key) * SCALE
        dqs.append(jnp.where(low_q, both[:ROWS], both[ROWS:]).astype(BF16))
        dk = dot(dscores, q2, TN) * SCALE
        dv = dot(probs, da2, TN)
        dks.append(dk + swapped(dk))
        dvs.append(dv + swapped(dv))
        atts.append(att)
    att = jnp.concatenate(atts, 1)
    dq = jnp.concatenate(dqs, 1)
    dk = jnp.where(low_k, dks[0], dks[1])
    dv = jnp.where(low_k, dvs[0], dvs[1])
    att_ref[...] = att
    dq_ref[...] = dq
    own_grad_ref[0] = dk[256:]
    own_grad_ref[1] = dv[256:]
    dk, dv = dk.astype(BF16), dv.astype(BF16)
    far_grad_ref[0] = dk[:128]
    far_grad_ref[1] = dv[:128]
    near_grad_ref[0] = dk[128:256]
    near_grad_ref[1] = dv[128:256]
    rounded = jnp.concatenate([dk, dv], axis=1)
    for half, out in ((0, send_ref), (1, keep_ref)):
        tp = tp_ref[half]
        t_own, t_out = tp[:, :LANES], tp[:, LANES:]
        out[:, :256] = dot(t_out, att).astype(BF16)
        out[:, 256:512] = dot(t_own, dq).astype(BF16)
        out[:, 512:] = (dot(t_own, rounded[256:]) + dot(th_ref[half], rounded[:256])).astype(BF16)


def attention(first, steps, place, far, near, own, q, da, wk, wv, tp, th):
    def columns(rows, cols):
        return pl.BlockSpec((rows, cols), lambda i: (0, first + i))

    def fresh(rows, cols):
        return pl.BlockSpec((rows, cols), lambda i: (0, i))

    def struct(rows, cols, dtype):
        return jax.ShapeDtypeStruct((rows, cols * steps), dtype)

    return pl.pallas_call(
        attention_kernel,
        grid=(steps,),
        out_shape=(
            struct(ROWS, QCOLS, BF16),
            struct(ROWS, QCOLS, BF16),
            jax.ShapeDtypeStruct((2, ROWS, KCOLS * steps), F32),
            jax.ShapeDtypeStruct((2, ROWS, KCOLS * steps), BF16),
            jax.ShapeDtypeStruct((2, ROWS, KCOLS * steps), BF16),
            struct(512, GCOLS, BF16),
            struct(512, GCOLS, BF16),
        ),
        in_specs=[
            pl.BlockSpec(memory_space=pltpu.SMEM),
            whole(ROWS, MODEL),
            whole(ROWS, MODEL),
            whole(ROWS, MODEL),
            columns(ROWS, QCOLS),
            columns(ROWS, QCOLS),
            columns(MODEL, KCOLS),
            columns(MODEL, KCOLS),
            whole(2, 512, 2 * LANES),
            whole(2, 512, 2 * LANES),
        ],
        out_specs=(
            fresh(ROWS, QCOLS),
            fresh(ROWS, QCOLS),
            pl.BlockSpec((2, ROWS, KCOLS), lambda i: (0, 0, i)),
            pl.BlockSpec((2, ROWS, KCOLS), lambda i: (0, 0, i)),
            pl.BlockSpec((2, ROWS, KCOLS), lambda i: (0, 0, i)),
            fresh(512, GCOLS),
            fresh(512, GCOLS),
        ),
        compiler_params=pltpu.CompilerParams(
            dimension_semantics=("arbitrary",), vmem_limit_bytes=28 << 20
        ),
        cost_estimate=SMALL,
        name="attention",
    )(place, far, near, own, q, da, wk, wv, tp, th)


def cut(addends, rows):
    total = addends[0][rows, :].astype(F32)
    for other in addends[1:]:
        total = total + other[rows, :].astype(F32)
    return total


def fold_kernel(count, quarter, *refs):
    addends, outs = refs[:count], refs[count:]
    for d in range(4):
        outs[d][...] = cut(addends, slice(d * quarter, (d + 1) * quarter)).astype(outs[d].dtype)


def folded(*addends):
    rows, cols = addends[0].shape
    return pl.pallas_call(
        functools.partial(fold_kernel, len(addends), rows // 4),
        grid=(1,),
        out_shape=tuple(
            jax.ShapeDtypeStruct((rows // 4, cols), BF16 if d else F32) for d in range(4)
        ),
        in_specs=[whole(rows, cols)] * len(addends),
        out_specs=(whole(rows // 4, cols),) * 4,
        compiler_params=pltpu.CompilerParams(vmem_limit_bytes=20 << 20),
        name="fold",
    )(*addends)


def place_kernel(count, *refs):
    fold_kernel(2, 128, *refs[:2], *refs[2 + count :])


def folded_into(first, keep, got, wide=()):
    rows, cols = keep.shape
    given = pl.BlockSpec((rows, GCOLS), lambda i: (0, i))
    return pl.pallas_call(
        functools.partial(place_kernel, len(wide)),
        grid=(cols // GCOLS,),
        out_shape=tuple(
            jax.ShapeDtypeStruct((rows // 4, STEPS * GCOLS), BF16 if d else F32) for d in range(4)
        ),
        in_specs=[given, given] + [pl.BlockSpec(memory_space=pl.ANY)] * len(wide),
        out_specs=(pl.BlockSpec((rows // 4, GCOLS), lambda i: (0, first + i)),) * 4,
        input_output_aliases={2 + d: d for d in range(len(wide))},
        compiler_params=pltpu.CompilerParams(vmem_limit_bytes=12 << 20),
        name="place",
    )(keep, got, *wide)


def halve_kernel(own_ref, a_ref, b_ref, c_ref, keep_ref, send_ref):
    total = cut((own_ref, a_ref, b_ref, c_ref), slice(0, 8))
    keep_ref[...] = total[:4]
    send_ref[...] = total[4:].astype(BF16)


def halved(*addends):
    cols = addends[0].shape[1]
    return pl.pallas_call(
        halve_kernel,
        grid=(1,),
        out_shape=(
            jax.ShapeDtypeStruct((4, cols), F32),
            jax.ShapeDtypeStruct((4, cols), BF16),
        ),
        in_specs=[whole(8, cols)] * 4,
        out_specs=(whole(4, cols),) * 2,
        compiler_params=pltpu.CompilerParams(vmem_limit_bytes=4 << 20),
        name="halve",
    )(*addends)


def last_kernel(own_ref, got_ref, q_ref, k_ref, v_ref, o_ref):
    total = own_ref[...] + got_ref[...].astype(F32)
    for step in range(STEPS):
        base = step * GCOLS
        at = slice(step * 256, step * 256 + 256)
        o_ref[:, at] = total[:, base : base + 256]
        q_ref[:, at] = total[:, base + 256 : base + 512]
        at = slice(step * 128, step * 128 + 128)
        k_ref[:, at] = total[:, base + 512 : base + 640]
        v_ref[:, at] = total[:, base + 640 : base + 768]


def summed_last(own, got):
    shapes = [(4, 1024), (4, 512), (4, 512), (4, 1024)]
    return pl.pallas_call(
        last_kernel,
        grid=(1,),
        out_shape=tuple(jax.ShapeDtypeStruct(shape, F32) for shape in shapes),
        in_specs=[whole(*own.shape)] * 2,
        out_specs=tuple(whole(*shape) for shape in shapes),
        compiler_params=pltpu.CompilerParams(vmem_limit_bytes=4 << 20),
        name="last",
    )(own, got)


def middle_kernel(att_one, att_two, dq_one, dq_two, wo_ref, wq_ref, out_ref, base_ref):
    att = jnp.concatenate([att_one[...], att_two[...]], axis=1)
    out_ref[...] = dot(att, wo_ref[...]).astype(BF16)
    dq = jnp.concatenate([dq_one[...], dq_two[...]], axis=1)
    base_ref[...] = dot(dq, wq_ref[...], NT)


def middle(atts, dqs, wo, wq):
    block = pl.BlockSpec((ROWS, QCOLS), lambda i: (0, i))
    return pl.pallas_call(
        middle_kernel,
        grid=(STEPS,),
        out_shape=(
            jax.ShapeDtypeStruct((ROWS, MODEL), BF16),
            jax.ShapeDtypeStruct((ROWS, MODEL), F32),
        ),
        in_specs=[whole(*a.shape) for a in (*atts, *dqs)]
        + [
            pl.BlockSpec((MODEL, QCOLS), lambda i: (0, i)),
            pl.BlockSpec((QCOLS, MODEL), lambda i: (i, 0)),
        ],
        out_specs=(block, block),
        compiler_params=pltpu.CompilerParams(vmem_limit_bytes=12 << 20),
        name="middle",
    )(*atts, *dqs, wo, wq)


def tail_kernel(base_ref, own_one, own_two, handed, near, far, wk_ref, wv_ref, out_ref):
    total = base_ref[...]
    for i, w_ref in enumerate((wk_ref, wv_ref)):
        grad = jnp.concatenate([own_one[i], own_two[i]], axis=1)
        for part in (handed[0, i], near[i], far[i]):
            grad = grad + part.astype(F32)
        total = total + dot(grad.astype(BF16), w_ref[...], NT)
    out_ref[...] = total.astype(BF16)


def tail(*args):
    return pl.pallas_call(
        tail_kernel,
        grid=(1,),
        out_shape=jax.ShapeDtypeStruct((ROWS, MODEL), BF16),
        in_specs=[whole(*a.shape) for a in args],
        out_specs=whole(ROWS, MODEL),
        compiler_params=pltpu.CompilerParams(vmem_limit_bytes=20 << 20),
        name="tail",
    )(*args)


def after(value, *others):
    return lax.optimization_barrier((value, *others))[0]


def shards(tokens, query_weight, key_weight, value_matrix, out_weight, out_cotangent):
    near = passed_along(tokens, 1)
    far = passed_along(tokens, 2, range(0, 256, 2))
    me = lax.axis_index(AXIS)
    start = jnp.maximum(2 - me, 0) * ROWS
    place = jnp.stack([(me // 8) % 4, (me // 2) % 4, me % 2, me // 32, start]).astype(jnp.int32)
    wq, wk, wv, wo = map(in_hbm, (query_weight, key_weight, value_matrix, out_weight))
    q, da = early(in_hbm(tokens), in_hbm(out_cotangent), wq, wo)
    near = after(near, q)
    mate = passed_along(near, 1, range(0, 256, 2))
    (tp,) = prepared(prep_kernel, after(place, near), tokens, out_cotangent)
    th, far = prepared(halo_kernel, after(place, tp), far, mate, near)

    def attend(first, steps, place):
        return attention(first, steps, place, far, near, tokens, q, da, wk, wv, tp, th)

    one = attend(0, 3, place)
    got_one = to_mate(one[-2])
    two = attend(3, 1, after(place, one[-1]))
    got_two = to_mate(two[-2])
    sums = folded_into(0, one[-1], after(got_one, two[-1]))
    own, *sends = folded_into(3, two[-1], after(got_two, sums[0]), sums)
    ring_one = ring([None, *sends], 0)

    attn_out, base = middle((one[0], after(two[0], own)), (one[1], two[1]), wo, wq)
    grads = lax.optimization_barrier((one[3], two[3], one[4], two[4], base))
    near_grad = jnp.concatenate(grads[0:2], axis=-1)
    far_grad = jnp.concatenate(grads[2:4], axis=-1)
    handed = passed_along(jnp.stack([near_grad, far_grad]), -1, range(1, 256, 2))
    summed = (near_grad.astype(F32) + handed[1].astype(F32)).astype(BF16)

    back_near = passed_along(after(summed, ring_one[0]), -1, range(0, 256, 2))
    back_far = passed_along(after(far_grad, ring_one[0]), -2, range(0, 256, 2))

    own, *sends = folded(after(own, base, back_near, back_far), *ring_one)
    ring_two = ring([None, *sends], 1)
    tokens_grad = tail(
        after(base, own), one[2], two[2], handed, back_near, back_far, key_weight, value_matrix
    )
    own, *sends = folded(after(own, tokens_grad), *ring_two)
    ring_three = [along_z(sends[d - 1], 2 * d) for d in (1, 3, 2)]
    own, send = halved(own, *ring_three)
    got = along_z(send, 1)
    query_rows, key_rows, value_rows, out_rows = summed_last(own, got)
    return attn_out, tokens_grad, query_rows, key_rows, value_rows, out_rows.T


def solution(mesh):
    rows = P(AXIS, None)
    return jax.shard_map(
        shards,
        mesh=mesh,
        in_specs=(rows, P(), P(), P(), P(), rows),
        out_specs=(rows, rows, rows, rows, rows, P(None, AXIS)),
        check_vma=False,
    )
```

```python
import functools

import jax
import jax.numpy as jnp
from jax import lax
from jax.experimental import pallas as pl
from jax.experimental.pallas import tpu as pltpu
from jax.sharding import PartitionSpec as P

AXIS = "seq"
ROWS = 128
MODEL = 1024
LANES = 128
STEPS = 4
QCOLS = 256
KCOLS = 128
GCOLS = 768
SCALE = 0.125
MASKED = -1e30
BF16 = jnp.bfloat16
SMALL = pl.CostEstimate(flops=1000, transcendentals=0, bytes_accessed=1000)
F32 = jnp.float32
NT = (((1,), (1,)), ((), ()))
TN = (((0,), (0,)), ((), ()))


def dot(a, b, dims=(((1,), (0,)), ((), ()))):
    return lax.dot_general(a, b, dims, preferred_element_type=F32)


def flat(z, x, y, c):
    return ((z * 4 + x) * 4 + y) * 2 + c


def in_hbm(array):
    return pltpu.with_memory_space_constraint(array, pltpu.HBM)


def route_of(step):
    places = [(z, x, y, c) for z in range(8) for x in range(4) for y in range(4) for c in range(2)]
    return [(flat(*p), flat(*step(*p))) for p in places]


def to_mate(array):
    return lax.ppermute(array, AXIS, route_of(lambda z, x, y, c: (z, x, y, 1 - c)))


def plane_step(phase, d, z, x, y, c):
    if c == phase:
        return z, (x + d) % 4, y, c
    return z, x, (y + d) % 4, c


def ring(blocks, phase):
    return [
        lax.ppermute(blocks[d], AXIS, route_of(functools.partial(plane_step, phase, d)))
        for d in (1, 3, 2)
    ]


def along_z(block, distance):
    return lax.ppermute(
        block, AXIS, route_of(lambda z, x, y, c: ((z + distance) % 8, x, y, c))
    )


def passed_along(block, distance, sources=range(256)):
    return lax.ppermute(
        block, AXIS, [(i, i + distance) for i in sources if i + distance in range(256)]
    )


def reorder(place, t_ref, out_ref):
    x, y, core, mine = place[0], place[1], place[2], place[3]
    low = lax.broadcasted_iota(jnp.int32, (8, 2 * LANES), 0) < 4
    for half in range(2):
        target = 1 - core if half == 0 else core
        zero = target == 0
        for d1 in range(4):
            for d2 in range(4):
                xs = lax.rem(x + jnp.where(zero, d1, d2), 4)
                ys = lax.rem(y + jnp.where(zero, d2, d1), 4)
                for z in range(0, 8, 4):
                    rows = []
                    for pair in range(2):
                        base = xs * 32 + ys * 8
                        at = base + lax.rem(mine + z + 2 * pair, 8) * 128
                        one = t_ref[pl.ds(pl.multiple_of(at, 8), 8), :]
                        at = base + lax.rem(mine + z + 2 * pair + 1, 8) * 128
                        two = t_ref[pl.ds(pl.multiple_of(at, 8), 8), :]
                        c0 = jnp.where(low, one, pltpu.roll(two, 4, 0))
                        c1 = jnp.where(low, pltpu.roll(one, 4, 0), two)
                        rows.append(jnp.where(zero, c0, c1))
                    row = (d1 * 4 + d2) * 32 + z * 4
                    out_ref[half, row : row + 16, :] = jnp.concatenate(rows, 0).astype(BF16)


def early_kernel(tok_ref, cot_ref, wq_ref, wo_ref, q_ref, da_ref):
    q_ref[...] = dot(tok_ref[...], wq_ref[...]).astype(BF16)
    da_ref[...] = dot(cot_ref[...], wo_ref[...], NT).astype(BF16)


def whole(*shape):
    return pl.BlockSpec(shape, lambda i: (0,) * len(shape))


def early(tokens, cotangent, wq, wo):
    block = pl.BlockSpec((ROWS, QCOLS), lambda i: (0, i))
    return pl.pallas_call(
        early_kernel,
        grid=(STEPS,),
        out_shape=(jax.ShapeDtypeStruct((ROWS, MODEL), BF16),) * 2,
        in_specs=[
            whole(ROWS, MODEL),
            whole(ROWS, MODEL),
            pl.BlockSpec((MODEL, QCOLS), lambda i: (0, i)),
            pl.BlockSpec((QCOLS, MODEL), lambda i: (i, 0)),
        ],
        out_specs=(block, block),
        compiler_params=pltpu.CompilerParams(
            dimension_semantics=("arbitrary",), vmem_limit_bytes=12 << 20
        ),
        name="early",
    )(tokens, cotangent, wq, wo)


def prep_kernel(place, a_ref, b_ref, out_ref, t_ref):
    t_ref[:, :LANES] = a_ref[...].astype(F32).T
    t_ref[:, LANES:] = b_ref[...].astype(F32).T
    reorder(place, t_ref, out_ref)


def halo_kernel(place, far_ref, mate_ref, near_ref, out_ref, got_ref, t_ref):
    @pl.when(place[2] == 0)
    def _():
        got_ref[...] = far_ref[...]

    @pl.when(place[2] == 1)
    def _():
        got_ref[...] = mate_ref[...]

    prep_kernel(place, got_ref, near_ref, out_ref, t_ref)


def prepared(kernel, place, *blocks):
    order = jax.ShapeDtypeStruct((2, 512, 2 * LANES), BF16), whole(2, 512, 2 * LANES)
    outs = [order] if len(blocks) == 2 else [order, (jax.ShapeDtypeStruct((ROWS, MODEL), BF16), whole(ROWS, MODEL))]
    return pl.pallas_call(
        kernel,
        grid=(1,),
        out_shape=[o[0] for o in outs],
        in_specs=[pl.BlockSpec(memory_space=pltpu.SMEM)] + [whole(ROWS, MODEL)] * len(blocks),
        out_specs=[o[1] for o in outs],
        scratch_shapes=[pltpu.VMEM((MODEL, 2 * LANES), F32)],
        compiler_params=pltpu.CompilerParams(vmem_limit_bytes=12 << 20),
        name="prep",
    )(place, *blocks)


def swapped(a):
    return pltpu.roll(a, 64, 1)


def attention_kernel(
    place,
    far_ref,
    near_ref,
    own_ref,
    q_ref,
    da_ref,
    wk_ref,
    wv_ref,
    tp_ref,
    th_ref,
    att_ref,
    dq_ref,
    own_grad_ref,
    near_grad_ref,
    far_grad_ref,
    send_ref,
    keep_ref,
):
    window = jnp.concatenate([far_ref[...], near_ref[...], own_ref[...]], axis=0)
    keys = dot(window, wk_ref[...])
    values = dot(window, wv_ref[...])
    start = place[4]
    row = lax.rem(lax.broadcasted_iota(jnp.int32, (256, 384), 0), 128)
    col = lax.broadcasted_iota(jnp.int32, (256, 384), 1)
    allowed = (col <= row + 256) & (col >= start)
    low_k = lax.broadcasted_iota(jnp.int32, (384, LANES), 1) < 64
    low_q = lax.broadcasted_iota(jnp.int32, (ROWS, LANES), 1) < 64
    zero = jnp.zeros((ROWS, LANES), BF16)
    keys_swapped, values_swapped = swapped(keys), swapped(values)
    atts, dqs, dks, dvs = [], [], [], []
    for head in range(2):
        own_half = low_k if head == 0 else ~low_k
        key = jnp.where(own_half, keys, keys_swapped).astype(BF16)
        value = jnp.where(own_half, values, values_swapped).astype(BF16)
        cols = slice(head * LANES, (head + 1) * LANES)
        q = q_ref[:, cols]
        da = da_ref[:, cols]
        q2 = jnp.concatenate([jnp.where(low_q, q, zero), jnp.where(low_q, zero, q)], 0)
        da2 = jnp.concatenate([jnp.where(low_q, da, zero), jnp.where(low_q, zero, da)], 0)
        scores = jnp.where(allowed, dot(q2, key, NT) * SCALE, MASKED)
        highest = jnp.max(scores, axis=-1, keepdims=True)
        weights = jnp.exp(scores - highest)
        weights = weights * (1.0 / jnp.sum(weights, axis=-1, keepdims=True))
        probs = weights.astype(BF16)
        both = dot(probs, value)
        att = jnp.where(low_q, both[:ROWS], both[ROWS:]).astype(BF16)
        att_f = att.astype(F32)
        delta = jnp.sum(
            da2.astype(F32) * jnp.concatenate([att_f, att_f], 0), axis=-1, keepdims=True
        )
        dscores = (weights * (dot(da2, value, NT) - delta)).astype(BF16)
        both = dot(dscores, key) * SCALE
        dqs.append(jnp.where(low_q, both[:ROWS], both[ROWS:]).astype(BF16))
        dk = dot(dscores, q2, TN) * SCALE
        dv = dot(probs, da2, TN)
        dks.append(dk + swapped(dk))
        dvs.append(dv + swapped(dv))
        atts.append(att)
    att = jnp.concatenate(atts, 1)
    dq = jnp.concatenate(dqs, 1)
    dk = jnp.where(low_k, dks[0], dks[1])
    dv = jnp.where(low_k, dvs[0], dvs[1])
    att_ref[...] = att
    dq_ref[...] = dq
    own_grad_ref[0] = dk[256:]
    own_grad_ref[1] = dv[256:]
    dk, dv = dk.astype(BF16), dv.astype(BF16)
    far_grad_ref[0] = dk[:128]
    far_grad_ref[1] = dv[:128]
    near_grad_ref[0] = dk[128:256]
    near_grad_ref[1] = dv[128:256]
    rounded = jnp.concatenate([dk, dv], axis=1)
    for half, out in ((0, send_ref), (1, keep_ref)):
        tp = tp_ref[half]
        t_own, t_out = tp[:, :LANES], tp[:, LANES:]
        out[:, :256] = dot(t_out, att).astype(BF16)
        out[:, 256:512] = dot(t_own, dq).astype(BF16)
        out[:, 512:] = (dot(t_own, rounded[256:]) + dot(th_ref[half], rounded[:256])).astype(BF16)


def attention(first, steps, place, far, near, own, q, da, wk, wv, tp, th):
    def columns(rows, cols):
        return pl.BlockSpec((rows, cols), lambda i: (0, first + i))

    def fresh(rows, cols):
        return pl.BlockSpec((rows, cols), lambda i: (0, i))

    def struct(rows, cols, dtype):
        return jax.ShapeDtypeStruct((rows, cols * steps), dtype)

    return pl.pallas_call(
        attention_kernel,
        grid=(steps,),
        out_shape=(
            struct(ROWS, QCOLS, BF16),
            struct(ROWS, QCOLS, BF16),
            jax.ShapeDtypeStruct((2, ROWS, KCOLS * steps), F32),
            jax.ShapeDtypeStruct((2, ROWS, KCOLS * steps), BF16),
            jax.ShapeDtypeStruct((2, ROWS, KCOLS * steps), BF16),
            struct(512, GCOLS, BF16),
            struct(512, GCOLS, BF16),
        ),
        in_specs=[
            pl.BlockSpec(memory_space=pltpu.SMEM),
            whole(ROWS, MODEL),
            whole(ROWS, MODEL),
            whole(ROWS, MODEL),
            columns(ROWS, QCOLS),
            columns(ROWS, QCOLS),
            columns(MODEL, KCOLS),
            columns(MODEL, KCOLS),
            whole(2, 512, 2 * LANES),
            whole(2, 512, 2 * LANES),
        ],
        out_specs=(
            fresh(ROWS, QCOLS),
            fresh(ROWS, QCOLS),
            pl.BlockSpec((2, ROWS, KCOLS), lambda i: (0, 0, i)),
            pl.BlockSpec((2, ROWS, KCOLS), lambda i: (0, 0, i)),
            pl.BlockSpec((2, ROWS, KCOLS), lambda i: (0, 0, i)),
            fresh(512, GCOLS),
            fresh(512, GCOLS),
        ),
        compiler_params=pltpu.CompilerParams(
            dimension_semantics=("arbitrary",), vmem_limit_bytes=28 << 20
        ),
        cost_estimate=SMALL,
        name="attention",
    )(place, far, near, own, q, da, wk, wv, tp, th)


def cut(addends, rows):
    total = addends[0][rows, :].astype(F32)
    for other in addends[1:]:
        total = total + other[rows, :].astype(F32)
    return total


def fold_kernel(count, quarter, *refs):
    addends, outs = refs[:count], refs[count:]
    for d in range(4):
        outs[d][...] = cut(addends, slice(d * quarter, (d + 1) * quarter)).astype(outs[d].dtype)


def folded(*addends):
    rows, cols = addends[0].shape
    return pl.pallas_call(
        functools.partial(fold_kernel, len(addends), rows // 4),
        grid=(1,),
        out_shape=tuple(
            jax.ShapeDtypeStruct((rows // 4, cols), BF16 if d else F32) for d in range(4)
        ),
        in_specs=[whole(rows, cols)] * len(addends),
        out_specs=(whole(rows // 4, cols),) * 4,
        compiler_params=pltpu.CompilerParams(vmem_limit_bytes=20 << 20),
        name="fold",
    )(*addends)


def place_kernel(count, *refs):
    fold_kernel(2, 128, *refs[:2], *refs[2 + count :])


def folded_into(first, keep, got, wide=()):
    rows, cols = keep.shape
    given = pl.BlockSpec((rows, GCOLS), lambda i: (0, i))
    return pl.pallas_call(
        functools.partial(place_kernel, len(wide)),
        grid=(cols // GCOLS,),
        out_shape=tuple(
            jax.ShapeDtypeStruct((rows // 4, STEPS * GCOLS), BF16 if d else F32) for d in range(4)
        ),
        in_specs=[given, given] + [pl.BlockSpec(memory_space=pl.ANY)] * len(wide),
        out_specs=(pl.BlockSpec((rows // 4, GCOLS), lambda i: (0, first + i)),) * 4,
        input_output_aliases={2 + d: d for d in range(len(wide))},
        compiler_params=pltpu.CompilerParams(vmem_limit_bytes=12 << 20),
        name="place",
    )(keep, got, *wide)


def halve_kernel(own_ref, a_ref, b_ref, c_ref, keep_ref, send_ref):
    total = cut((own_ref, a_ref, b_ref, c_ref), slice(0, 8))
    keep_ref[...] = total[:4]
    send_ref[...] = total[4:].astype(BF16)


def halved(*addends):
    cols = addends[0].shape[1]
    return pl.pallas_call(
        halve_kernel,
        grid=(1,),
        out_shape=(
            jax.ShapeDtypeStruct((4, cols), F32),
            jax.ShapeDtypeStruct((4, cols), BF16),
        ),
        in_specs=[whole(8, cols)] * 4,
        out_specs=(whole(4, cols),) * 2,
        compiler_params=pltpu.CompilerParams(vmem_limit_bytes=4 << 20),
        name="halve",
    )(*addends)


def last_kernel(own_ref, got_ref, q_ref, k_ref, v_ref, o_ref):
    total = own_ref[...] + got_ref[...].astype(F32)
    for step in range(STEPS):
        base = step * GCOLS
        at = slice(step * 256, step * 256 + 256)
        o_ref[:, at] = total[:, base : base + 256]
        q_ref[:, at] = total[:, base + 256 : base + 512]
        at = slice(step * 128, step * 128 + 128)
        k_ref[:, at] = total[:, base + 512 : base + 640]
        v_ref[:, at] = total[:, base + 640 : base + 768]


def summed_last(own, got):
    shapes = [(4, 1024), (4, 512), (4, 512), (4, 1024)]
    return pl.pallas_call(
        last_kernel,
        grid=(1,),
        out_shape=tuple(jax.ShapeDtypeStruct(shape, F32) for shape in shapes),
        in_specs=[whole(*own.shape)] * 2,
        out_specs=tuple(whole(*shape) for shape in shapes),
        compiler_params=pltpu.CompilerParams(vmem_limit_bytes=4 << 20),
        name="last",
    )(own, got)


def middle_kernel(att_one, att_two, dq_one, dq_two, wo_ref, wq_ref, out_ref, base_ref):
    att = jnp.concatenate([att_one[...], att_two[...]], axis=1)
    out_ref[...] = dot(att, wo_ref[...]).astype(BF16)
    dq = jnp.concatenate([dq_one[...], dq_two[...]], axis=1)
    base_ref[...] = dot(dq, wq_ref[...], NT)


def middle(atts, dqs, wo, wq):
    block = pl.BlockSpec((ROWS, QCOLS), lambda i: (0, i))
    return pl.pallas_call(
        middle_kernel,
        grid=(STEPS,),
        out_shape=(
            jax.ShapeDtypeStruct((ROWS, MODEL), BF16),
            jax.ShapeDtypeStruct((ROWS, MODEL), F32),
        ),
        in_specs=[whole(*a.shape) for a in (*atts, *dqs)]
        + [
            pl.BlockSpec((MODEL, QCOLS), lambda i: (0, i)),
            pl.BlockSpec((QCOLS, MODEL), lambda i: (i, 0)),
        ],
        out_specs=(block, block),
        compiler_params=pltpu.CompilerParams(vmem_limit_bytes=12 << 20),
        name="middle",
    )(*atts, *dqs, wo, wq)


def tail_kernel(base_ref, own_one, own_two, handed, near, far, wk_ref, wv_ref, out_ref):
    total = base_ref[...]
    for i, w_ref in enumerate((wk_ref, wv_ref)):
        grad = jnp.concatenate([own_one[i], own_two[i]], axis=1)
        for part in (handed[0, i], near[i], far[i]):
            grad = grad + part.astype(F32)
        total = total + dot(grad.astype(BF16), w_ref[...], NT)
    out_ref[...] = total.astype(BF16)


def tail(*args):
    return pl.pallas_call(
        tail_kernel,
        grid=(1,),
        out_shape=jax.ShapeDtypeStruct((ROWS, MODEL), BF16),
        in_specs=[whole(*a.shape) for a in args],
        out_specs=whole(ROWS, MODEL),
        compiler_params=pltpu.CompilerParams(vmem_limit_bytes=20 << 20),
        name="tail",
    )(*args)


def after(value, *others):
    return lax.optimization_barrier((value, *others))[0]


def shards(tokens, query_weight, key_weight, value_matrix, out_weight, out_cotangent):
    near = passed_along(tokens, 1)
    far = passed_along(tokens, 2, range(0, 256, 2))
    me = lax.axis_index(AXIS)
    start = jnp.maximum(2 - me, 0) * ROWS
    place = jnp.stack([(me // 8) % 4, (me // 2) % 4, me % 2, me // 32, start]).astype(jnp.int32)
    wq, wk, wv, wo = map(in_hbm, (query_weight, key_weight, value_matrix, out_weight))
    q, da = early(in_hbm(tokens), in_hbm(out_cotangent), wq, wo)
    near = after(near, q)
    mate = passed_along(near, 1, range(0, 256, 2))
    (tp,) = prepared(prep_kernel, after(place, near), tokens, out_cotangent)
    th, far = prepared(halo_kernel, after(place, tp), far, mate, near)

    def attend(first, steps, place):
        return attention(first, steps, place, far, near, tokens, q, da, wk, wv, tp, th)

    one = attend(0, 3, place)
    got_one = to_mate(one[-2])
    two = attend(3, 1, after(place, one[-1]))
    got_two = to_mate(two[-2])
    sums = folded_into(0, one[-1], after(got_one, two[-1]))
    own, *sends = folded_into(3, two[-1], after(got_two, sums[0]), sums)
    ring_one = ring([None, *sends], 0)

    attn_out, base = middle((one[0], after(two[0], own)), (one[1], two[1]), wo, wq)
    grads = lax.optimization_barrier((one[3], two[3], one[4], two[4], ring_one[0]))
    near_grad = jnp.concatenate(grads[0:2], axis=-1)
    far_grad = jnp.concatenate(grads[2:4], axis=-1)
    handed = passed_along(jnp.stack([near_grad, far_grad]), -1, range(1, 256, 2))
    summed = (near_grad.astype(F32) + handed[1].astype(F32)).astype(BF16)
    own, *sends = folded(after(own, base, summed), *ring_one)
    ring_two = ring([None, *sends], 1)
    back_near = passed_along(after(summed, own), -1, range(0, 256, 2))
    back_far = passed_along(after(far_grad, own), -2, range(0, 256, 2))
    own, *sends = folded(own, *ring_two)
    ring_three = [along_z(sends[d - 1], 2 * d) for d in (1, 3, 2)]
    own, send = halved(own, *ring_three)
    got = along_z(send, 1)
    tokens_grad = tail(base, one[2], two[2], handed, back_near, back_far, key_weight, value_matrix)
    query_rows, key_rows, value_rows, out_rows = summed_last(after(own, tokens_grad), got)
    return attn_out, tokens_grad, query_rows, key_rows, value_rows, out_rows.T


def solution(mesh):
    rows = P(AXIS, None)
    return jax.shard_map(
        shards,
        mesh=mesh,
        in_specs=(rows, P(), P(), P(), P(), rows),
        out_specs=(rows, rows, rows, rows, rows, P(None, AXIS)),
        check_vma=False,
    )
```

```python
import functools

import jax
import jax.numpy as jnp
from jax import lax
from jax.experimental import pallas as pl
from jax.experimental.pallas import tpu as pltpu
from jax.sharding import PartitionSpec as P

AXIS = "seq"
ROWS = 128
MODEL = 1024
LANES = 128
STEPS = 4
QCOLS = 256
KCOLS = 128
GCOLS = 768
SCALE = 0.125
MASKED = -1e30
BF16 = jnp.bfloat16
SMALL = pl.CostEstimate(flops=1000, transcendentals=0, bytes_accessed=1000)
F32 = jnp.float32
NT = (((1,), (1,)), ((), ()))
TN = (((0,), (0,)), ((), ()))


def dot(a, b, dims=(((1,), (0,)), ((), ()))):
    return lax.dot_general(a, b, dims, preferred_element_type=F32)


def flat(z, x, y, c):
    return ((z * 4 + x) * 4 + y) * 2 + c


def in_hbm(array):
    return pltpu.with_memory_space_constraint(array, pltpu.HBM)


def route_of(step):
    places = [(z, x, y, c) for z in range(8) for x in range(4) for y in range(4) for c in range(2)]
    return [(flat(*p), flat(*step(*p))) for p in places]


def to_mate(array):
    return lax.ppermute(array, AXIS, route_of(lambda z, x, y, c: (z, x, y, 1 - c)))


def plane_step(phase, d, z, x, y, c):
    if c == phase:
        return z, (x + d) % 4, y, c
    return z, x, (y + d) % 4, c


def ring(blocks, phase):
    return [
        lax.ppermute(blocks[d], AXIS, route_of(functools.partial(plane_step, phase, d)))
        for d in (1, 3, 2)
    ]


def along_z(block, distance):
    return lax.ppermute(
        block, AXIS, route_of(lambda z, x, y, c: ((z + distance) % 8, x, y, c))
    )


def passed_along(block, distance, sources=range(256)):
    return lax.ppermute(
        block, AXIS, [(i, i + distance) for i in sources if i + distance in range(256)]
    )


def reorder(place, t_ref, out_ref):
    x, y, core, mine = place[0], place[1], place[2], place[3]
    low = lax.broadcasted_iota(jnp.int32, (8, 2 * LANES), 0) < 4
    for half in range(2):
        target = 1 - core if half == 0 else core
        zero = target == 0
        for d1 in range(4):
            for d2 in range(4):
                xs = lax.rem(x + jnp.where(zero, d1, d2), 4)
                ys = lax.rem(y + jnp.where(zero, d2, d1), 4)
                for z in range(0, 8, 4):
                    rows = []
                    for pair in range(2):
                        base = xs * 32 + ys * 8
                        at = base + lax.rem(mine + z + 2 * pair, 8) * 128
                        one = t_ref[pl.ds(pl.multiple_of(at, 8), 8), :]
                        at = base + lax.rem(mine + z + 2 * pair + 1, 8) * 128
                        two = t_ref[pl.ds(pl.multiple_of(at, 8), 8), :]
                        c0 = jnp.where(low, one, pltpu.roll(two, 4, 0))
                        c1 = jnp.where(low, pltpu.roll(one, 4, 0), two)
                        rows.append(jnp.where(zero, c0, c1))
                    row = (d1 * 4 + d2) * 32 + z * 4
                    out_ref[half, row : row + 16, :] = jnp.concatenate(rows, 0).astype(BF16)


def early_kernel(tok_ref, cot_ref, wq_ref, wo_ref, q_ref, da_ref):
    q_ref[...] = dot(tok_ref[...], wq_ref[...]).astype(BF16)
    da_ref[...] = dot(cot_ref[...], wo_ref[...], NT).astype(BF16)


def whole(*shape):
    return pl.BlockSpec(shape, lambda i: (0,) * len(shape))


def early(tokens, cotangent, wq, wo):
    block = pl.BlockSpec((ROWS, QCOLS), lambda i: (0, i))
    return pl.pallas_call(
        early_kernel,
        grid=(STEPS,),
        out_shape=(jax.ShapeDtypeStruct((ROWS, MODEL), BF16),) * 2,
        in_specs=[
            whole(ROWS, MODEL),
            whole(ROWS, MODEL),
            pl.BlockSpec((MODEL, QCOLS), lambda i: (0, i)),
            pl.BlockSpec((QCOLS, MODEL), lambda i: (i, 0)),
        ],
        out_specs=(block, block),
        compiler_params=pltpu.CompilerParams(
            dimension_semantics=("arbitrary",), vmem_limit_bytes=12 << 20
        ),
        name="early",
    )(tokens, cotangent, wq, wo)


def prep_kernel(place, a_ref, b_ref, out_ref, t_ref):
    t_ref[:, :LANES] = a_ref[...].astype(F32).T
    t_ref[:, LANES:] = b_ref[...].astype(F32).T
    reorder(place, t_ref, out_ref)


def halo_kernel(place, far_ref, mate_ref, near_ref, out_ref, got_ref, t_ref):
    @pl.when(place[2] == 0)
    def _():
        got_ref[...] = far_ref[...]

    @pl.when(place[2] == 1)
    def _():
        got_ref[...] = mate_ref[...]

    prep_kernel(place, got_ref, near_ref, out_ref, t_ref)


def prepared(kernel, place, *blocks):
    order = jax.ShapeDtypeStruct((2, 512, 2 * LANES), BF16), whole(2, 512, 2 * LANES)
    outs = [order] if len(blocks) == 2 else [order, (jax.ShapeDtypeStruct((ROWS, MODEL), BF16), whole(ROWS, MODEL))]
    return pl.pallas_call(
        kernel,
        grid=(1,),
        out_shape=[o[0] for o in outs],
        in_specs=[pl.BlockSpec(memory_space=pltpu.SMEM)] + [whole(ROWS, MODEL)] * len(blocks),
        out_specs=[o[1] for o in outs],
        scratch_shapes=[pltpu.VMEM((MODEL, 2 * LANES), F32)],
        compiler_params=pltpu.CompilerParams(vmem_limit_bytes=12 << 20),
        name="prep",
    )(place, *blocks)


def swapped(a):
    return pltpu.roll(a, 64, 1)


def attention_kernel(
    place,
    far_ref,
    near_ref,
    own_ref,
    q_ref,
    da_ref,
    wk_ref,
    wv_ref,
    tp_ref,
    th_ref,
    att_ref,
    dq_ref,
    own_grad_ref,
    near_grad_ref,
    far_grad_ref,
    send_ref,
    keep_ref,
):
    window = jnp.concatenate([far_ref[...], near_ref[...], own_ref[...]], axis=0)
    keys = dot(window, wk_ref[...])
    values = dot(window, wv_ref[...])
    start = place[4]
    row = lax.rem(lax.broadcasted_iota(jnp.int32, (256, 384), 0), 128)
    col = lax.broadcasted_iota(jnp.int32, (256, 384), 1)
    allowed = (col <= row + 256) & (col >= start)
    low_k = lax.broadcasted_iota(jnp.int32, (384, LANES), 1) < 64
    low_q = lax.broadcasted_iota(jnp.int32, (ROWS, LANES), 1) < 64
    zero = jnp.zeros((ROWS, LANES), BF16)
    keys_swapped, values_swapped = swapped(keys), swapped(values)
    atts, dqs, dks, dvs = [], [], [], []
    for head in range(2):
        own_half = low_k if head == 0 else ~low_k
        key = jnp.where(own_half, keys, keys_swapped).astype(BF16)
        value = jnp.where(own_half, values, values_swapped).astype(BF16)
        cols = slice(head * LANES, (head + 1) * LANES)
        q = q_ref[:, cols]
        da = da_ref[:, cols]
        q2 = jnp.concatenate([jnp.where(low_q, q, zero), jnp.where(low_q, zero, q)], 0)
        da2 = jnp.concatenate([jnp.where(low_q, da, zero), jnp.where(low_q, zero, da)], 0)
        scores = jnp.where(allowed, dot(q2, key, NT) * SCALE, MASKED)
        highest = jnp.max(scores, axis=-1, keepdims=True)
        weights = jnp.exp(scores - highest)
        weights = weights * (1.0 / jnp.sum(weights, axis=-1, keepdims=True))
        probs = weights.astype(BF16)
        both = dot(probs, value)
        att = jnp.where(low_q, both[:ROWS], both[ROWS:]).astype(BF16)
        att_f = att.astype(F32)
        delta = jnp.sum(
            da2.astype(F32) * jnp.concatenate([att_f, att_f], 0), axis=-1, keepdims=True
        )
        dscores = (weights * (dot(da2, value, NT) - delta)).astype(BF16)
        both = dot(dscores, key) * SCALE
        dqs.append(jnp.where(low_q, both[:ROWS], both[ROWS:]).astype(BF16))
        dk = dot(dscores, q2, TN) * SCALE
        dv = dot(probs, da2, TN)
        dks.append(dk + swapped(dk))
        dvs.append(dv + swapped(dv))
        atts.append(att)
    att = jnp.concatenate(atts, 1)
    dq = jnp.concatenate(dqs, 1)
    dk = jnp.where(low_k, dks[0], dks[1])
    dv = jnp.where(low_k, dvs[0], dvs[1])
    att_ref[...] = att
    dq_ref[...] = dq
    own_grad_ref[0] = dk[256:]
    own_grad_ref[1] = dv[256:]
    dk, dv = dk.astype(BF16), dv.astype(BF16)
    far_grad_ref[0] = dk[:128]
    far_grad_ref[1] = dv[:128]
    near_grad_ref[0] = dk[128:256]
    near_grad_ref[1] = dv[128:256]
    rounded = jnp.concatenate([dk, dv], axis=1)
    for half, out in ((0, send_ref), (1, keep_ref)):
        tp = tp_ref[half]
        t_own, t_out = tp[:, :LANES], tp[:, LANES:]
        out[:, :256] = dot(t_out, att).astype(BF16)
        out[:, 256:512] = dot(t_own, dq).astype(BF16)
        out[:, 512:] = (dot(t_own, rounded[256:]) + dot(th_ref[half], rounded[:256])).astype(BF16)


def attention(first, steps, place, far, near, own, q, da, wk, wv, tp, th):
    def columns(rows, cols):
        return pl.BlockSpec((rows, cols), lambda i: (0, first + i))

    def fresh(rows, cols):
        return pl.BlockSpec((rows, cols), lambda i: (0, i))

    def struct(rows, cols, dtype):
        return jax.ShapeDtypeStruct((rows, cols * steps), dtype)

    return pl.pallas_call(
        attention_kernel,
        grid=(steps,),
        out_shape=(
            struct(ROWS, QCOLS, BF16),
            struct(ROWS, QCOLS, BF16),
            jax.ShapeDtypeStruct((2, ROWS, KCOLS * steps), F32),
            jax.ShapeDtypeStruct((2, ROWS, KCOLS * steps), BF16),
            jax.ShapeDtypeStruct((2, ROWS, KCOLS * steps), BF16),
            struct(512, GCOLS, BF16),
            struct(512, GCOLS, BF16),
        ),
        in_specs=[
            pl.BlockSpec(memory_space=pltpu.SMEM),
            whole(ROWS, MODEL),
            whole(ROWS, MODEL),
            whole(ROWS, MODEL),
            columns(ROWS, QCOLS),
            columns(ROWS, QCOLS),
            columns(MODEL, KCOLS),
            columns(MODEL, KCOLS),
            whole(2, 512, 2 * LANES),
            whole(2, 512, 2 * LANES),
        ],
        out_specs=(
            fresh(ROWS, QCOLS),
            fresh(ROWS, QCOLS),
            pl.BlockSpec((2, ROWS, KCOLS), lambda i: (0, 0, i)),
            pl.BlockSpec((2, ROWS, KCOLS), lambda i: (0, 0, i)),
            pl.BlockSpec((2, ROWS, KCOLS), lambda i: (0, 0, i)),
            fresh(512, GCOLS),
            fresh(512, GCOLS),
        ),
        compiler_params=pltpu.CompilerParams(
            dimension_semantics=("arbitrary",), vmem_limit_bytes=28 << 20
        ),
        cost_estimate=SMALL,
        name="attention",
    )(place, far, near, own, q, da, wk, wv, tp, th)


def cut(addends, rows):
    total = addends[0][rows, :].astype(F32)
    for other in addends[1:]:
        total = total + other[rows, :].astype(F32)
    return total


def fold_kernel(count, quarter, *refs):
    addends, outs = refs[:count], refs[count:]
    for d in range(4):
        outs[d][...] = cut(addends, slice(d * quarter, (d + 1) * quarter)).astype(outs[d].dtype)


def folded(*addends):
    rows, cols = addends[0].shape
    return pl.pallas_call(
        functools.partial(fold_kernel, len(addends), rows // 4),
        grid=(1,),
        out_shape=tuple(
            jax.ShapeDtypeStruct((rows // 4, cols), BF16 if d else F32) for d in range(4)
        ),
        in_specs=[whole(rows, cols)] * len(addends),
        out_specs=(whole(rows // 4, cols),) * 4,
        compiler_params=pltpu.CompilerParams(vmem_limit_bytes=20 << 20),
        name="fold",
    )(*addends)


def place_kernel(count, *refs):
    fold_kernel(2, 128, *refs[:2], *refs[2 + count :])


def folded_into(first, keep, got, wide=()):
    rows, cols = keep.shape
    given = pl.BlockSpec((rows, GCOLS), lambda i: (0, i))
    return pl.pallas_call(
        functools.partial(place_kernel, len(wide)),
        grid=(cols // GCOLS,),
        out_shape=tuple(
            jax.ShapeDtypeStruct((rows // 4, STEPS * GCOLS), BF16 if d else F32) for d in range(4)
        ),
        in_specs=[given, given] + [pl.BlockSpec(memory_space=pl.ANY)] * len(wide),
        out_specs=(pl.BlockSpec((rows // 4, GCOLS), lambda i: (0, first + i)),) * 4,
        input_output_aliases={2 + d: d for d in range(len(wide))},
        compiler_params=pltpu.CompilerParams(vmem_limit_bytes=12 << 20),
        name="place",
    )(keep, got, *wide)


def halve_kernel(own_ref, a_ref, b_ref, c_ref, keep_ref, send_ref):
    total = cut((own_ref, a_ref, b_ref, c_ref), slice(0, 8))
    keep_ref[...] = total[:4]
    send_ref[...] = total[4:].astype(BF16)


def halved(*addends):
    cols = addends[0].shape[1]
    return pl.pallas_call(
        halve_kernel,
        grid=(1,),
        out_shape=(
            jax.ShapeDtypeStruct((4, cols), F32),
            jax.ShapeDtypeStruct((4, cols), BF16),
        ),
        in_specs=[whole(8, cols)] * 4,
        out_specs=(whole(4, cols),) * 2,
        compiler_params=pltpu.CompilerParams(vmem_limit_bytes=4 << 20),
        name="halve",
    )(*addends)


def last_kernel(own_ref, got_ref, q_ref, k_ref, v_ref, o_ref):
    total = own_ref[...] + got_ref[...].astype(F32)
    for step in range(STEPS):
        base = step * GCOLS
        at = slice(step * 256, step * 256 + 256)
        o_ref[:, at] = total[:, base : base + 256]
        q_ref[:, at] = total[:, base + 256 : base + 512]
        at = slice(step * 128, step * 128 + 128)
        k_ref[:, at] = total[:, base + 512 : base + 640]
        v_ref[:, at] = total[:, base + 640 : base + 768]


def summed_last(own, got):
    shapes = [(4, 1024), (4, 512), (4, 512), (4, 1024)]
    return pl.pallas_call(
        last_kernel,
        grid=(1,),
        out_shape=tuple(jax.ShapeDtypeStruct(shape, F32) for shape in shapes),
        in_specs=[whole(*own.shape)] * 2,
        out_specs=tuple(whole(*shape) for shape in shapes),
        compiler_params=pltpu.CompilerParams(vmem_limit_bytes=4 << 20),
        name="last",
    )(own, got)


def middle_kernel(att_one, att_two, dq_one, dq_two, wo_ref, wq_ref, out_ref, base_ref):
    att = jnp.concatenate([att_one[...], att_two[...]], axis=1)
    out_ref[...] = dot(att, wo_ref[...]).astype(BF16)
    dq = jnp.concatenate([dq_one[...], dq_two[...]], axis=1)
    base_ref[...] = dot(dq, wq_ref[...], NT)


def middle(atts, dqs, wo, wq):
    block = pl.BlockSpec((ROWS, QCOLS), lambda i: (0, i))
    return pl.pallas_call(
        middle_kernel,
        grid=(STEPS,),
        out_shape=(
            jax.ShapeDtypeStruct((ROWS, MODEL), BF16),
            jax.ShapeDtypeStruct((ROWS, MODEL), F32),
        ),
        in_specs=[whole(*a.shape) for a in (*atts, *dqs)]
        + [
            pl.BlockSpec((MODEL, QCOLS), lambda i: (0, i)),
            pl.BlockSpec((QCOLS, MODEL), lambda i: (i, 0)),
        ],
        out_specs=(block, block),
        compiler_params=pltpu.CompilerParams(vmem_limit_bytes=12 << 20),
        name="middle",
    )(*atts, *dqs, wo, wq)


def tail_kernel(place, base_ref, own_one, own_two, mine_ref, other_ref, wk_ref, wv_ref, out_ref):
    total = base_ref[...]
    for i, w_ref in enumerate((wk_ref, wv_ref)):
        grad = jnp.concatenate([own_one[i], own_two[i]], axis=1)
        grad = grad + jnp.where(place[2] == i, mine_ref[...], other_ref[...].astype(F32))
        total = total + dot(grad.astype(BF16), w_ref[...], NT)
    out_ref[...] = total.astype(BF16)


def tail(place, *args):
    return pl.pallas_call(
        tail_kernel,
        grid=(1,),
        out_shape=jax.ShapeDtypeStruct((ROWS, MODEL), BF16),
        in_specs=[pl.BlockSpec(memory_space=pltpu.SMEM)] + [whole(*a.shape) for a in args],
        out_specs=whole(ROWS, MODEL),
        compiler_params=pltpu.CompilerParams(vmem_limit_bytes=20 << 20),
        name="tail",
    )(place, *args)


def on_place(kernel, name, outs, *args):
    return pl.pallas_call(
        kernel,
        grid=(1,),
        out_shape=tuple(jax.ShapeDtypeStruct(shape, kind) for shape, kind in outs),
        in_specs=[pl.BlockSpec(memory_space=pltpu.SMEM)] + [whole(*a.shape) for a in args[1:]],
        out_specs=tuple(whole(*shape) for shape, _ in outs),
        compiler_params=pltpu.CompilerParams(vmem_limit_bytes=8 << 20),
        name=name,
    )(*args)


def hand_kernel(place, near_one, near_two, far_one, far_two, give_ref, keep_ref):
    core = place[2]
    for i, (one, two) in enumerate(((near_one, near_two), (far_one, far_two))):
        split = one.shape[2]
        give_ref[i, :, :split] = one[1 - core]
        give_ref[i, :, split:] = two[1 - core]
        keep_ref[i, :, :split] = one[core]
        keep_ref[i, :, split:] = two[core]


def handed(*args):
    return on_place(hand_kernel, "hand", [((2, ROWS, 512), BF16)] * 2, *args)


def met_kernel(place, keep_ref, got_ref, back_ref, near_ref):
    def fill(zero, one):
        back_ref[0] = (zero[0].astype(F32) + one[1].astype(F32)).astype(BF16)
        back_ref[1] = zero[1]
        near_ref[...] = one[0]

    @pl.when(place[2] == 0)
    def _():
        fill(keep_ref, got_ref)

    @pl.when(place[2] == 1)
    def _():
        fill(got_ref, keep_ref)


def met(*args):
    return on_place(met_kernel, "met", [((2, ROWS, 512), BF16), ((ROWS, 512), BF16)], *args)


def turn_kernel(place, back_ref, near_ref, mine_ref, other_ref):
    at_zero = back_ref[1].astype(F32) + near_ref[...].astype(F32)
    at_one = back_ref[0].astype(F32)

    @pl.when(place[2] == 0)
    def _():
        mine_ref[...] = at_zero
        other_ref[...] = at_one.astype(BF16)

    @pl.when(place[2] == 1)
    def _():
        mine_ref[...] = at_one
        other_ref[...] = at_zero.astype(BF16)


def turned(*args):
    return on_place(turn_kernel, "turn", [((ROWS, 512), F32), ((ROWS, 512), BF16)], *args)


def after(value, *others):
    return lax.optimization_barrier((value, *others))[0]


def shards(tokens, query_weight, key_weight, value_matrix, out_weight, out_cotangent):
    near = passed_along(tokens, 1)
    far = passed_along(tokens, 2, range(0, 256, 2))
    me = lax.axis_index(AXIS)
    start = jnp.maximum(2 - me, 0) * ROWS
    place = jnp.stack([(me // 8) % 4, (me // 2) % 4, me % 2, me // 32, start]).astype(jnp.int32)
    wq, wk, wv, wo = map(in_hbm, (query_weight, key_weight, value_matrix, out_weight))
    q, da = early(in_hbm(tokens), in_hbm(out_cotangent), wq, wo)
    near = after(near, q)
    mate = passed_along(near, 1, range(0, 256, 2))
    (tp,) = prepared(prep_kernel, after(place, near), tokens, out_cotangent)
    th, far = prepared(halo_kernel, after(place, tp), far, mate, near)

    def attend(first, steps, place):
        return attention(first, steps, place, far, near, tokens, q, da, wk, wv, tp, th)

    one = attend(0, 3, place)
    got_one = to_mate(one[-2])
    two = attend(3, 1, after(place, one[-1]))
    got_two = to_mate(two[-2])
    sums = folded_into(0, one[-1], after(got_one, two[-1]))
    hand_give, hand_keep = handed(after(place, sums[0]), one[3], two[3], one[4], two[4])
    own, *sends = folded_into(3, two[-1], after(got_two, hand_keep), sums)
    ring_one = ring([None, *sends], 0)

    attn_out, base = middle((one[0], after(two[0], own)), (one[1], two[1]), wo, wq)
    back, near_one = met(after(place, base), hand_keep, to_mate(hand_give))
    own, *sends = folded(after(own, base, back), *ring_one)
    ring_two = ring([None, *sends], 1)
    own, *sends = folded(own, *ring_two)
    back = passed_along(after(back, own), -2)
    ring_three = [along_z(sends[d - 1], 2 * d) for d in (1, 3, 2)]
    own, send = halved(own, *ring_three)
    got = along_z(send, 1)
    mine, other = turned(after(place, own), back, near_one)
    other = to_mate(other)
    tokens_grad = tail(place, base, one[2], two[2], mine, other, key_weight, value_matrix)
    query_rows, key_rows, value_rows, out_rows = summed_last(after(own, tokens_grad), got)
    return attn_out, tokens_grad, query_rows, key_rows, value_rows, out_rows.T


def solution(mesh):
    rows = P(AXIS, None)
    return jax.shard_map(
        shards,
        mesh=mesh,
        in_specs=(rows, P(), P(), P(), P(), rows),
        out_specs=(rows, rows, rows, rows, rows, P(None, AXIS)),
        check_vma=False,
    )
```

```python
import functools

import jax
import jax.numpy as jnp
from jax import lax
from jax.experimental import pallas as pl
from jax.experimental.pallas import tpu as pltpu
from jax.sharding import PartitionSpec as P

AXIS = "seq"
ROWS = 128
MODEL = 1024
LANES = 128
STEPS = 4
QCOLS = 256
KCOLS = 128
GCOLS = 768
SCALE = 0.125
MASKED = -1e30
BF16 = jnp.bfloat16
SMALL = pl.CostEstimate(flops=1000, transcendentals=0, bytes_accessed=1000)
F32 = jnp.float32
NT = (((1,), (1,)), ((), ()))
TN = (((0,), (0,)), ((), ()))


def dot(a, b, dims=(((1,), (0,)), ((), ()))):
    return lax.dot_general(a, b, dims, preferred_element_type=F32)


def flat(z, x, y, c):
    return ((z * 4 + x) * 4 + y) * 2 + c


def in_hbm(array):
    return pltpu.with_memory_space_constraint(array, pltpu.HBM)


def route_of(step):
    places = [(z, x, y, c) for z in range(8) for x in range(4) for y in range(4) for c in range(2)]
    return [(flat(*p), flat(*step(*p))) for p in places]


def to_mate(array):
    return lax.ppermute(array, AXIS, route_of(lambda z, x, y, c: (z, x, y, 1 - c)))


def plane_step(phase, d, z, x, y, c):
    if c == phase:
        return z, (x + d) % 4, y, c
    return z, x, (y + d) % 4, c


def ring(blocks, phase):
    return [
        lax.ppermute(blocks[d], AXIS, route_of(functools.partial(plane_step, phase, d)))
        for d in (1, 3, 2)
    ]


def along_z(block, distance):
    return lax.ppermute(
        block, AXIS, route_of(lambda z, x, y, c: ((z + distance) % 8, x, y, c))
    )


def passed_along(block, distance, sources=range(256)):
    return lax.ppermute(
        block, AXIS, [(i, i + distance) for i in sources if i + distance in range(256)]
    )


def reorder(place, t_ref, out_ref):
    x, y, core, mine = place[0], place[1], place[2], place[3]
    low = lax.broadcasted_iota(jnp.int32, (8, 2 * LANES), 0) < 4
    for half in range(2):
        target = 1 - core if half == 0 else core
        zero = target == 0
        for d1 in range(4):
            for d2 in range(4):
                xs = lax.rem(x + jnp.where(zero, d1, d2), 4)
                ys = lax.rem(y + jnp.where(zero, d2, d1), 4)
                for z in range(0, 8, 4):
                    rows = []
                    for pair in range(2):
                        base = xs * 32 + ys * 8
                        at = base + lax.rem(mine + z + 2 * pair, 8) * 128
                        one = t_ref[pl.ds(pl.multiple_of(at, 8), 8), :]
                        at = base + lax.rem(mine + z + 2 * pair + 1, 8) * 128
                        two = t_ref[pl.ds(pl.multiple_of(at, 8), 8), :]
                        c0 = jnp.where(low, one, pltpu.roll(two, 4, 0))
                        c1 = jnp.where(low, pltpu.roll(one, 4, 0), two)
                        rows.append(jnp.where(zero, c0, c1))
                    row = (d1 * 4 + d2) * 32 + z * 4
                    out_ref[half, row : row + 16, :] = jnp.concatenate(rows, 0).astype(BF16)


def early_kernel(tok_ref, cot_ref, wq_ref, wo_ref, q_ref, da_ref):
    q_ref[...] = dot(tok_ref[...], wq_ref[...]).astype(BF16)
    da_ref[...] = dot(cot_ref[...], wo_ref[...], NT).astype(BF16)


def whole(*shape):
    return pl.BlockSpec(shape, lambda i: (0,) * len(shape))


def early(tokens, cotangent, wq, wo):
    block = pl.BlockSpec((ROWS, QCOLS), lambda i: (0, i))
    return pl.pallas_call(
        early_kernel,
        grid=(STEPS,),
        out_shape=(jax.ShapeDtypeStruct((ROWS, MODEL), BF16),) * 2,
        in_specs=[
            whole(ROWS, MODEL),
            whole(ROWS, MODEL),
            pl.BlockSpec((MODEL, QCOLS), lambda i: (0, i)),
            pl.BlockSpec((QCOLS, MODEL), lambda i: (i, 0)),
        ],
        out_specs=(block, block),
        compiler_params=pltpu.CompilerParams(
            dimension_semantics=("arbitrary",), vmem_limit_bytes=12 << 20
        ),
        name="early",
    )(tokens, cotangent, wq, wo)


def prep_kernel(place, a_ref, b_ref, out_ref, t_ref):
    t_ref[:, :LANES] = a_ref[...].astype(F32).T
    t_ref[:, LANES:] = b_ref[...].astype(F32).T
    reorder(place, t_ref, out_ref)


def halo_kernel(place, far_ref, mate_ref, near_ref, out_ref, got_ref, t_ref):
    @pl.when(place[2] == 0)
    def _():
        got_ref[...] = far_ref[...]

    @pl.when(place[2] == 1)
    def _():
        got_ref[...] = mate_ref[...]

    prep_kernel(place, got_ref, near_ref, out_ref, t_ref)


def prepared(kernel, place, *blocks):
    order = jax.ShapeDtypeStruct((2, 512, 2 * LANES), BF16), whole(2, 512, 2 * LANES)
    outs = [order] if len(blocks) == 2 else [order, (jax.ShapeDtypeStruct((ROWS, MODEL), BF16), whole(ROWS, MODEL))]
    return pl.pallas_call(
        kernel,
        grid=(1,),
        out_shape=[o[0] for o in outs],
        in_specs=[pl.BlockSpec(memory_space=pltpu.SMEM)] + [whole(ROWS, MODEL)] * len(blocks),
        out_specs=[o[1] for o in outs],
        scratch_shapes=[pltpu.VMEM((MODEL, 2 * LANES), F32)],
        compiler_params=pltpu.CompilerParams(vmem_limit_bytes=12 << 20),
        name="prep",
    )(place, *blocks)


def swapped(a):
    return pltpu.roll(a, 64, 1)


def attention_kernel(
    place,
    far_ref,
    near_ref,
    own_ref,
    q_ref,
    da_ref,
    wk_ref,
    wv_ref,
    tp_ref,
    th_ref,
    att_ref,
    dq_ref,
    own_grad_ref,
    near_grad_ref,
    far_grad_ref,
    send_ref,
    keep_ref,
):
    window = jnp.concatenate([far_ref[...], near_ref[...], own_ref[...]], axis=0)
    keys = dot(window, wk_ref[...])
    values = dot(window, wv_ref[...])
    start = place[4]
    row = lax.rem(lax.broadcasted_iota(jnp.int32, (256, 384), 0), 128)
    col = lax.broadcasted_iota(jnp.int32, (256, 384), 1)
    allowed = (col <= row + 256) & (col >= start)
    low_k = lax.broadcasted_iota(jnp.int32, (384, LANES), 1) < 64
    low_q = lax.broadcasted_iota(jnp.int32, (ROWS, LANES), 1) < 64
    zero = jnp.zeros((ROWS, LANES), BF16)
    keys_swapped, values_swapped = swapped(keys), swapped(values)
    atts, dqs, dks, dvs = [], [], [], []
    for head in range(2):
        own_half = low_k if head == 0 else ~low_k
        key = jnp.where(own_half, keys, keys_swapped).astype(BF16)
        value = jnp.where(own_half, values, values_swapped).astype(BF16)
        cols = slice(head * LANES, (head + 1) * LANES)
        q = q_ref[:, cols]
        da = da_ref[:, cols]
        q2 = jnp.concatenate([jnp.where(low_q, q, zero), jnp.where(low_q, zero, q)], 0)
        da2 = jnp.concatenate([jnp.where(low_q, da, zero), jnp.where(low_q, zero, da)], 0)
        scores = jnp.where(allowed, dot(q2, key, NT) * SCALE, MASKED)
        highest = jnp.max(scores, axis=-1, keepdims=True)
        weights = jnp.exp(scores - highest)
        weights = weights * (1.0 / jnp.sum(weights, axis=-1, keepdims=True))
        probs = weights.astype(BF16)
        both = dot(probs, value)
        att = jnp.where(low_q, both[:ROWS], both[ROWS:]).astype(BF16)
        att_f = att.astype(F32)
        delta = jnp.sum(
            da2.astype(F32) * jnp.concatenate([att_f, att_f], 0), axis=-1, keepdims=True
        )
        dscores = (weights * (dot(da2, value, NT) - delta)).astype(BF16)
        both = dot(dscores, key) * SCALE
        dqs.append(jnp.where(low_q, both[:ROWS], both[ROWS:]).astype(BF16))
        dk = dot(dscores, q2, TN) * SCALE
        dv = dot(probs, da2, TN)
        dks.append(dk + swapped(dk))
        dvs.append(dv + swapped(dv))
        atts.append(att)
    att = jnp.concatenate(atts, 1)
    dq = jnp.concatenate(dqs, 1)
    dk = jnp.where(low_k, dks[0], dks[1])
    dv = jnp.where(low_k, dvs[0], dvs[1])
    att_ref[...] = att
    dq_ref[...] = dq
    own_grad_ref[0] = dk[256:]
    own_grad_ref[1] = dv[256:]
    dk, dv = dk.astype(BF16), dv.astype(BF16)
    far_grad_ref[0] = dk[:128]
    far_grad_ref[1] = dv[:128]
    near_grad_ref[0] = dk[128:256]
    near_grad_ref[1] = dv[128:256]
    rounded = jnp.concatenate([dk, dv], axis=1)
    for half, out in ((0, send_ref), (1, keep_ref)):
        tp = tp_ref[half]
        t_own, t_out = tp[:, :LANES], tp[:, LANES:]
        out[:, :256] = dot(t_out, att).astype(BF16)
        out[:, 256:512] = dot(t_own, dq).astype(BF16)
        out[:, 512:] = (dot(t_own, rounded[256:]) + dot(th_ref[half], rounded[:256])).astype(BF16)


def attention(first, steps, place, far, near, own, q, da, wk, wv, tp, th):
    def columns(rows, cols):
        return pl.BlockSpec((rows, cols), lambda i: (0, first + i))

    def fresh(rows, cols):
        return pl.BlockSpec((rows, cols), lambda i: (0, i))

    def struct(rows, cols, dtype):
        return jax.ShapeDtypeStruct((rows, cols * steps), dtype)

    return pl.pallas_call(
        attention_kernel,
        grid=(steps,),
        out_shape=(
            struct(ROWS, QCOLS, BF16),
            struct(ROWS, QCOLS, BF16),
            jax.ShapeDtypeStruct((2, ROWS, KCOLS * steps), F32),
            jax.ShapeDtypeStruct((2, ROWS, KCOLS * steps), BF16),
            jax.ShapeDtypeStruct((2, ROWS, KCOLS * steps), BF16),
            struct(512, GCOLS, BF16),
            struct(512, GCOLS, BF16),
        ),
        in_specs=[
            pl.BlockSpec(memory_space=pltpu.SMEM),
            whole(ROWS, MODEL),
            whole(ROWS, MODEL),
            whole(ROWS, MODEL),
            columns(ROWS, QCOLS),
            columns(ROWS, QCOLS),
            columns(MODEL, KCOLS),
            columns(MODEL, KCOLS),
            whole(2, 512, 2 * LANES),
            whole(2, 512, 2 * LANES),
        ],
        out_specs=(
            fresh(ROWS, QCOLS),
            fresh(ROWS, QCOLS),
            pl.BlockSpec((2, ROWS, KCOLS), lambda i: (0, 0, i)),
            pl.BlockSpec((2, ROWS, KCOLS), lambda i: (0, 0, i)),
            pl.BlockSpec((2, ROWS, KCOLS), lambda i: (0, 0, i)),
            fresh(512, GCOLS),
            fresh(512, GCOLS),
        ),
        compiler_params=pltpu.CompilerParams(
            dimension_semantics=("arbitrary",), vmem_limit_bytes=28 << 20
        ),
        cost_estimate=SMALL,
        name="attention",
    )(place, far, near, own, q, da, wk, wv, tp, th)


def cut(addends, rows):
    total = addends[0][rows, :].astype(F32)
    for other in addends[1:]:
        total = total + other[rows, :].astype(F32)
    return total


def fold_kernel(count, quarter, *refs):
    addends, outs = refs[:count], refs[count:]
    for d in range(4):
        outs[d][...] = cut(addends, slice(d * quarter, (d + 1) * quarter)).astype(outs[d].dtype)


def folded(*addends):
    rows, cols = addends[0].shape
    return pl.pallas_call(
        functools.partial(fold_kernel, len(addends), rows // 4),
        grid=(1,),
        out_shape=tuple(
            jax.ShapeDtypeStruct((rows // 4, cols), BF16 if d else F32) for d in range(4)
        ),
        in_specs=[whole(rows, cols)] * len(addends),
        out_specs=(whole(rows // 4, cols),) * 4,
        compiler_params=pltpu.CompilerParams(vmem_limit_bytes=20 << 20),
        name="fold",
    )(*addends)


def place_kernel(count, *refs):
    fold_kernel(2, 128, *refs[:2], *refs[2 + count :])


def folded_into(first, keep, got, wide=()):
    rows, cols = keep.shape
    given = pl.BlockSpec((rows, GCOLS), lambda i: (0, i))
    return pl.pallas_call(
        functools.partial(place_kernel, len(wide)),
        grid=(cols // GCOLS,),
        out_shape=tuple(
            jax.ShapeDtypeStruct((rows // 4, STEPS * GCOLS), BF16 if d else F32) for d in range(4)
        ),
        in_specs=[given, given] + [pl.BlockSpec(memory_space=pl.ANY)] * len(wide),
        out_specs=(pl.BlockSpec((rows // 4, GCOLS), lambda i: (0, first + i)),) * 4,
        input_output_aliases={2 + d: d for d in range(len(wide))},
        compiler_params=pltpu.CompilerParams(vmem_limit_bytes=12 << 20),
        name="place",
    )(keep, got, *wide)


def halve_kernel(own_ref, a_ref, b_ref, c_ref, keep_ref, send_ref):
    total = cut((own_ref, a_ref, b_ref, c_ref), slice(0, 8))
    keep_ref[...] = total[:4]
    send_ref[...] = total[4:].astype(BF16)


def halved(*addends):
    cols = addends[0].shape[1]
    return pl.pallas_call(
        halve_kernel,
        grid=(1,),
        out_shape=(
            jax.ShapeDtypeStruct((4, cols), F32),
            jax.ShapeDtypeStruct((4, cols), BF16),
        ),
        in_specs=[whole(8, cols)] * 4,
        out_specs=(whole(4, cols),) * 2,
        compiler_params=pltpu.CompilerParams(vmem_limit_bytes=4 << 20),
        name="halve",
    )(*addends)


def last_kernel(own_ref, got_ref, q_ref, k_ref, v_ref, o_ref):
    total = own_ref[...] + got_ref[...].astype(F32)
    for step in range(STEPS):
        base = step * GCOLS
        at = slice(step * 256, step * 256 + 256)
        o_ref[:, at] = total[:, base : base + 256]
        q_ref[:, at] = total[:, base + 256 : base + 512]
        at = slice(step * 128, step * 128 + 128)
        k_ref[:, at] = total[:, base + 512 : base + 640]
        v_ref[:, at] = total[:, base + 640 : base + 768]


def summed_last(own, got):
    shapes = [(4, 1024), (4, 512), (4, 512), (4, 1024)]
    return pl.pallas_call(
        last_kernel,
        grid=(1,),
        out_shape=tuple(jax.ShapeDtypeStruct(shape, F32) for shape in shapes),
        in_specs=[whole(*own.shape)] * 2,
        out_specs=tuple(whole(*shape) for shape in shapes),
        compiler_params=pltpu.CompilerParams(vmem_limit_bytes=4 << 20),
        name="last",
    )(own, got)


def middle_kernel(att_one, att_two, dq_one, dq_two, wo_ref, wq_ref, out_ref, base_ref):
    att = jnp.concatenate([att_one[...], att_two[...]], axis=1)
    out_ref[...] = dot(att, wo_ref[...]).astype(BF16)
    dq = jnp.concatenate([dq_one[...], dq_two[...]], axis=1)
    base_ref[...] = dot(dq, wq_ref[...], NT)


def middle(atts, dqs, wo, wq):
    block = pl.BlockSpec((ROWS, QCOLS), lambda i: (0, i))
    return pl.pallas_call(
        middle_kernel,
        grid=(STEPS,),
        out_shape=(
            jax.ShapeDtypeStruct((ROWS, MODEL), BF16),
            jax.ShapeDtypeStruct((ROWS, MODEL), F32),
        ),
        in_specs=[whole(*a.shape) for a in (*atts, *dqs)]
        + [
            pl.BlockSpec((MODEL, QCOLS), lambda i: (0, i)),
            pl.BlockSpec((QCOLS, MODEL), lambda i: (i, 0)),
        ],
        out_specs=(block, block),
        compiler_params=pltpu.CompilerParams(vmem_limit_bytes=12 << 20),
        name="middle",
    )(*atts, *dqs, wo, wq)


def tail_kernel(place, base_ref, own_one, own_two, mine_ref, other_ref, wk_ref, wv_ref, out_ref):
    total = base_ref[...]
    for i, w_ref in enumerate((wk_ref, wv_ref)):
        grad = jnp.concatenate([own_one[i], own_two[i]], axis=1)
        grad = grad + jnp.where(place[2] == i, mine_ref[...], other_ref[...].astype(F32))
        total = total + dot(grad.astype(BF16), w_ref[...], NT)
    out_ref[...] = total.astype(BF16)


def tail(place, *args):
    return pl.pallas_call(
        tail_kernel,
        grid=(1,),
        out_shape=jax.ShapeDtypeStruct((ROWS, MODEL), BF16),
        in_specs=[pl.BlockSpec(memory_space=pltpu.SMEM)] + [whole(*a.shape) for a in args],
        out_specs=whole(ROWS, MODEL),
        compiler_params=pltpu.CompilerParams(vmem_limit_bytes=20 << 20),
        name="tail",
    )(place, *args)


def on_place(kernel, name, outs, *args):
    return pl.pallas_call(
        kernel,
        grid=(1,),
        out_shape=tuple(jax.ShapeDtypeStruct(shape, kind) for shape, kind in outs),
        in_specs=[pl.BlockSpec(memory_space=pltpu.SMEM)] + [whole(*a.shape) for a in args[1:]],
        out_specs=tuple(whole(*shape) for shape, _ in outs),
        compiler_params=pltpu.CompilerParams(vmem_limit_bytes=8 << 20),
        name=name,
    )(*args)


def hand_kernel(place, near_one, near_two, far_one, far_two, give_ref, keep_ref):
    core = place[2]
    for i, (one, two) in enumerate(((near_one, near_two), (far_one, far_two))):
        split = one.shape[2]
        give_ref[i, :, :split] = one[1 - core]
        give_ref[i, :, split:] = two[1 - core]
        keep_ref[i, :, :split] = one[core]
        keep_ref[i, :, split:] = two[core]


def handed(*args):
    return on_place(hand_kernel, "hand", [((2, ROWS, 512), BF16)] * 2, *args)


def met_kernel(place, keep_ref, got_ref, back_ref, near_ref):
    def fill(zero, one):
        back_ref[0] = (zero[0].astype(F32) + one[1].astype(F32)).astype(BF16)
        back_ref[1] = zero[1]
        near_ref[...] = one[0]

    @pl.when(place[2] == 0)
    def _():
        fill(keep_ref, got_ref)

    @pl.when(place[2] == 1)
    def _():
        fill(got_ref, keep_ref)


def met(*args):
    return on_place(met_kernel, "met", [((2, ROWS, 512), BF16), ((ROWS, 512), BF16)], *args)


def turn_kernel(place, back_ref, near_ref, mine_ref, other_ref):
    at_zero = back_ref[1].astype(F32) + near_ref[...].astype(F32)
    at_one = back_ref[0].astype(F32)

    @pl.when(place[2] == 0)
    def _():
        mine_ref[...] = at_zero
        other_ref[...] = at_one.astype(BF16)

    @pl.when(place[2] == 1)
    def _():
        mine_ref[...] = at_one
        other_ref[...] = at_zero.astype(BF16)


def turned(*args):
    return on_place(turn_kernel, "turn", [((ROWS, 512), F32), ((ROWS, 512), BF16)], *args)


def after(value, *others):
    return lax.optimization_barrier((value, *others))[0]


def shards(tokens, query_weight, key_weight, value_matrix, out_weight, out_cotangent):
    near = passed_along(tokens, 1)
    far = passed_along(tokens, 2, range(0, 256, 2))
    me = lax.axis_index(AXIS)
    start = jnp.maximum(2 - me, 0) * ROWS
    place = jnp.stack([(me // 8) % 4, (me // 2) % 4, me % 2, me // 32, start]).astype(jnp.int32)
    wq, wk, wv, wo = map(in_hbm, (query_weight, key_weight, value_matrix, out_weight))
    q, da = early(in_hbm(tokens), in_hbm(out_cotangent), wq, wo)
    near = after(near, q)
    mate = passed_along(near, 1, range(0, 256, 2))
    (tp,) = prepared(prep_kernel, after(place, near), tokens, out_cotangent)
    th, far = prepared(halo_kernel, after(place, tp), far, mate, near)

    def attend(first, steps, place):
        return attention(first, steps, place, far, near, tokens, q, da, wk, wv, tp, th)

    one = attend(0, 3, place)
    got_one = to_mate(one[-2])
    two = attend(3, 1, after(place, one[-1]))
    got_two = to_mate(two[-2])
    sums = folded_into(0, one[-1], after(got_one, two[-1]))
    hand_give, hand_keep = handed(after(place, sums[0]), one[3], two[3], one[4], two[4])
    own, *sends = folded_into(3, two[-1], after(got_two, hand_keep), sums)
    ring_one = ring([None, *sends], 0)

    attn_out, base = middle((one[0], after(two[0], own)), (one[1], two[1]), wo, wq)
    back, near_one = met(after(place, base), hand_keep, to_mate(hand_give))
    own, *sends = folded(after(own, base, back), *ring_one)
    ring_two = ring([None, *sends], 1)
    back = jnp.stack([passed_along(after(back[i], own), -2) for i in range(2)])
    own, *sends = folded(own, *ring_two)
    ring_three = [along_z(sends[d - 1], 2 * d) for d in (1, 3, 2)]
    own, send = halved(own, *ring_three)
    got = along_z(send, 1)
    mine, other = turned(after(place, own), back, near_one)
    other = to_mate(other)
    tokens_grad = tail(place, base, one[2], two[2], mine, other, key_weight, value_matrix)
    query_rows, key_rows, value_rows, out_rows = summed_last(after(own, tokens_grad), got)
    return attn_out, tokens_grad, query_rows, key_rows, value_rows, out_rows.T


def solution(mesh):
    rows = P(AXIS, None)
    return jax.shard_map(
        shards,
        mesh=mesh,
        in_specs=(rows, P(), P(), P(), P(), rows),
        out_specs=(rows, rows, rows, rows, rows, P(None, AXIS)),
        check_vma=False,
    )
```

```python
import functools

import jax
import jax.numpy as jnp
from jax import lax
from jax.experimental import pallas as pl
from jax.experimental.pallas import tpu as pltpu
from jax.sharding import PartitionSpec as P

AXIS = "seq"
ROWS = 128
MODEL = 1024
LANES = 128
STEPS = 4
QCOLS = 256
KCOLS = 128
GCOLS = 768
SCALE = 0.125
MASKED = -1e30
BF16 = jnp.bfloat16
SMALL = pl.CostEstimate(flops=1000, transcendentals=0, bytes_accessed=1000)
F32 = jnp.float32
NT = (((1,), (1,)), ((), ()))
TN = (((0,), (0,)), ((), ()))


def dot(a, b, dims=(((1,), (0,)), ((), ()))):
    return lax.dot_general(a, b, dims, preferred_element_type=F32)


def flat(z, x, y, c):
    return ((z * 4 + x) * 4 + y) * 2 + c


def in_hbm(array):
    return pltpu.with_memory_space_constraint(array, pltpu.HBM)


def route_of(step):
    places = [(z, x, y, c) for z in range(8) for x in range(4) for y in range(4) for c in range(2)]
    return [(flat(*p), flat(*step(*p))) for p in places]


def to_mate(array):
    return lax.ppermute(array, AXIS, route_of(lambda z, x, y, c: (z, x, y, 1 - c)))


def plane_step(phase, d, z, x, y, c):
    if c == phase:
        return z, (x + d) % 4, y, c
    return z, x, (y + d) % 4, c


def ring(blocks, phase):
    return [
        lax.ppermute(blocks[d], AXIS, route_of(functools.partial(plane_step, phase, d)))
        for d in (2, 1, 3)
    ]


def along_z(block, distance):
    return lax.ppermute(
        block, AXIS, route_of(lambda z, x, y, c: ((z + distance) % 8, x, y, c))
    )


def passed_along(block, distance, sources=range(256)):
    return lax.ppermute(
        block, AXIS, [(i, i + distance) for i in sources if i + distance in range(256)]
    )


def reorder(place, t_ref, out_ref):
    x, y, core, mine = place[0], place[1], place[2], place[3]
    low = lax.broadcasted_iota(jnp.int32, (8, 2 * LANES), 0) < 4
    for half in range(2):
        target = 1 - core if half == 0 else core
        zero = target == 0
        for d1 in range(4):
            for d2 in range(4):
                xs = lax.rem(x + jnp.where(zero, d1, d2), 4)
                ys = lax.rem(y + jnp.where(zero, d2, d1), 4)
                for z in range(0, 8, 4):
                    rows = []
                    for pair in range(2):
                        base = xs * 32 + ys * 8
                        at = base + lax.rem(mine + z + 2 * pair, 8) * 128
                        one = t_ref[pl.ds(pl.multiple_of(at, 8), 8), :]
                        at = base + lax.rem(mine + z + 2 * pair + 1, 8) * 128
                        two = t_ref[pl.ds(pl.multiple_of(at, 8), 8), :]
                        c0 = jnp.where(low, one, pltpu.roll(two, 4, 0))
                        c1 = jnp.where(low, pltpu.roll(one, 4, 0), two)
                        rows.append(jnp.where(zero, c0, c1))
                    row = (d1 * 4 + d2) * 32 + z * 4
                    out_ref[half, row : row + 16, :] = jnp.concatenate(rows, 0).astype(BF16)


def early_kernel(tok_ref, cot_ref, wq_ref, wo_ref, q_ref, da_ref):
    q_ref[...] = dot(tok_ref[...], wq_ref[...]).astype(BF16)
    da_ref[...] = dot(cot_ref[...], wo_ref[...], NT).astype(BF16)


def whole(*shape):
    return pl.BlockSpec(shape, lambda i: (0,) * len(shape))


def early(tokens, cotangent, wq, wo):
    block = pl.BlockSpec((ROWS, QCOLS), lambda i: (0, i))
    return pl.pallas_call(
        early_kernel,
        grid=(STEPS,),
        out_shape=(jax.ShapeDtypeStruct((ROWS, MODEL), BF16),) * 2,
        in_specs=[
            whole(ROWS, MODEL),
            whole(ROWS, MODEL),
            pl.BlockSpec((MODEL, QCOLS), lambda i: (0, i)),
            pl.BlockSpec((QCOLS, MODEL), lambda i: (i, 0)),
        ],
        out_specs=(block, block),
        compiler_params=pltpu.CompilerParams(
            dimension_semantics=("arbitrary",), vmem_limit_bytes=12 << 20
        ),
        name="early",
    )(tokens, cotangent, wq, wo)


def prep_kernel(place, a_ref, b_ref, out_ref, t_ref):
    t_ref[:, :LANES] = a_ref[...].astype(F32).T
    t_ref[:, LANES:] = b_ref[...].astype(F32).T
    reorder(place, t_ref, out_ref)


def halo_kernel(place, far_ref, mate_ref, near_ref, out_ref, got_ref, t_ref):
    @pl.when(place[2] == 0)
    def _():
        got_ref[...] = far_ref[...]

    @pl.when(place[2] == 1)
    def _():
        got_ref[...] = mate_ref[...]

    prep_kernel(place, got_ref, near_ref, out_ref, t_ref)


def prepared(kernel, place, *blocks):
    order = jax.ShapeDtypeStruct((2, 512, 2 * LANES), BF16), whole(2, 512, 2 * LANES)
    outs = [order] if len(blocks) == 2 else [order, (jax.ShapeDtypeStruct((ROWS, MODEL), BF16), whole(ROWS, MODEL))]
    return pl.pallas_call(
        kernel,
        grid=(1,),
        out_shape=[o[0] for o in outs],
        in_specs=[pl.BlockSpec(memory_space=pltpu.SMEM)] + [whole(ROWS, MODEL)] * len(blocks),
        out_specs=[o[1] for o in outs],
        scratch_shapes=[pltpu.VMEM((MODEL, 2 * LANES), F32)],
        compiler_params=pltpu.CompilerParams(vmem_limit_bytes=12 << 20),
        name="prep",
    )(place, *blocks)


def swapped(a):
    return pltpu.roll(a, 64, 1)


def attention_kernel(
    place,
    far_ref,
    near_ref,
    own_ref,
    q_ref,
    da_ref,
    wk_ref,
    wv_ref,
    tp_ref,
    th_ref,
    att_ref,
    dq_ref,
    own_grad_ref,
    near_grad_ref,
    far_grad_ref,
    send_ref,
    keep_ref,
):
    window = jnp.concatenate([far_ref[...], near_ref[...], own_ref[...]], axis=0)
    keys = dot(window, wk_ref[...])
    values = dot(window, wv_ref[...])
    start = place[4]
    row = lax.rem(lax.broadcasted_iota(jnp.int32, (256, 384), 0), 128)
    col = lax.broadcasted_iota(jnp.int32, (256, 384), 1)
    allowed = (col <= row + 256) & (col >= start)
    low_k = lax.broadcasted_iota(jnp.int32, (384, LANES), 1) < 64
    low_q = lax.broadcasted_iota(jnp.int32, (ROWS, LANES), 1) < 64
    zero = jnp.zeros((ROWS, LANES), BF16)
    keys_swapped, values_swapped = swapped(keys), swapped(values)
    atts, dqs, dks, dvs = [], [], [], []
    for head in range(2):
        own_half = low_k if head == 0 else ~low_k
        key = jnp.where(own_half, keys, keys_swapped).astype(BF16)
        value = jnp.where(own_half, values, values_swapped).astype(BF16)
        cols = slice(head * LANES, (head + 1) * LANES)
        q = q_ref[:, cols]
        da = da_ref[:, cols]
        q2 = jnp.concatenate([jnp.where(low_q, q, zero), jnp.where(low_q, zero, q)], 0)
        da2 = jnp.concatenate([jnp.where(low_q, da, zero), jnp.where(low_q, zero, da)], 0)
        scores = jnp.where(allowed, dot(q2, key, NT) * SCALE, MASKED)
        highest = jnp.max(scores, axis=-1, keepdims=True)
        weights = jnp.exp(scores - highest)
        weights = weights * (1.0 / jnp.sum(weights, axis=-1, keepdims=True))
        probs = weights.astype(BF16)
        both = dot(probs, value)
        att = jnp.where(low_q, both[:ROWS], both[ROWS:]).astype(BF16)
        att_f = att.astype(F32)
        delta = jnp.sum(
            da2.astype(F32) * jnp.concatenate([att_f, att_f], 0), axis=-1, keepdims=True
        )
        dscores = (weights * (dot(da2, value, NT) - delta)).astype(BF16)
        both = dot(dscores, key) * SCALE
        dqs.append(jnp.where(low_q, both[:ROWS], both[ROWS:]).astype(BF16))
        dk = dot(dscores, q2, TN) * SCALE
        dv = dot(probs, da2, TN)
        dks.append(dk + swapped(dk))
        dvs.append(dv + swapped(dv))
        atts.append(att)
    att = jnp.concatenate(atts, 1)
    dq = jnp.concatenate(dqs, 1)
    dk = jnp.where(low_k, dks[0], dks[1])
    dv = jnp.where(low_k, dvs[0], dvs[1])
    att_ref[...] = att
    dq_ref[...] = dq
    own_grad_ref[0] = dk[256:]
    own_grad_ref[1] = dv[256:]
    dk, dv = dk.astype(BF16), dv.astype(BF16)
    far_grad_ref[0] = dk[:128]
    far_grad_ref[1] = dv[:128]
    near_grad_ref[0] = dk[128:256]
    near_grad_ref[1] = dv[128:256]
    rounded = jnp.concatenate([dk, dv], axis=1)
    for half, out in ((0, send_ref), (1, keep_ref)):
        tp = tp_ref[half]
        t_own, t_out = tp[:, :LANES], tp[:, LANES:]
        out[:, :256] = dot(t_out, att).astype(BF16)
        out[:, 256:512] = dot(t_own, dq).astype(BF16)
        out[:, 512:] = (dot(t_own, rounded[256:]) + dot(th_ref[half], rounded[:256])).astype(BF16)


def attention(first, steps, place, far, near, own, q, da, wk, wv, tp, th):
    def columns(rows, cols):
        return pl.BlockSpec((rows, cols), lambda i: (0, first + i))

    def fresh(rows, cols):
        return pl.BlockSpec((rows, cols), lambda i: (0, i))

    def struct(rows, cols, dtype):
        return jax.ShapeDtypeStruct((rows, cols * steps), dtype)

    return pl.pallas_call(
        attention_kernel,
        grid=(steps,),
        out_shape=(
            struct(ROWS, QCOLS, BF16),
            struct(ROWS, QCOLS, BF16),
            jax.ShapeDtypeStruct((2, ROWS, KCOLS * steps), F32),
            jax.ShapeDtypeStruct((2, ROWS, KCOLS * steps), BF16),
            jax.ShapeDtypeStruct((2, ROWS, KCOLS * steps), BF16),
            struct(512, GCOLS, BF16),
            struct(512, GCOLS, BF16),
        ),
        in_specs=[
            pl.BlockSpec(memory_space=pltpu.SMEM),
            whole(ROWS, MODEL),
            whole(ROWS, MODEL),
            whole(ROWS, MODEL),
            columns(ROWS, QCOLS),
            columns(ROWS, QCOLS),
            columns(MODEL, KCOLS),
            columns(MODEL, KCOLS),
            whole(2, 512, 2 * LANES),
            whole(2, 512, 2 * LANES),
        ],
        out_specs=(
            fresh(ROWS, QCOLS),
            fresh(ROWS, QCOLS),
            pl.BlockSpec((2, ROWS, KCOLS), lambda i: (0, 0, i)),
            pl.BlockSpec((2, ROWS, KCOLS), lambda i: (0, 0, i)),
            pl.BlockSpec((2, ROWS, KCOLS), lambda i: (0, 0, i)),
            fresh(512, GCOLS),
            fresh(512, GCOLS),
        ),
        compiler_params=pltpu.CompilerParams(
            dimension_semantics=("arbitrary",), vmem_limit_bytes=28 << 20
        ),
        cost_estimate=SMALL,
        name="attention",
    )(place, far, near, own, q, da, wk, wv, tp, th)


def cut(addends, rows):
    total = addends[0][rows, :].astype(F32)
    for other in addends[1:]:
        total = total + other[rows, :].astype(F32)
    return total


def fold_kernel(count, quarter, *refs):
    addends, outs = refs[:count], refs[count:]
    for d in range(4):
        outs[d][...] = cut(addends, slice(d * quarter, (d + 1) * quarter)).astype(outs[d].dtype)


def folded(*addends):
    rows, cols = addends[0].shape
    return pl.pallas_call(
        functools.partial(fold_kernel, len(addends), rows // 4),
        grid=(1,),
        out_shape=tuple(
            jax.ShapeDtypeStruct((rows // 4, cols), BF16 if d else F32) for d in range(4)
        ),
        in_specs=[whole(rows, cols)] * len(addends),
        out_specs=(whole(rows // 4, cols),) * 4,
        compiler_params=pltpu.CompilerParams(vmem_limit_bytes=20 << 20),
        name="fold",
    )(*addends)


def place_kernel(count, *refs):
    fold_kernel(2, 128, *refs[:2], *refs[2 + count :])


def folded_into(first, keep, got, wide=()):
    rows, cols = keep.shape
    given = pl.BlockSpec((rows, GCOLS), lambda i: (0, i))
    return pl.pallas_call(
        functools.partial(place_kernel, len(wide)),
        grid=(cols // GCOLS,),
        out_shape=tuple(
            jax.ShapeDtypeStruct((rows // 4, STEPS * GCOLS), BF16 if d else F32) for d in range(4)
        ),
        in_specs=[given, given] + [pl.BlockSpec(memory_space=pl.ANY)] * len(wide),
        out_specs=(pl.BlockSpec((rows // 4, GCOLS), lambda i: (0, first + i)),) * 4,
        input_output_aliases={2 + d: d for d in range(len(wide))},
        compiler_params=pltpu.CompilerParams(vmem_limit_bytes=12 << 20),
        name="place",
    )(keep, got, *wide)


def halve_kernel(own_ref, a_ref, b_ref, c_ref, keep_ref, send_ref):
    total = cut((own_ref, a_ref, b_ref, c_ref), slice(0, 8))
    keep_ref[...] = total[:4]
    send_ref[...] = total[4:].astype(BF16)


def halved(*addends):
    cols = addends[0].shape[1]
    return pl.pallas_call(
        halve_kernel,
        grid=(1,),
        out_shape=(
            jax.ShapeDtypeStruct((4, cols), F32),
            jax.ShapeDtypeStruct((4, cols), BF16),
        ),
        in_specs=[whole(8, cols)] * 4,
        out_specs=(whole(4, cols),) * 2,
        compiler_params=pltpu.CompilerParams(vmem_limit_bytes=4 << 20),
        name="halve",
    )(*addends)


def last_kernel(own_ref, got_ref, q_ref, k_ref, v_ref, o_ref):
    total = own_ref[...] + got_ref[...].astype(F32)
    for step in range(STEPS):
        base = step * GCOLS
        at = slice(step * 256, step * 256 + 256)
        o_ref[:, at] = total[:, base : base + 256]
        q_ref[:, at] = total[:, base + 256 : base + 512]
        at = slice(step * 128, step * 128 + 128)
        k_ref[:, at] = total[:, base + 512 : base + 640]
        v_ref[:, at] = total[:, base + 640 : base + 768]


def summed_last(own, got):
    shapes = [(4, 1024), (4, 512), (4, 512), (4, 1024)]
    return pl.pallas_call(
        last_kernel,
        grid=(1,),
        out_shape=tuple(jax.ShapeDtypeStruct(shape, F32) for shape in shapes),
        in_specs=[whole(*own.shape)] * 2,
        out_specs=tuple(whole(*shape) for shape in shapes),
        compiler_params=pltpu.CompilerParams(vmem_limit_bytes=4 << 20),
        name="last",
    )(own, got)


def middle_kernel(att_one, att_two, dq_one, dq_two, wo_ref, wq_ref, out_ref, base_ref):
    att = jnp.concatenate([att_one[...], att_two[...]], axis=1)
    out_ref[...] = dot(att, wo_ref[...]).astype(BF16)
    dq = jnp.concatenate([dq_one[...], dq_two[...]], axis=1)
    base_ref[...] = dot(dq, wq_ref[...], NT)


def middle(atts, dqs, wo, wq):
    block = pl.BlockSpec((ROWS, QCOLS), lambda i: (0, i))
    return pl.pallas_call(
        middle_kernel,
        grid=(STEPS,),
        out_shape=(
            jax.ShapeDtypeStruct((ROWS, MODEL), BF16),
            jax.ShapeDtypeStruct((ROWS, MODEL), F32),
        ),
        in_specs=[whole(*a.shape) for a in (*atts, *dqs)]
        + [
            pl.BlockSpec((MODEL, QCOLS), lambda i: (0, i)),
            pl.BlockSpec((QCOLS, MODEL), lambda i: (i, 0)),
        ],
        out_specs=(block, block),
        compiler_params=pltpu.CompilerParams(vmem_limit_bytes=12 << 20),
        name="middle",
    )(*atts, *dqs, wo, wq)


def tail_kernel(place, base_ref, own_one, own_two, mine_ref, other_ref, wk_ref, wv_ref, out_ref):
    total = base_ref[...]
    for i, w_ref in enumerate((wk_ref, wv_ref)):
        grad = jnp.concatenate([own_one[i], own_two[i]], axis=1)
        grad = grad + jnp.where(place[2] == i, mine_ref[...], other_ref[...].astype(F32))
        total = total + dot(grad.astype(BF16), w_ref[...], NT)
    out_ref[...] = total.astype(BF16)


def tail(place, *args):
    return pl.pallas_call(
        tail_kernel,
        grid=(1,),
        out_shape=jax.ShapeDtypeStruct((ROWS, MODEL), BF16),
        in_specs=[pl.BlockSpec(memory_space=pltpu.SMEM)] + [whole(*a.shape) for a in args],
        out_specs=whole(ROWS, MODEL),
        compiler_params=pltpu.CompilerParams(vmem_limit_bytes=20 << 20),
        name="tail",
    )(place, *args)


def on_place(kernel, name, outs, *args):
    return pl.pallas_call(
        kernel,
        grid=(1,),
        out_shape=tuple(jax.ShapeDtypeStruct(shape, kind) for shape, kind in outs),
        in_specs=[pl.BlockSpec(memory_space=pltpu.SMEM)] + [whole(*a.shape) for a in args[1:]],
        out_specs=tuple(whole(*shape) for shape, _ in outs),
        compiler_params=pltpu.CompilerParams(vmem_limit_bytes=8 << 20),
        name=name,
    )(*args)


def hand_kernel(place, near_one, near_two, far_one, far_two, give_ref, keep_ref):
    core = place[2]
    for i, (one, two) in enumerate(((near_one, near_two), (far_one, far_two))):
        split = one.shape[2]
        give_ref[i, :, :split] = one[1 - core]
        give_ref[i, :, split:] = two[1 - core]
        keep_ref[i, :, :split] = one[core]
        keep_ref[i, :, split:] = two[core]


def handed(*args):
    return on_place(hand_kernel, "hand", [((2, ROWS, 512), BF16)] * 2, *args)


def met_kernel(place, keep_ref, got_ref, back_ref, near_ref):
    def fill(zero, one):
        back_ref[0] = (zero[0].astype(F32) + one[1].astype(F32)).astype(BF16)
        back_ref[1] = zero[1]
        near_ref[...] = one[0]

    @pl.when(place[2] == 0)
    def _():
        fill(keep_ref, got_ref)

    @pl.when(place[2] == 1)
    def _():
        fill(got_ref, keep_ref)


def met(*args):
    return on_place(met_kernel, "met", [((2, ROWS, 512), BF16), ((ROWS, 512), BF16)], *args)


def turn_kernel(place, back_ref, near_ref, mine_ref, other_ref):
    at_zero = back_ref[1].astype(F32) + near_ref[...].astype(F32)
    at_one = back_ref[0].astype(F32)

    @pl.when(place[2] == 0)
    def _():
        mine_ref[...] = at_zero
        other_ref[...] = at_one.astype(BF16)

    @pl.when(place[2] == 1)
    def _():
        mine_ref[...] = at_one
        other_ref[...] = at_zero.astype(BF16)


def turned(*args):
    return on_place(turn_kernel, "turn", [((ROWS, 512), F32), ((ROWS, 512), BF16)], *args)


def after(value, *others):
    return lax.optimization_barrier((value, *others))[0]


def shards(tokens, query_weight, key_weight, value_matrix, out_weight, out_cotangent):
    near = passed_along(tokens, 1)
    far = passed_along(tokens, 2, range(0, 256, 2))
    me = lax.axis_index(AXIS)
    start = jnp.maximum(2 - me, 0) * ROWS
    place = jnp.stack([(me // 8) % 4, (me // 2) % 4, me % 2, me // 32, start]).astype(jnp.int32)
    wq, wk, wv, wo = map(in_hbm, (query_weight, key_weight, value_matrix, out_weight))
    q, da = early(in_hbm(tokens), in_hbm(out_cotangent), wq, wo)
    near = after(near, q)
    mate = passed_along(near, 1, range(0, 256, 2))
    (tp,) = prepared(prep_kernel, after(place, near), tokens, out_cotangent)
    th, far = prepared(halo_kernel, after(place, tp), far, mate, near)

    def attend(first, steps, place):
        return attention(first, steps, place, far, near, tokens, q, da, wk, wv, tp, th)

    one = attend(0, 3, place)
    got_one = to_mate(one[-2])
    two = attend(3, 1, after(place, one[-1]))
    got_two = to_mate(two[-2])
    sums = folded_into(0, one[-1], after(got_one, two[-1]))
    hand_give, hand_keep = handed(after(place, sums[0]), one[3], two[3], one[4], two[4])
    own, *sends = folded_into(3, two[-1], after(got_two, hand_keep), sums)
    ring_one = ring([None, *sends], 0)

    attn_out, base = middle((one[0], after(two[0], own)), (one[1], two[1]), wo, wq)
    back, near_one = met(after(place, base), hand_keep, to_mate(hand_give))
    own, *sends = folded(after(own, base, back), *ring_one)
    ring_two = ring([None, *sends], 1)
    back = jnp.stack([passed_along(after(back[i], own), -2) for i in range(2)])
    own, *sends = folded(own, *ring_two)
    ring_three = [along_z(sends[d - 1], 2 * d) for d in (1, 3, 2)]
    own, send = halved(own, *ring_three)
    got = along_z(send, 1)
    mine, other = turned(place, back, near_one)
    other = to_mate(after(other, own))
    tokens_grad = tail(place, base, one[2], two[2], mine, other, key_weight, value_matrix)
    query_rows, key_rows, value_rows, out_rows = summed_last(after(own, tokens_grad), got)
    return attn_out, tokens_grad, query_rows, key_rows, value_rows, out_rows.T


def solution(mesh):
    rows = P(AXIS, None)
    return jax.shard_map(
        shards,
        mesh=mesh,
        in_specs=(rows, P(), P(), P(), P(), rows),
        out_specs=(rows, rows, rows, rows, rows, P(None, AXIS)),
        check_vma=False,
    )
```

```python
import functools

import jax
import jax.numpy as jnp
from jax import lax
from jax.experimental import pallas as pl
from jax.experimental.pallas import tpu as pltpu
from jax.sharding import PartitionSpec as P

AXIS = "seq"
ROWS = 128
MODEL = 1024
LANES = 128
STEPS = 4
QCOLS = 256
KCOLS = 128
GCOLS = 768
SCALE = 0.125
MASKED = -1e30
BF16 = jnp.bfloat16
SMALL = pl.CostEstimate(flops=1000, transcendentals=0, bytes_accessed=1000)
F32 = jnp.float32
NT = (((1,), (1,)), ((), ()))
TN = (((0,), (0,)), ((), ()))


def dot(a, b, dims=(((1,), (0,)), ((), ()))):
    return lax.dot_general(a, b, dims, preferred_element_type=F32)


def flat(z, x, y, c):
    return ((z * 4 + x) * 4 + y) * 2 + c


def in_hbm(array):
    return pltpu.with_memory_space_constraint(array, pltpu.HBM)


def route_of(step):
    places = [(z, x, y, c) for z in range(8) for x in range(4) for y in range(4) for c in range(2)]
    return [(flat(*p), flat(*step(*p))) for p in places]


def to_mate(array):
    return lax.ppermute(array, AXIS, route_of(lambda z, x, y, c: (z, x, y, 1 - c)))


def plane_step(phase, d, z, x, y, c):
    if c == phase:
        return z, (x + d) % 4, y, c
    return z, x, (y + d) % 4, c


def ring(blocks, phase):
    return [
        lax.ppermute(blocks[d], AXIS, route_of(functools.partial(plane_step, phase, d)))
        for d in (2, 1, 3)
    ]


def along_z(block, distance):
    return lax.ppermute(
        block, AXIS, route_of(lambda z, x, y, c: ((z + distance) % 8, x, y, c))
    )


def passed_along(block, distance, sources=range(256)):
    return lax.ppermute(
        block, AXIS, [(i, i + distance) for i in sources if i + distance in range(256)]
    )


def reorder(place, t_ref, out_ref):
    x, y, core, mine = place[0], place[1], place[2], place[3]
    low = lax.broadcasted_iota(jnp.int32, (8, 2 * LANES), 0) < 4
    for half in range(2):
        target = 1 - core if half == 0 else core
        zero = target == 0
        for d1 in range(4):
            for d2 in range(4):
                xs = lax.rem(x + jnp.where(zero, d1, d2), 4)
                ys = lax.rem(y + jnp.where(zero, d2, d1), 4)
                for z in range(0, 8, 4):
                    rows = []
                    for pair in range(2):
                        base = xs * 32 + ys * 8
                        at = base + lax.rem(mine + z + 2 * pair, 8) * 128
                        one = t_ref[pl.ds(pl.multiple_of(at, 8), 8), :]
                        at = base + lax.rem(mine + z + 2 * pair + 1, 8) * 128
                        two = t_ref[pl.ds(pl.multiple_of(at, 8), 8), :]
                        c0 = jnp.where(low, one, pltpu.roll(two, 4, 0))
                        c1 = jnp.where(low, pltpu.roll(one, 4, 0), two)
                        rows.append(jnp.where(zero, c0, c1))
                    row = (d1 * 4 + d2) * 32 + z * 4
                    out_ref[half, row : row + 16, :] = jnp.concatenate(rows, 0).astype(BF16)


def early_kernel(tok_ref, cot_ref, wq_ref, wo_ref, q_ref, da_ref):
    q_ref[...] = dot(tok_ref[...], wq_ref[...]).astype(BF16)
    da_ref[...] = dot(cot_ref[...], wo_ref[...], NT).astype(BF16)


def whole(*shape):
    return pl.BlockSpec(shape, lambda i: (0,) * len(shape))


def early(tokens, cotangent, wq, wo):
    block = pl.BlockSpec((ROWS, QCOLS), lambda i: (0, i))
    return pl.pallas_call(
        early_kernel,
        grid=(STEPS,),
        out_shape=(jax.ShapeDtypeStruct((ROWS, MODEL), BF16),) * 2,
        in_specs=[
            whole(ROWS, MODEL),
            whole(ROWS, MODEL),
            pl.BlockSpec((MODEL, QCOLS), lambda i: (0, i)),
            pl.BlockSpec((QCOLS, MODEL), lambda i: (i, 0)),
        ],
        out_specs=(block, block),
        compiler_params=pltpu.CompilerParams(
            dimension_semantics=("arbitrary",), vmem_limit_bytes=12 << 20
        ),
        name="early",
    )(tokens, cotangent, wq, wo)


def prep_kernel(place, a_ref, b_ref, out_ref, t_ref):
    t_ref[:, :LANES] = a_ref[...].astype(F32).T
    t_ref[:, LANES:] = b_ref[...].astype(F32).T
    reorder(place, t_ref, out_ref)


def halo_kernel(place, far_ref, mate_ref, near_ref, out_ref, got_ref, t_ref):
    @pl.when(place[2] == 0)
    def _():
        got_ref[...] = far_ref[...]

    @pl.when(place[2] == 1)
    def _():
        got_ref[...] = mate_ref[...]

    prep_kernel(place, got_ref, near_ref, out_ref, t_ref)


def prepared(kernel, place, *blocks):
    order = jax.ShapeDtypeStruct((2, 512, 2 * LANES), BF16), whole(2, 512, 2 * LANES)
    outs = [order] if len(blocks) == 2 else [order, (jax.ShapeDtypeStruct((ROWS, MODEL), BF16), whole(ROWS, MODEL))]
    return pl.pallas_call(
        kernel,
        grid=(1,),
        out_shape=[o[0] for o in outs],
        in_specs=[pl.BlockSpec(memory_space=pltpu.SMEM)] + [whole(ROWS, MODEL)] * len(blocks),
        out_specs=[o[1] for o in outs],
        scratch_shapes=[pltpu.VMEM((MODEL, 2 * LANES), F32)],
        compiler_params=pltpu.CompilerParams(vmem_limit_bytes=12 << 20),
        name="prep",
    )(place, *blocks)


def swapped(a):
    return pltpu.roll(a, 64, 1)


def attention_kernel(
    place,
    far_ref,
    near_ref,
    own_ref,
    q_ref,
    da_ref,
    wk_ref,
    wv_ref,
    tp_ref,
    th_ref,
    att_ref,
    dq_ref,
    own_grad_ref,
    near_grad_ref,
    far_grad_ref,
    send_ref,
    keep_ref,
):
    window = jnp.concatenate([far_ref[...], near_ref[...], own_ref[...]], axis=0)
    keys = dot(window, wk_ref[...])
    values = dot(window, wv_ref[...])
    start = place[4]
    row = lax.rem(lax.broadcasted_iota(jnp.int32, (256, 384), 0), 128)
    col = lax.broadcasted_iota(jnp.int32, (256, 384), 1)
    allowed = (col <= row + 256) & (col >= start)
    low_k = lax.broadcasted_iota(jnp.int32, (384, LANES), 1) < 64
    low_q = lax.broadcasted_iota(jnp.int32, (ROWS, LANES), 1) < 64
    zero = jnp.zeros((ROWS, LANES), BF16)
    keys_swapped, values_swapped = swapped(keys), swapped(values)
    atts, dqs, dks, dvs = [], [], [], []
    for head in range(2):
        own_half = low_k if head == 0 else ~low_k
        key = jnp.where(own_half, keys, keys_swapped).astype(BF16)
        value = jnp.where(own_half, values, values_swapped).astype(BF16)
        cols = slice(head * LANES, (head + 1) * LANES)
        q = q_ref[:, cols]
        da = da_ref[:, cols]
        q2 = jnp.concatenate([jnp.where(low_q, q, zero), jnp.where(low_q, zero, q)], 0)
        da2 = jnp.concatenate([jnp.where(low_q, da, zero), jnp.where(low_q, zero, da)], 0)
        scores = jnp.where(allowed, dot(q2, key, NT) * SCALE, MASKED)
        highest = jnp.max(scores, axis=-1, keepdims=True)
        weights = jnp.exp(scores - highest)
        weights = weights * (1.0 / jnp.sum(weights, axis=-1, keepdims=True))
        probs = weights.astype(BF16)
        both = dot(probs, value)
        att = jnp.where(low_q, both[:ROWS], both[ROWS:]).astype(BF16)
        att_f = att.astype(F32)
        delta = jnp.sum(
            da2.astype(F32) * jnp.concatenate([att_f, att_f], 0), axis=-1, keepdims=True
        )
        dscores = (weights * (dot(da2, value, NT) - delta)).astype(BF16)
        both = dot(dscores, key) * SCALE
        dqs.append(jnp.where(low_q, both[:ROWS], both[ROWS:]).astype(BF16))
        dk = dot(dscores, q2, TN) * SCALE
        dv = dot(probs, da2, TN)
        dks.append(dk + swapped(dk))
        dvs.append(dv + swapped(dv))
        atts.append(att)
    att = jnp.concatenate(atts, 1)
    dq = jnp.concatenate(dqs, 1)
    dk = jnp.where(low_k, dks[0], dks[1])
    dv = jnp.where(low_k, dvs[0], dvs[1])
    att_ref[...] = att
    dq_ref[...] = dq
    own_grad_ref[0] = dk[256:]
    own_grad_ref[1] = dv[256:]
    dk, dv = dk.astype(BF16), dv.astype(BF16)
    far_grad_ref[0] = dk[:128]
    far_grad_ref[1] = dv[:128]
    near_grad_ref[0] = dk[128:256]
    near_grad_ref[1] = dv[128:256]
    rounded = jnp.concatenate([dk, dv], axis=1)
    for half, out in ((0, send_ref), (1, keep_ref)):
        tp = tp_ref[half]
        t_own, t_out = tp[:, :LANES], tp[:, LANES:]
        out[:, :256] = dot(t_out, att).astype(BF16)
        out[:, 256:512] = dot(t_own, dq).astype(BF16)
        out[:, 512:] = (dot(t_own, rounded[256:]) + dot(th_ref[half], rounded[:256])).astype(BF16)


def attention(first, steps, place, far, near, own, q, da, wk, wv, tp, th):
    def columns(rows, cols):
        return pl.BlockSpec((rows, cols), lambda i: (0, first + i))

    def fresh(rows, cols):
        return pl.BlockSpec((rows, cols), lambda i: (0, i))

    def struct(rows, cols, dtype):
        return jax.ShapeDtypeStruct((rows, cols * steps), dtype)

    return pl.pallas_call(
        attention_kernel,
        grid=(steps,),
        out_shape=(
            struct(ROWS, QCOLS, BF16),
            struct(ROWS, QCOLS, BF16),
            jax.ShapeDtypeStruct((2, ROWS, KCOLS * steps), F32),
            jax.ShapeDtypeStruct((2, ROWS, KCOLS * steps), BF16),
            jax.ShapeDtypeStruct((2, ROWS, KCOLS * steps), BF16),
            struct(512, GCOLS, BF16),
            struct(512, GCOLS, BF16),
        ),
        in_specs=[
            pl.BlockSpec(memory_space=pltpu.SMEM),
            whole(ROWS, MODEL),
            whole(ROWS, MODEL),
            whole(ROWS, MODEL),
            columns(ROWS, QCOLS),
            columns(ROWS, QCOLS),
            columns(MODEL, KCOLS),
            columns(MODEL, KCOLS),
            whole(2, 512, 2 * LANES),
            whole(2, 512, 2 * LANES),
        ],
        out_specs=(
            fresh(ROWS, QCOLS),
            fresh(ROWS, QCOLS),
            pl.BlockSpec((2, ROWS, KCOLS), lambda i: (0, 0, i)),
            pl.BlockSpec((2, ROWS, KCOLS), lambda i: (0, 0, i)),
            pl.BlockSpec((2, ROWS, KCOLS), lambda i: (0, 0, i)),
            fresh(512, GCOLS),
            fresh(512, GCOLS),
        ),
        compiler_params=pltpu.CompilerParams(
            dimension_semantics=("arbitrary",), vmem_limit_bytes=28 << 20
        ),
        cost_estimate=SMALL,
        name="attention",
    )(place, far, near, own, q, da, wk, wv, tp, th)


def cut(addends, rows):
    total = addends[0][rows, :].astype(F32)
    for other in addends[1:]:
        total = total + other[rows, :].astype(F32)
    return total


def fold_kernel(count, quarter, *refs):
    addends, outs = refs[:count], refs[count:]
    for d in range(4):
        outs[d][...] = cut(addends, slice(d * quarter, (d + 1) * quarter)).astype(outs[d].dtype)


def folded(*addends):
    rows, cols = addends[0].shape
    return pl.pallas_call(
        functools.partial(fold_kernel, len(addends), rows // 4),
        grid=(1,),
        out_shape=tuple(
            jax.ShapeDtypeStruct((rows // 4, cols), BF16 if d else F32) for d in range(4)
        ),
        in_specs=[whole(rows, cols)] * len(addends),
        out_specs=(whole(rows // 4, cols),) * 4,
        compiler_params=pltpu.CompilerParams(vmem_limit_bytes=20 << 20),
        name="fold",
    )(*addends)


def place_kernel(count, *refs):
    fold_kernel(2, 128, *refs[:2], *refs[2 + count :])


def folded_into(first, keep, got, wide=()):
    rows, cols = keep.shape
    given = pl.BlockSpec((rows, GCOLS), lambda i: (0, i))
    return pl.pallas_call(
        functools.partial(place_kernel, len(wide)),
        grid=(cols // GCOLS,),
        out_shape=tuple(
            jax.ShapeDtypeStruct((rows // 4, STEPS * GCOLS), BF16 if d else F32) for d in range(4)
        ),
        in_specs=[given, given] + [pl.BlockSpec(memory_space=pl.ANY)] * len(wide),
        out_specs=(pl.BlockSpec((rows // 4, GCOLS), lambda i: (0, first + i)),) * 4,
        input_output_aliases={2 + d: d for d in range(len(wide))},
        compiler_params=pltpu.CompilerParams(vmem_limit_bytes=12 << 20),
        name="place",
    )(keep, got, *wide)


def halve_kernel(own_ref, a_ref, b_ref, c_ref, keep_ref, send_ref):
    total = cut((own_ref, a_ref, b_ref, c_ref), slice(0, 8))
    keep_ref[...] = total[:4]
    send_ref[...] = total[4:].astype(BF16)


def halved(*addends):
    cols = addends[0].shape[1]
    return pl.pallas_call(
        halve_kernel,
        grid=(1,),
        out_shape=(
            jax.ShapeDtypeStruct((4, cols), F32),
            jax.ShapeDtypeStruct((4, cols), BF16),
        ),
        in_specs=[whole(8, cols)] * 4,
        out_specs=(whole(4, cols),) * 2,
        compiler_params=pltpu.CompilerParams(vmem_limit_bytes=4 << 20),
        name="halve",
    )(*addends)


def last_kernel(own_ref, got_ref, q_ref, k_ref, v_ref, o_ref):
    total = own_ref[...] + got_ref[...].astype(F32)
    for step in range(STEPS):
        base = step * GCOLS
        at = slice(step * 256, step * 256 + 256)
        o_ref[:, at] = total[:, base : base + 256]
        q_ref[:, at] = total[:, base + 256 : base + 512]
        at = slice(step * 128, step * 128 + 128)
        k_ref[:, at] = total[:, base + 512 : base + 640]
        v_ref[:, at] = total[:, base + 640 : base + 768]


def summed_last(own, got):
    shapes = [(4, 1024), (4, 512), (4, 512), (4, 1024)]
    return pl.pallas_call(
        last_kernel,
        grid=(1,),
        out_shape=tuple(jax.ShapeDtypeStruct(shape, F32) for shape in shapes),
        in_specs=[whole(*own.shape)] * 2,
        out_specs=tuple(whole(*shape) for shape in shapes),
        compiler_params=pltpu.CompilerParams(vmem_limit_bytes=4 << 20),
        name="last",
    )(own, got)


def middle_kernel(att_one, att_two, dq_one, dq_two, wo_ref, wq_ref, out_ref, base_ref):
    att = jnp.concatenate([att_one[...], att_two[...]], axis=1)
    out_ref[...] = dot(att, wo_ref[...]).astype(BF16)
    dq = jnp.concatenate([dq_one[...], dq_two[...]], axis=1)
    base_ref[...] = dot(dq, wq_ref[...], NT)


def middle(atts, dqs, wo, wq):
    block = pl.BlockSpec((ROWS, QCOLS), lambda i: (0, i))
    return pl.pallas_call(
        middle_kernel,
        grid=(STEPS,),
        out_shape=(
            jax.ShapeDtypeStruct((ROWS, MODEL), BF16),
            jax.ShapeDtypeStruct((ROWS, MODEL), F32),
        ),
        in_specs=[whole(*a.shape) for a in (*atts, *dqs)]
        + [
            pl.BlockSpec((MODEL, QCOLS), lambda i: (0, i)),
            pl.BlockSpec((QCOLS, MODEL), lambda i: (i, 0)),
        ],
        out_specs=(block, block),
        compiler_params=pltpu.CompilerParams(vmem_limit_bytes=12 << 20),
        name="middle",
    )(*atts, *dqs, wo, wq)


def tail_kernel(place, base_ref, own_one, own_two, mine_ref, other_ref, wk_ref, wv_ref, out_ref):
    total = base_ref[...]
    for i, w_ref in enumerate((wk_ref, wv_ref)):
        grad = jnp.concatenate([own_one[i], own_two[i]], axis=1)
        grad = grad + jnp.where(place[2] == i, mine_ref[...], other_ref[...].astype(F32))
        total = total + dot(grad.astype(BF16), w_ref[...], NT)
    out_ref[...] = total.astype(BF16)


def tail(place, *args):
    return pl.pallas_call(
        tail_kernel,
        grid=(1,),
        out_shape=jax.ShapeDtypeStruct((ROWS, MODEL), BF16),
        in_specs=[pl.BlockSpec(memory_space=pltpu.SMEM)] + [whole(*a.shape) for a in args],
        out_specs=whole(ROWS, MODEL),
        compiler_params=pltpu.CompilerParams(vmem_limit_bytes=20 << 20),
        name="tail",
    )(place, *args)


def on_place(kernel, name, outs, *args):
    return pl.pallas_call(
        kernel,
        grid=(1,),
        out_shape=tuple(jax.ShapeDtypeStruct(shape, kind) for shape, kind in outs),
        in_specs=[pl.BlockSpec(memory_space=pltpu.SMEM)] + [whole(*a.shape) for a in args[1:]],
        out_specs=tuple(whole(*shape) for shape, _ in outs),
        compiler_params=pltpu.CompilerParams(vmem_limit_bytes=8 << 20),
        name=name,
    )(*args)


def hand_kernel(place, near_one, near_two, far_one, far_two, give_ref, keep_ref):
    core = place[2]
    for i, (one, two) in enumerate(((near_one, near_two), (far_one, far_two))):
        split = one.shape[2]
        give_ref[i, :, :split] = one[1 - core]
        give_ref[i, :, split:] = two[1 - core]
        keep_ref[i, :, :split] = one[core]
        keep_ref[i, :, split:] = two[core]


def handed(*args):
    return on_place(hand_kernel, "hand", [((2, ROWS, 512), BF16)] * 2, *args)


def met_kernel(place, keep_ref, got_ref, back_ref, near_ref):
    def fill(zero, one):
        back_ref[0] = (zero[0].astype(F32) + one[1].astype(F32)).astype(BF16)
        back_ref[1] = zero[1]
        near_ref[...] = one[0]

    @pl.when(place[2] == 0)
    def _():
        fill(keep_ref, got_ref)

    @pl.when(place[2] == 1)
    def _():
        fill(got_ref, keep_ref)


def met(*args):
    return on_place(met_kernel, "met", [((2, ROWS, 512), BF16), ((ROWS, 512), BF16)], *args)


def turn_kernel(place, back_ref, near_ref, mine_ref, other_ref):
    at_zero = back_ref[1].astype(F32) + near_ref[...].astype(F32)
    at_one = back_ref[0].astype(F32)

    @pl.when(place[2] == 0)
    def _():
        mine_ref[...] = at_zero
        other_ref[...] = at_one.astype(BF16)

    @pl.when(place[2] == 1)
    def _():
        mine_ref[...] = at_one
        other_ref[...] = at_zero.astype(BF16)


def turned(*args):
    return on_place(turn_kernel, "turn", [((ROWS, 512), F32), ((ROWS, 512), BF16)], *args)


def after(value, *others):
    return lax.optimization_barrier((value, *others))[0]


def shards(tokens, query_weight, key_weight, value_matrix, out_weight, out_cotangent):
    near = passed_along(tokens, 1)
    far = passed_along(tokens, 2, range(0, 256, 2))
    me = lax.axis_index(AXIS)
    start = jnp.maximum(2 - me, 0) * ROWS
    place = jnp.stack([(me // 8) % 4, (me // 2) % 4, me % 2, me // 32, start]).astype(jnp.int32)
    wq, wk, wv, wo = map(in_hbm, (query_weight, key_weight, value_matrix, out_weight))
    q, da = early(in_hbm(tokens), in_hbm(out_cotangent), wq, wo)
    near = after(near, q)
    mate = passed_along(near, 1, range(0, 256, 2))
    (tp,) = prepared(prep_kernel, after(place, near), tokens, out_cotangent)
    th, far = prepared(halo_kernel, after(place, tp), far, mate, near)

    def attend(first, steps, place):
        return attention(first, steps, place, far, near, tokens, q, da, wk, wv, tp, th)

    one = attend(0, 3, place)
    got_one = to_mate(one[-2])
    two = attend(3, 1, after(place, one[-1]))
    got_two = to_mate(two[-2])
    sums = folded_into(0, one[-1], after(got_one, two[-1]))
    hand_give, hand_keep = handed(after(place, sums[0]), one[3], two[3], one[4], two[4])
    own, *sends = folded_into(3, two[-1], after(got_two, hand_keep), sums)
    ring_one = ring([None, *sends], 0)

    attn_out, base = middle((one[0], after(two[0], own)), (one[1], two[1]), wo, wq)
    back, near_one = met(after(place, base), hand_keep, to_mate(hand_give))
    own, *sends = folded(after(own, base, back), *ring_one)
    ring_two = ring([None, *sends], 1)
    back = jnp.stack([passed_along(after(back[i], own), -2) for i in range(2)])
    own, *sends = folded(own, *ring_two)
    ring_three = [along_z(sends[d - 1], 2 * d) for d in (2, 1, 3)]
    own, send = halved(own, *ring_three)
    got = along_z(send, 1)
    mine, other = turned(place, back, near_one)
    other = to_mate(after(other, own))
    tokens_grad = tail(place, base, one[2], two[2], mine, other, key_weight, value_matrix)
    query_rows, key_rows, value_rows, out_rows = summed_last(after(own, tokens_grad), got)
    return attn_out, tokens_grad, query_rows, key_rows, value_rows, out_rows.T


def solution(mesh):
    rows = P(AXIS, None)
    return jax.shard_map(
        shards,
        mesh=mesh,
        in_specs=(rows, P(), P(), P(), P(), rows),
        out_specs=(rows, rows, rows, rows, rows, P(None, AXIS)),
        check_vma=False,
    )
```
